32 devices in a mesh: item: 8 (over z, x), bucket: 4 (over y, core).
Axes of the slice: x: 2, y: 2, z: 4, core: 2. Of those that a mesh axis runs over, the one named last changes fastest.
Arguments:
- code_rows: bfloat16 [8192, 64], P('item'), may hold values from -6 to 6
- centroids: bfloat16 [32768, 64], P('bucket'), may hold values from -0.5 to 0.5
Outputs:
- grad_codes: float32 [8192, 64], P('item')
- new_centroids: float32 [32768, 64], P('bucket')
The draws below stay inside these ranges and needn't reach their ends.
All inputs are finite; a program needn't handle non-finite values.
Results may differ from the reference program's by a relative error of at most 0.0032.
Values sent between devices are 32-bit elements; how exact they have to be, the bound alone decides.
No kernel may reach another device: no remote copies, remote signals or barrier semaphores. Data moves between devices by JAX's collectives and lax.ppermute only.
A program may use at most 128 MiB of HBM per device.

```python
import jax
import jax.numpy as jnp
from jax import lax

DIM = 64
BUCKETS = 32768
ROWS_DEV = 1024
ITERS = 3
ROWS = 8192
N_ITEM = 8


def centroid_table(key):
    base = jax.random.truncated_normal(jax.random.fold_in(key, 11), -4.0, 4.0, (BUCKETS, DIM), jnp.float32) / 8.0
    return base


def draw_centroids(key, part):
    return centroid_table(key).astype(jnp.bfloat16)


def draw_codes_rows(key):
    return jax.random.truncated_normal(jax.random.fold_in(key, 12), -4.0, 4.0, (ROWS, DIM), jnp.float32) / 8.0


def draw_code_rows(key, part):
    values = draw_codes_rows(key)
    table = centroid_table(key)
    position = jnp.arange(ROWS)
    target = position // 64 * 448 % BUCKETS
    factors = jnp.array([2.0, 2.5, 3.0], jnp.float32)[position // 64 % 3]
    magnitude = 2.0 * factors * jnp.sqrt(16.0 / DIM)
    signs = jnp.where(table[target] >= 0.0, 1.0, -1.0)
    aligned = signs * magnitude[:, None]
    values = jnp.where((position % 64 == 0)[:, None], aligned, values)
    return values.astype(jnp.bfloat16)


def setup_inputs(seed: int = 0) -> dict:
    keys = jax.random.split(jax.random.key(seed), 3)
    return {
        "code_rows": draw_code_rows(jax.random.fold_in(keys[2], 71), 0),
        "centroids": draw_centroids(jax.random.fold_in(keys[2], 71), 0),
    }


score_scale = 20.0
step_rate = 0.2
epsilon = 1e-06

def block_scores(block, centroids):
    return score_scale * jnp.dot(block, centroids.T, preferred_element_type=jnp.float32)

def reference(code_rows, centroids):
    row_blocks = code_rows.reshape(N_ITEM, ROWS_DEV, DIM)
    log_rows = jnp.log(jnp.float32(ROWS))
    log_buckets = jnp.log(jnp.float32(BUCKETS))
    potential_col = jnp.zeros((BUCKETS,), jnp.float32)
    potential_row = jnp.zeros((N_ITEM, ROWS_DEV), jnp.float32)
    for iteration in range(ITERS):

        def row_pass(block, potential_col=potential_col):
            values = block_scores(block, centroids) + potential_col[None, :]
            highest = lax.optimization_barrier(jnp.max(values, axis=1))
            summed = lax.optimization_barrier(jnp.sum(jnp.exp(values - highest[:, None]), axis=1))
            return -log_rows - (highest + jnp.log(summed))
        potential_row = lax.map(row_pass, row_blocks)

        def col_highest(pair):
            block, potential = pair
            return lax.optimization_barrier(jnp.max(block_scores(block, centroids) + potential[:, None], axis=0))
        highest = lax.optimization_barrier(jnp.max(lax.map(col_highest, (row_blocks, potential_row)), axis=0))

        def col_summed(pair, highest=highest):
            block, potential = pair
            values = block_scores(block, centroids) + potential[:, None]
            return lax.optimization_barrier(jnp.sum(jnp.exp(values - highest[None, :]), axis=0))
        totals = lax.optimization_barrier(jnp.sum(lax.map(col_summed, (row_blocks, potential_row)), axis=0))
        potential_col = -log_buckets - (highest + jnp.log(totals))

    def final_pass(carry, pair):
        block, potential = pair
        scores = block_scores(block, centroids)
        plan = jnp.exp(scores + potential[:, None] + potential_col[None, :] + log_rows)
        masses = lax.optimization_barrier(jnp.sum(plan, axis=1))
        highest = lax.optimization_barrier(jnp.max(scores, axis=1))
        totals = lax.optimization_barrier(jnp.sum(jnp.exp(scores - highest[:, None]), axis=1))
        delta = (masses[:, None] * jnp.exp(scores - highest[:, None]) / totals[:, None] - plan).astype(jnp.bfloat16)
        grad_block = score_scale * jnp.dot(delta, centroids, preferred_element_type=jnp.float32)
        carry = carry + score_scale * jnp.dot(delta.T, block, preferred_element_type=jnp.float32)
        return (carry, grad_block)
    gradient, grad_blocks = lax.scan(final_pass, jnp.zeros((BUCKETS, DIM), jnp.float32), (row_blocks, potential_row))
    grad_codes = grad_blocks.reshape(ROWS, DIM)
    moved = centroids.astype(jnp.float32) - step_rate * gradient
    new_centroids = moved * lax.rsqrt(lax.optimization_barrier(jnp.mean(moved * moved, axis=1, keepdims=True)) + epsilon)
    return (grad_codes, new_centroids)
```

```python
import functools
import math

import jax
import jax.numpy as jnp
from jax import lax
from jax.experimental import pallas as pl
from jax.experimental.pallas import tpu as pltpu
from jax.sharding import PartitionSpec as P

ITERS = 3

score_scale = 20.0
step_rate = 0.2
epsilon = 1e-06

CHUNK = 512
LANES = 128
POTS = 16


def swap(value, axis, bit):
    size = lax.axis_size(axis)
    return lax.ppermute(value, axis, [(k, k ^ bit) for k in range(size)])


def bits_of(axis):
    size = lax.axis_size(axis)
    return [1 << k for k in range(size.bit_length() - 1)]


def add_over(value, axis):
    for bit in bits_of(axis):
        value = value + swap(value, axis, bit)
    return value


def gather_blocks(value, axis):
    held = {0: value}
    for bit in reversed(bits_of(axis)):
        held.update({key | bit: swap(block, axis, bit) for key, block in list(held.items())})
    return held


def weights(w_ref, columns, repeat):
    tile = w_ref[:, columns]
    return [tile] * repeat


def thirds(value):
    high = value.astype(jnp.bfloat16).astype(jnp.float32)
    middle = (value - high).astype(jnp.bfloat16).astype(jnp.float32)
    return high, middle, value - high - middle


def left_pots(column, shape):
    lane = lax.broadcasted_iota(jnp.int32, shape, 1)
    high, middle, low = thirds(column)
    out = jnp.where(lane < 3, 1.0, 0.0)
    out = jnp.where(lane == 3, high, out)
    out = jnp.where(lane == 4, middle, out)
    out = jnp.where(lane == 5, low, out)
    return out.astype(jnp.bfloat16)


def right_pots(row, width):
    sub = lax.broadcasted_iota(jnp.int32, (POTS, width), 0)
    high, middle, low = thirds(row)
    out = jnp.where((sub >= 3) & (sub < 6), 1.0, 0.0)
    out = jnp.where(sub == 0, high, out)
    out = jnp.where(sub == 1, middle, out)
    out = jnp.where(sub == 2, low, out)
    return out.astype(jnp.bfloat16)


def column_of(rows):
    return jnp.transpose(rows)


def row_of(column):
    wide = jnp.broadcast_to(column, (column.shape[0], LANES))
    return jnp.transpose(wide)[0:8, :]


def slices(value):
    return [value[:, k * LANES : (k + 1) * LANES] for k in range(value.shape[1] // LANES)]


def folded(values, op):
    values = list(values)
    while len(values) > 1:
        values = [op(*values[k : k + 2]) if k + 1 < len(values) else values[k] for k in range(0, len(values), 2)]
    return values[0]


def lse_kernel(l_ref, w_ref, out_ref, y_ref, part_ref, *, repeat):
    block, width = y_ref.shape
    left = l_ref[...]
    part_ref[...] = jnp.full(part_ref.shape, -jnp.inf, jnp.float32)

    @pl.loop(0, width // CHUNK)
    def _(step):
        at = pl.ds(pl.multiple_of(step * CHUNK, CHUNK), CHUNK)
        right = jnp.concatenate(weights(w_ref, at, repeat), axis=0)
        y = jnp.dot(left, right, preferred_element_type=jnp.float32)
        y_ref[:, at] = y
        part_ref[...] = jnp.maximum(part_ref[...], folded(slices(y), jnp.maximum))

    highest = jnp.max(part_ref[...], axis=1, keepdims=True)
    part_ref[...] = jnp.zeros(part_ref.shape, jnp.float32)
    wide = jnp.broadcast_to(highest, (block, LANES))

    @pl.loop(0, width // CHUNK)
    def _(step):
        at = pl.ds(pl.multiple_of(step * CHUNK, CHUNK), CHUNK)
        terms = [jnp.exp(piece - wide) for piece in slices(y_ref[:, at])]
        part_ref[...] += folded(terms, jnp.add)

    summed = jnp.sum(part_ref[...], axis=1, keepdims=True)
    lane = lax.broadcasted_iota(jnp.int32, (block, LANES), 1)
    both = jnp.where(lane == 0, highest, summed)
    out_ref[...] = jnp.transpose(both)[0:8, :]


def sink_kernel(
    l_ref, p_ref, w_ref, q_ref, sums_ref, pot_ref, row_ref, y_ref, part_ref, wide_ref, wpot_ref, acc_ref,
    *, first, rows_total, buckets_total, repeat
):
    block, width = y_ref.shape
    step_id = pl.program_id(0)

    @pl.when(step_id == 0)
    def _():
        acc_ref[...] = jnp.zeros(acc_ref.shape, jnp.float32)

        @pl.loop(0, width // CHUNK)
        def _(step):
            at = pl.ds(pl.multiple_of(step * CHUNK, CHUNK), CHUNK)
            row = q_ref[0:1, at]
            if not first:
                row = row - jnp.log(q_ref[1:2, at] * float(rows_total))
            row_ref[0:1, at] = row
            wpot_ref[:, at] = right_pots(row, CHUNK)

    if first:
        old = jnp.zeros((block, 1), jnp.float32)
    else:
        old = column_of(p_ref[...])[:, 0:1]
    left = jnp.concatenate([l_ref[...], left_pots(old, (block, LANES))], axis=1)[:, : LANES + POTS]
    part_ref[...] = jnp.full(part_ref.shape, -jnp.inf if first else 0.0, jnp.float32)

    @pl.loop(0, width // CHUNK)
    def _(step):
        at = pl.ds(pl.multiple_of(step * CHUNK, CHUNK), CHUNK)
        right = jnp.concatenate(weights(w_ref, at, repeat) + [wpot_ref[:, at]], axis=0)
        y = jnp.dot(left, right, preferred_element_type=jnp.float32)
        if first:
            y_ref[:, at] = y
            part_ref[...] = jnp.maximum(part_ref[...], folded(slices(y), jnp.maximum))
        else:
            y = jnp.exp(y)
            y_ref[:, at] = y
            part_ref[...] += folded(slices(y), jnp.add)

    if first:
        highest = jnp.max(part_ref[...], axis=1, keepdims=True)
        wide_ref[...] = jnp.broadcast_to(highest, (block, LANES))
        part_ref[...] = jnp.zeros(part_ref.shape, jnp.float32)

        @pl.loop(0, width // CHUNK)
        def _(step):
            at = pl.ds(pl.multiple_of(step * CHUNK, CHUNK), CHUNK)
            terms = [jnp.exp(piece - wide_ref[...]) for piece in slices(y_ref[:, at])]
            y_ref[:, at] = jnp.concatenate(terms, axis=1)
            part_ref[...] += folded(terms, jnp.add)

    summed = jnp.sum(part_ref[...], axis=1, keepdims=True)
    if first:
        new = -math.log(buckets_total) - (highest + jnp.log(summed))
    else:
        new = old - jnp.log(summed * float(buckets_total))
    pot_ref[...] = row_of(new)
    wide_ref[...] = jnp.broadcast_to(1.0 / (summed * float(buckets_total)), (block, LANES))

    @pl.loop(0, width // CHUNK)
    def _(step):
        at = pl.ds(pl.multiple_of(step * CHUNK, CHUNK), CHUNK)
        sums = [
            jnp.sum((piece * wide_ref[...]).reshape(block // 8, 8, LANES), axis=0) for piece in slices(y_ref[:, at])
        ]
        acc_ref[:, at] += jnp.concatenate(sums, axis=1)

    @pl.when(step_id == pl.num_programs(0) - 1)
    def _():
        sums_ref[...] = jnp.sum(acc_ref[...], axis=0, keepdims=True)


def final_kernel(
    l_ref, p_ref, w_ref, q_ref, r_ref, *rest, repeat, update
):
    if update:
        own_ref, out_ref, wide_ref, wpot_ref, acc_ref = rest
    else:
        out_ref, wide_ref, wpot_ref, acc_ref = rest
    block = l_ref.shape[0]
    width = w_ref.shape[1]

    @pl.when(pl.program_id(0) == 0)
    def _():
        @pl.loop(0, width // CHUNK)
        def _(step):
            at = pl.ds(pl.multiple_of(step * CHUNK, CHUNK), CHUNK)
            wpot_ref[:, at] = right_pots(q_ref[0:1, at], CHUNK)

    columns = column_of(p_ref[...])
    left = jnp.concatenate([l_ref[...], left_pots(columns[:, 0:1], (block, LANES))], axis=1)[:, : LANES + POTS]
    wide_ref[...] = jnp.broadcast_to(columns[:, 1:2], (block, LANES))
    acc_ref[...] = jnp.zeros(acc_ref.shape, jnp.float32)

    @pl.loop(0, width // CHUNK)
    def _(step):
        at = pl.ds(pl.multiple_of(step * CHUNK, CHUNK), CHUNK)
        right = jnp.concatenate(weights(w_ref, at, repeat) + [wpot_ref[:, at]], axis=0)
        y = jnp.dot(left, right, preferred_element_type=jnp.float32)
        scale = q_ref[1:2, at]
        delta = jnp.concatenate(
            [
                (jnp.exp(piece) * (wide_ref[...] * factor - 1.0)).astype(jnp.bfloat16)
                for piece, factor in zip(slices(y), slices(scale))
            ],
            axis=1,
        )
        acc_ref[...] += lax.dot_general(
            delta, r_ref[:, at], (((1,), (1,)), ((), ())), preferred_element_type=jnp.float32
        )

    gradient = score_scale * acc_ref[...]
    if not update:
        out_ref[...] = gradient
    else:
        moved = own_ref[...].astype(jnp.float32) - step_rate * gradient
        scaled = moved * lax.rsqrt(jnp.mean(moved * moved, axis=1, keepdims=True) + epsilon)
        half = block // 2
        out_ref[...] = jnp.concatenate([scaled[:half], scaled[half:]], axis=1)


VMEM = functools.partial(pltpu.VMEM)


def block_of(count, width):
    return min(count, 256 if width <= 16384 else 128)


def params():
    return pltpu.CompilerParams(dimension_semantics=("arbitrary",), vmem_limit_bytes=60 * 1024 * 1024)


def cost(count, width, passes):
    return pl.CostEstimate(
        flops=2 * count * width * 256 * passes, transcendentals=count * width, bytes_accessed=width * 256 * 2
    )


def full(array):
    return pl.BlockSpec(array.shape, lambda k: (0, 0))


def lse(left, right, repeat):
    count, width = left.shape[0], right.shape[1]
    block = block_of(count, width)
    return pl.pallas_call(
        functools.partial(lse_kernel, repeat=repeat),
        grid=(count // block,),
        in_specs=[pl.BlockSpec((block, LANES), lambda k: (k, 0)), full(right)],
        out_specs=pl.BlockSpec((8, block), lambda k: (0, k)),
        out_shape=jax.ShapeDtypeStruct((8, count), jnp.float32),
        scratch_shapes=[VMEM((block, width), jnp.float32), VMEM((block, LANES), jnp.float32)],
        compiler_params=params(),
        cost_estimate=cost(count, width, 1),
        name="row_lse",
    )(left, right)


def sink(left, p_rows, right, q_rows, first, rows_total, buckets_total):
    count, width = left.shape[0], right.shape[1]
    block = block_of(count, width)
    return pl.pallas_call(
        functools.partial(
            sink_kernel, first=first, rows_total=rows_total, buckets_total=buckets_total, repeat=1
        ),
        grid=(count // block,),
        in_specs=[
            pl.BlockSpec((block, LANES), lambda k: (k, 0)),
            pl.BlockSpec((8, block), lambda k: (0, k)),
            full(right),
            full(q_rows),
        ],
        out_specs=[
            pl.BlockSpec((1, width), lambda k: (0, 0)),
            pl.BlockSpec((8, block), lambda k: (0, k)),
            pl.BlockSpec((1, width), lambda k: (0, 0)),
        ],
        out_shape=[
            jax.ShapeDtypeStruct((1, width), jnp.float32),
            jax.ShapeDtypeStruct((8, count), jnp.float32),
            jax.ShapeDtypeStruct((1, width), jnp.float32),
        ],
        scratch_shapes=[
            VMEM((block, width), jnp.float32),
            VMEM((block, LANES), jnp.float32),
            VMEM((block, LANES), jnp.float32),
            VMEM((POTS, width), jnp.bfloat16),
            VMEM((8, width), jnp.float32),
        ],
        compiler_params=params(),
        cost_estimate=cost(count, width, 1),
        name="sinkhorn_first" if first else "sinkhorn_next",
    )(left, p_rows, right, q_rows)


def final(left, p_rows, right, q_rows, other, repeat, own=None):
    count, width = left.shape[0], right.shape[1]
    block = block_of(count, width)
    update = own is not None
    dim = other.shape[0]
    in_specs = [
        pl.BlockSpec((block, LANES), lambda k: (k, 0)),
        pl.BlockSpec((8, block), lambda k: (0, k)),
        full(right),
        full(q_rows),
        full(other),
    ]
    args = [left, p_rows, right, q_rows, other]
    if update:
        in_specs.append(pl.BlockSpec((block, dim), lambda k: (k, 0)))
        args.append(own)
        out_spec = pl.BlockSpec((block // 2, 2 * dim), lambda k: (k, 0))
        out_shape = jax.ShapeDtypeStruct((count // 2, 2 * dim), jnp.float32)
    else:
        out_spec = pl.BlockSpec((block, dim), lambda k: (k, 0))
        out_shape = jax.ShapeDtypeStruct((count, dim), jnp.float32)
    out = pl.pallas_call(
        functools.partial(final_kernel, repeat=repeat, update=update),
        grid=(count // block,),
        in_specs=in_specs,
        out_specs=out_spec,
        out_shape=out_shape,
        scratch_shapes=[
            VMEM((block, LANES), jnp.float32),
            VMEM((POTS, width), jnp.bfloat16),
            VMEM((block, dim), jnp.float32),
        ],
        compiler_params=params(),
        cost_estimate=cost(count, width, 2),
        name="centroid_update" if update else "code_gradient",
    )(*args)
    return out, block


def halves(scaled):
    high = lax.reduce_precision(scaled, 8, 7)
    return high.astype(jnp.bfloat16), (scaled - high).astype(jnp.bfloat16)


def eight(*rows):
    rows = [row.reshape(1, -1) for row in rows]
    return jnp.concatenate(rows + [jnp.zeros((8 - len(rows), rows[0].shape[1]), jnp.float32)], axis=0)


def body(code_rows, centroids):
    items = lax.axis_size("item")
    item = lax.axis_index("item")
    rows_own, dim = code_rows.shape
    rows_total = rows_own * items
    buckets_own = centroids.shape[0]
    buckets_total = buckets_own * lax.axis_size("bucket")
    share = buckets_own // items
    log_rows = math.log(rows_total)

    codes_f32 = code_rows.astype(jnp.float32)
    row_left = jnp.concatenate(halves(score_scale * codes_f32), axis=1)
    centroids_t = centroids.T
    stats = lse(row_left, centroids_t, 2)[0:2]
    codes_t = codes_f32.T

    blocks = gather_blocks(codes_t, "item")
    table = jnp.zeros((items,) + codes_t.shape, jnp.float32)
    for key, block in blocks.items():
        table = lax.dynamic_update_slice(table, block[None], (item ^ key, 0, 0))
    table = table.transpose(1, 0, 2).reshape(dim, rows_total)
    high, low = halves(score_scale * table)
    all_right = jnp.concatenate([high, low], axis=0)
    all_other = table.astype(jnp.bfloat16)
    own = lax.dynamic_slice_in_dim(centroids, item * share, share, axis=0)
    own_left = jnp.concatenate([own, own], axis=1)

    for bit in bits_of("bucket"):
        other = swap(stats, "bucket", bit)
        highest = jnp.maximum(stats[0], other[0])
        summed = stats[1] * jnp.exp(stats[0] - highest) + other[1] * jnp.exp(other[0] - highest)
        stats = jnp.stack([highest, summed])
    first_own = -log_rows - (stats[0] + jnp.log(stats[1]))
    row_first = lax.dynamic_update_slice(jnp.zeros((rows_total,), jnp.float32), first_own, (item * rows_own,))
    row_first = add_over(row_first, "item")

    p_rows = jnp.zeros((8, share), jnp.float32)
    q_rows = eight(row_first)
    sums = None
    for iteration in range(ITERS):
        sums, p_rows, row = sink(own_left, p_rows, all_right, q_rows, iteration == 0, rows_total, buckets_total)
        sums = add_over(sums, "bucket")
        if iteration < ITERS - 1:
            sums = add_over(sums, "item")
            q_rows = eight(row, sums)

    col_own = p_rows[0]
    col = lax.dynamic_update_slice(jnp.zeros((buckets_own,), jnp.float32), col_own, (item * share,))
    if buckets_own == rows_total:
        both = add_over(jnp.concatenate([sums, col.reshape(1, -1)], axis=0), "item")
        sums, col = both[0], both[1]
    else:
        sums, col = add_over(sums.reshape(-1), "item"), add_over(col, "item")
    mass = sums.reshape(-1) * float(rows_total)
    row = row.reshape(-1)
    row_pot = row + log_rows
    row_scale = mass * jnp.exp(row_first - row)

    update, block = final(
        own_left, eight(col_own, jnp.exp(-col_own)), all_right, eight(row_pot, row_scale), all_other, 1, own
    )

    def mine(values):
        return lax.dynamic_slice_in_dim(values, item * rows_own, rows_own, axis=0)

    grad, _ = final(
        row_left, eight(mine(row_pot), mine(row_scale)), centroids_t, eight(col, jnp.exp(-col)), centroids_t, 2
    )

    new_centroids = jnp.zeros((items, share, dim), jnp.float32)
    for key, piece in gather_blocks(update, "item").items():
        piece = piece.reshape(share // block, block // 2, 2, dim).transpose(0, 2, 1, 3).reshape(1, share, dim)
        new_centroids = lax.dynamic_update_slice(new_centroids, piece, (item ^ key, 0, 0))
    grad_codes = add_over(grad, "bucket")
    return (grad_codes, new_centroids.reshape(buckets_own, dim))


def solution(mesh):
    return jax.shard_map(
        body,
        mesh=mesh,
        in_specs=(P("item", None), P("bucket", None)),
        out_specs=(P("item", None), P("bucket", None)),
        check_vma=False,
    )
```

```python
import functools
import math

import jax
import jax.numpy as jnp
from jax import lax
from jax.experimental import pallas as pl
from jax.experimental.pallas import tpu as pltpu
from jax.sharding import PartitionSpec as P

ITERS = 3

score_scale = 20.0
step_rate = 0.2
epsilon = 1e-06

CHUNK = 2048
LANES = 128
POTS = 16


def swap(value, axis, bit):
    size = lax.axis_size(axis)
    return lax.ppermute(value, axis, [(k, k ^ bit) for k in range(size)])


def bits_of(axis):
    size = lax.axis_size(axis)
    return [1 << k for k in range(size.bit_length() - 1)]


def add_over(value, axis):
    for bit in bits_of(axis):
        value = value + swap(value, axis, bit)
    return value


def gather_blocks(value, axis):
    held = {0: value}
    for bit in reversed(bits_of(axis)):
        held.update({key | bit: swap(block, axis, bit) for key, block in list(held.items())})
    return held


def thirds(value):
    high = value.astype(jnp.bfloat16).astype(jnp.float32)
    middle = (value - high).astype(jnp.bfloat16).astype(jnp.float32)
    return high, middle, value - high - middle


def pots(row, width, at):
    sub = lax.broadcasted_iota(jnp.int32, (POTS, width), 0)
    high, middle, low = thirds(row)
    out = jnp.where(sub < 6, 1.0, 0.0)
    out = jnp.where(sub == at, high, out)
    out = jnp.where(sub == at + 1, middle, out)
    out = jnp.where(sub == at + 2, low, out)
    return out.astype(jnp.bfloat16)


def left_pots(row, width):
    return jnp.transpose(pots(row, width, 3).astype(jnp.float32)).astype(jnp.bfloat16)


def row_of(column):
    wide = jnp.broadcast_to(column, (column.shape[0], LANES))
    return jnp.transpose(wide)[0:8, :]


def slices(value):
    return [value[:, k * LANES : (k + 1) * LANES] for k in range(value.shape[1] // LANES)]


def folded(values, op):
    values = list(values)
    while len(values) > 1:
        values = [op(*values[k : k + 2]) if k + 1 < len(values) else values[k] for k in range(0, len(values), 2)]
    return values[0]


def own_pieces(item_ref, key, width):
    return pl.ds(pl.multiple_of((item_ref[0] ^ key) * width, width), width)


def table_kernel(item_ref, *refs, keys):
    pieces, (right_ref, other_ref) = refs[: len(keys)], refs[len(keys) :]
    dim = other_ref.shape[0]
    for key, piece_ref in zip(keys, pieces):
        at = own_pieces(item_ref, key, piece_ref.shape[1])
        piece = piece_ref[...]
        scaled = score_scale * piece
        high = scaled.astype(jnp.bfloat16)
        right_ref[0:dim, at] = high
        right_ref[dim : 2 * dim, at] = (scaled - high.astype(jnp.float32)).astype(jnp.bfloat16)
        other_ref[:, at] = piece.astype(jnp.bfloat16)


def spread_kernel(item_ref, *refs, keys, half):
    pieces, out_ref = refs[: len(keys)], refs[len(keys)]
    for key, piece_ref in zip(keys, pieces):
        count, twice = piece_ref.shape
        for part in range(count // half):
            piece = piece_ref[part * half : (part + 1) * half, :]
            for side in range(2):
                start = (item_ref[0] ^ key) * (2 * count) + (2 * part + side) * half
                at = pl.ds(pl.multiple_of(start, half), half)
                out_ref[at, :] = piece[:, side * (twice // 2) : (side + 1) * (twice // 2)]


def chunk_of(width):
    return min(width, CHUNK)


def chunks(width, run):
    size = chunk_of(width)

    @pl.loop(0, width // size)
    def _(step):
        run(pl.ds(pl.multiple_of(step * size, size), size))


def cases(count, run):
    step = pl.program_id(0)

    @pl.when(step == 0)
    def _():
        run(True, False)

    if count > 1:

        @pl.when((step > 0) & (step < count))
        def _():
            run(True, True)

    @pl.when(step == count)
    def _():
        run(False, True)


def lse_kernel(l_ref, w_ref, out_ref, y_ref, part_ref, sum_ref, wide_ref, *, repeat, count):
    block, width = y_ref.shape

    def run(new, old):
        if old:
            highest = jnp.max(part_ref[...], axis=1, keepdims=True)
            wide_ref[...] = jnp.broadcast_to(highest, (block, LANES))
            sum_ref[...] = jnp.zeros(sum_ref.shape, jnp.float32)
        if new:
            part_ref[...] = jnp.full(part_ref.shape, -jnp.inf, jnp.float32)

        def chunk(at):
            if old:
                terms = [jnp.exp(piece - wide_ref[...]) for piece in slices(y_ref[:, at])]
                sum_ref[...] += folded(terms, jnp.add)
            if new:
                right = jnp.concatenate([w_ref[:, at]] * repeat, axis=0)
                y = jnp.dot(l_ref[...], right, preferred_element_type=jnp.float32)
                y_ref[:, at] = y
                part_ref[...] = jnp.maximum(part_ref[...], folded(slices(y), jnp.maximum))

        chunks(width, chunk)
        if old:
            summed = jnp.sum(sum_ref[...], axis=1, keepdims=True)
            lane = lax.broadcasted_iota(jnp.int32, (block, LANES), 1)
            both = jnp.where(lane == 0, wide_ref[...], summed)
            out_ref[...] = jnp.transpose(both)[0:8, :]

    cases(count, run)


def sink_kernel(
    l_ref, p_ref, w_ref, q_ref, *rest, first, rows_total, buckets_total, count
):
    if not first:
        one_ref, two_ref, *rest = rest
    sums_ref, pot_ref, row_ref, y_ref, part_ref, high_ref, wide_ref, wpot_ref, acc_ref = rest
    block, width = y_ref.shape

    def run(new, old):
        if new and not old:
            acc_ref[...] = jnp.zeros(acc_ref.shape, jnp.float32)

            def prepare(at):
                row = q_ref[0:1, at]
                if not first:
                    row = row - jnp.log((one_ref[0:1, at] + two_ref[0:1, at]) * float(rows_total))
                row_ref[0:1, at] = row
                wpot_ref[:, at] = pots(row, chunk_of(width), 0)

            chunks(width, prepare)
        if new:
            was = jnp.zeros((1, block), jnp.float32) if first else p_ref[0:1, :]
            left = jnp.concatenate([l_ref[...], left_pots(was, block)], axis=1)
            part_ref[...] = jnp.full(part_ref.shape, -jnp.inf if first else 0.0, jnp.float32)

        def chunk(at):
            if old:
                sums = [
                    jnp.sum((piece * wide_ref[...]).reshape(block // 8, 8, LANES), axis=0)
                    for piece in slices(y_ref[:, at])
                ]
                acc_ref[:, at] += jnp.concatenate(sums, axis=1)
            if new:
                right = jnp.concatenate([w_ref[:, at], wpot_ref[:, at]], axis=0)
                y = jnp.dot(left, right, preferred_element_type=jnp.float32)
                if first:
                    y_ref[:, at] = y
                    part_ref[...] = jnp.maximum(part_ref[...], folded(slices(y), jnp.maximum))
                else:
                    y = jnp.exp(y)
                    y_ref[:, at] = y
                    part_ref[...] += folded(slices(y), jnp.add)

        chunks(width, chunk)
        if new and first:
            highest = jnp.max(part_ref[...], axis=1, keepdims=True)
            high_ref[...] = jnp.broadcast_to(highest, (block, LANES))
            part_ref[...] = jnp.zeros(part_ref.shape, jnp.float32)

            def again(at):
                terms = [jnp.exp(piece - high_ref[...]) for piece in slices(y_ref[:, at])]
                y_ref[:, at] = jnp.concatenate(terms, axis=1)
                part_ref[...] += folded(terms, jnp.add)

            chunks(width, again)
        if new:
            summed = jnp.sum(part_ref[...], axis=1, keepdims=True) * float(buckets_total)
            wide_ref[...] = jnp.broadcast_to(1.0 / summed, (block, LANES))
            summed = row_of(summed)
            if first:
                pot_ref[...] = -(row_of(high_ref[...]) + jnp.log(summed))
            else:
                pot_ref[...] = was - jnp.log(summed)
        if not new:
            sums_ref[...] = jnp.sum(acc_ref[...], axis=0, keepdims=True)

    cases(count, run)


def final_kernel(l_ref, p_ref, u_ref, w_ref, q_ref, v_ref, r_ref, *rest, repeat, update):
    if update:
        own_ref, out_ref, wide_ref, wpot_ref, acc_ref = rest
    else:
        out_ref, wide_ref, wpot_ref, acc_ref = rest
    block = l_ref.shape[0]
    width = w_ref.shape[1]

    @pl.when(pl.program_id(0) == 0)
    def _():
        def prepare(at):
            wpot_ref[:, at] = pots(q_ref[0:1, at], chunk_of(width), 0)

        chunks(width, prepare)

    left = jnp.concatenate([l_ref[...], left_pots(p_ref[0:1, :], block)], axis=1)
    wide_ref[...] = jnp.transpose(jnp.broadcast_to(u_ref[0:1, :], (LANES, block)))
    acc_ref[...] = jnp.zeros(acc_ref.shape, jnp.float32)

    def chunk(at):
        right = jnp.concatenate([w_ref[:, at]] * repeat + [wpot_ref[:, at]], axis=0)
        y = jnp.dot(left, right, preferred_element_type=jnp.float32)
        delta = jnp.concatenate(
            [
                (jnp.exp(piece) * (wide_ref[...] * factor - 1.0)).astype(jnp.bfloat16)
                for piece, factor in zip(slices(y), slices(v_ref[0:1, at]))
            ],
            axis=1,
        )
        acc_ref[...] += lax.dot_general(
            delta, r_ref[:, at], (((1,), (1,)), ((), ())), preferred_element_type=jnp.float32
        )

    chunks(width, chunk)
    gradient = score_scale * acc_ref[...]
    if not update:
        out_ref[...] = gradient
    else:
        moved = own_ref[...].astype(jnp.float32) - step_rate * gradient
        scaled = moved * lax.rsqrt(jnp.mean(moved * moved, axis=1, keepdims=True) + epsilon)
        half = block // 2
        out_ref[...] = jnp.concatenate([scaled[:half], scaled[half:]], axis=1)


VMEM = functools.partial(pltpu.VMEM)


def block_of(count, width):
    return min(count, 256 if width <= 16384 else 128)


def params():
    return pltpu.CompilerParams(dimension_semantics=("arbitrary",), vmem_limit_bytes=60 * 1024 * 1024)


def cost(count, width, passes):
    return pl.CostEstimate(
        flops=2 * count * width * 256 * passes, transcendentals=count * width, bytes_accessed=width * 256 * 2
    )


def full(array):
    return pl.BlockSpec(array.shape, lambda k: (0, 0))


def lse(left, right, repeat):
    rows, width = left.shape[0], right.shape[1]
    block = block_of(rows, width)
    count = rows // block
    return pl.pallas_call(
        functools.partial(lse_kernel, repeat=repeat, count=count),
        grid=(count + 1,),
        in_specs=[pl.BlockSpec((block, LANES), lambda k: (jnp.minimum(k, count - 1), 0)), full(right)],
        out_specs=pl.BlockSpec((8, block), lambda k: (0, jnp.maximum(k - 1, 0))),
        out_shape=jax.ShapeDtypeStruct((8, rows), jnp.float32),
        scratch_shapes=[VMEM((block, width), jnp.float32)] + [VMEM((block, LANES), jnp.float32)] * 3,
        compiler_params=params(),
        cost_estimate=cost(rows, width, 1),
        name="row_lse",
    )(left, right)


def sink(left, p_rows, right, row, sums, rows_total, buckets_total):
    rows, width = left.shape[0], right.shape[1]
    block = block_of(rows, width)
    count = rows // block
    first = sums is None
    line = pl.BlockSpec((1, width), lambda k: (0, 0))
    lines = [row] if first else [row, *sums]
    pot_spec = pl.BlockSpec((8, block), lambda k: (0, jnp.minimum(k, count - 1)))
    return pl.pallas_call(
        functools.partial(
            sink_kernel, first=first, rows_total=rows_total, buckets_total=buckets_total, count=count
        ),
        grid=(count + 1,),
        in_specs=[
            pl.BlockSpec((block, LANES), lambda k: (jnp.minimum(k, count - 1), 0)),
            pot_spec,
            full(right),
        ]
        + [line] * len(lines),
        out_specs=[line, pot_spec, line],
        out_shape=[
            jax.ShapeDtypeStruct((1, width), jnp.float32),
            jax.ShapeDtypeStruct((8, rows), jnp.float32),
            jax.ShapeDtypeStruct((1, width), jnp.float32),
        ],
        scratch_shapes=[VMEM((block, width), jnp.float32)]
        + [VMEM((block, LANES), jnp.float32)] * 3
        + [VMEM((POTS, width), jnp.bfloat16), VMEM((8, width), jnp.float32)],
        compiler_params=params(),
        cost_estimate=cost(rows, width, 1),
        name="sinkhorn_first" if first else "sinkhorn_next",
    )(left, p_rows, right, *lines)


def final(left, p_row, u_row, right, q_row, v_row, other, repeat, own=None):
    rows, width = left.shape[0], right.shape[1]
    block = block_of(rows, width)
    update = own is not None
    dim = other.shape[0]
    line = pl.BlockSpec((1, width), lambda k: (0, 0))
    part = pl.BlockSpec((1, block), lambda k: (0, k))
    in_specs = [pl.BlockSpec((block, LANES), lambda k: (k, 0)), part, part, full(right), line, line, full(other)]
    args = [left, p_row, u_row, right, q_row, v_row, other]
    if update:
        in_specs.append(pl.BlockSpec((block, dim), lambda k: (k, 0)))
        args.append(own)
        out_spec = pl.BlockSpec((block // 2, 2 * dim), lambda k: (k, 0))
        out_shape = jax.ShapeDtypeStruct((rows // 2, 2 * dim), jnp.float32)
    else:
        out_spec = pl.BlockSpec((block, dim), lambda k: (k, 0))
        out_shape = jax.ShapeDtypeStruct((rows, dim), jnp.float32)
    out = pl.pallas_call(
        functools.partial(final_kernel, repeat=repeat, update=update),
        grid=(rows // block,),
        in_specs=in_specs,
        out_specs=out_spec,
        out_shape=out_shape,
        scratch_shapes=[
            VMEM((block, LANES), jnp.float32),
            VMEM((POTS, width), jnp.bfloat16),
            VMEM((block, dim), jnp.float32),
        ],
        compiler_params=params(),
        cost_estimate=cost(rows, width, 2),
        name="centroid_update" if update else "code_gradient",
    )(*args)
    return out, block


def by_item(kernel, item, blocks, out_shape, name, **settings):
    keys = sorted(blocks)
    several = isinstance(out_shape, list)
    whole = lambda shape: pl.BlockSpec(shape, lambda k, item: (0, 0))
    shapes = out_shape if several else [out_shape]
    specs = [whole(one.shape) for one in shapes]
    return pl.pallas_call(
        functools.partial(kernel, keys=keys, **settings),
        grid_spec=pltpu.PrefetchScalarGridSpec(
            num_scalar_prefetch=1,
            grid=(1,),
            in_specs=[whole(blocks[key].shape) for key in keys],
            out_specs=specs if several else specs[0],
        ),
        out_shape=out_shape,
        compiler_params=params(),
        cost_estimate=pl.CostEstimate(flops=0, transcendentals=0, bytes_accessed=6 << 20),
        name=name,
    )(item.reshape(1).astype(jnp.int32), *[blocks[key] for key in keys])


def halves(scaled):
    high = lax.reduce_precision(scaled, 8, 7)
    return high.astype(jnp.bfloat16), (scaled - high).astype(jnp.bfloat16)


def body(code_rows, centroids):
    items = lax.axis_size("item")
    item = lax.axis_index("item")
    rows_own, dim = code_rows.shape
    rows_total = rows_own * items
    buckets_own = centroids.shape[0]
    buckets_total = buckets_own * lax.axis_size("bucket")
    share = buckets_own // items
    log_rows = math.log(rows_total)

    codes_f32 = code_rows.astype(jnp.float32)
    row_left = jnp.concatenate(halves(score_scale * codes_f32), axis=1)
    centroids_t = centroids.T
    stats = lse(row_left, centroids_t, 2)[0:2]

    right, other = by_item(
        table_kernel,
        item,
        gather_blocks(codes_f32.T, "item"),
        [
            jax.ShapeDtypeStruct((2 * dim, rows_total), jnp.bfloat16),
            jax.ShapeDtypeStruct((dim, rows_total), jnp.bfloat16),
        ],
        "table",
    )
    own = lax.dynamic_slice_in_dim(centroids, item * share, share, axis=0)
    own_left = jnp.concatenate([own, own], axis=1)

    for bit in bits_of("bucket"):
        received = swap(stats, "bucket", bit)
        highest = jnp.maximum(stats[0], received[0])
        summed = stats[1] * jnp.exp(stats[0] - highest) + received[1] * jnp.exp(received[0] - highest)
        stats = jnp.stack([highest, summed])
    first_own = -log_rows - (stats[0:1] + jnp.log(stats[1:2]))
    row_first = lax.dynamic_update_slice(jnp.zeros((1, rows_total), jnp.float32), first_own, (0, item * rows_own))
    row = row_first = add_over(row_first, "item")

    cols = jnp.zeros((8, share), jnp.float32)
    sums = None
    for iteration in range(ITERS):
        total, cols, row = sink(own_left, cols, right, row, sums, rows_total, buckets_total)
        total = add_over(total, "bucket")
        if iteration < ITERS - 1:
            for bit in bits_of("item")[:-1]:
                total = total + swap(total, "item", bit)
            sums = (total, swap(total, "item", bits_of("item")[-1]))

    col_own = cols[0:1]
    col = lax.dynamic_update_slice(jnp.zeros((1, buckets_own), jnp.float32), col_own, (0, item * share))
    if buckets_own == rows_total:
        both = add_over(jnp.concatenate([total, col], axis=0), "item")
        total, col = both[0:1], both[1:2]
    else:
        total, col = add_over(total, "item"), add_over(col, "item")
    row_scale = total * float(rows_total) * jnp.exp(row_first - row)
    row = row + log_rows

    update, block = final(own_left, col_own, jnp.exp(-col_own), right, row, row_scale, other, 1, own)

    def mine(values):
        return lax.dynamic_slice_in_dim(values, item * rows_own, rows_own, axis=1)

    grad, _ = final(row_left, mine(row), mine(row_scale), centroids_t, col, jnp.exp(-col), centroids_t, 2)

    new_centroids = by_item(
        spread_kernel,
        item,
        gather_blocks(update, "item"),
        jax.ShapeDtypeStruct((buckets_own, dim), jnp.float32),
        "spread",
        half=block // 2,
    )
    grad_codes = add_over(grad, "bucket")
    return (grad_codes, new_centroids)


def solution(mesh):
    return jax.shard_map(
        body,
        mesh=mesh,
        in_specs=(P("item", None), P("bucket", None)),
        out_specs=(P("item", None), P("bucket", None)),
        check_vma=False,
    )
```

```python
import functools
import math

import jax
import jax.numpy as jnp
from jax import lax
from jax.experimental import pallas as pl
from jax.experimental.pallas import tpu as pltpu
from jax.sharding import PartitionSpec as P


ITERS = 3

score_scale = 20.0
step_rate = 0.2
epsilon = 1e-06

CHUNK = 2048
LANES = 128
POTS = 16


def swap(value, axis, bit):
    size = lax.axis_size(axis)
    return lax.ppermute(value, axis, [(k, k ^ bit) for k in range(size)])


def bits_of(axis):
    size = lax.axis_size(axis)
    return [1 << k for k in range(size.bit_length() - 1)]


def add_over(value, axis):
    for bit in bits_of(axis):
        value = value + swap(value, axis, bit)
    return value


def gather_blocks(value, axis):
    held = {0: value}
    for bit in reversed(bits_of(axis)):
        for key, block in list(held.items()):
            held[key | bit] = swap(block, axis, bit)
    return held


def thirds(value):
    high = value.astype(jnp.bfloat16).astype(jnp.float32)
    middle = (value - high).astype(jnp.bfloat16).astype(jnp.float32)
    return high, middle, value - high - middle


def pots(row, width, at):
    sub = lax.broadcasted_iota(jnp.int32, (POTS, width), 0)
    high, middle, low = thirds(row)
    out = jnp.where(sub < 6, 1.0, 0.0)
    out = jnp.where(sub == at, high, out)
    out = jnp.where(sub == at + 1, middle, out)
    out = jnp.where(sub == at + 2, low, out)
    return out.astype(jnp.bfloat16)


def left_pots(row, width):
    return jnp.transpose(pots(row, width, 3).astype(jnp.float32)).astype(jnp.bfloat16)


def row_of(column):
    wide = jnp.broadcast_to(column, (column.shape[0], LANES))
    return jnp.transpose(wide)[0:8, :]


def slices(value):
    return [value[:, k * LANES : (k + 1) * LANES] for k in range(value.shape[1] // LANES)]


def folded(values, op):
    values = list(values)
    while len(values) > 1:
        values = [op(*values[k : k + 2]) if k + 1 < len(values) else values[k] for k in range(0, len(values), 2)]
    return values[0]


def place_kernel(item_ref, *refs, keys):
    pieces, out_ref = refs[: len(keys)], refs[len(keys)]
    for key, piece_ref in zip(keys, pieces):
        width = piece_ref.shape[1]
        at = pl.ds(pl.multiple_of((item_ref[0] ^ key) * width, width), width)
        out_ref[:, at] = piece_ref[...]


def table_kernel(core_ref, mine_ref, other_ref, right_ref, codes_ref):
    dim, width = mine_ref.shape
    for piece_ref, half in ((mine_ref, core_ref[0]), (other_ref, 1 - core_ref[0])):
        at = pl.ds(pl.multiple_of(half * width, width), width)
        piece = piece_ref[...]
        scaled = score_scale * piece
        high = scaled.astype(jnp.bfloat16)
        right_ref[0:dim, at] = high
        right_ref[dim : 2 * dim, at] = (scaled - high.astype(jnp.float32)).astype(jnp.bfloat16)
        codes_ref[:, at] = piece.astype(jnp.bfloat16)


def left_of(l_ref, split):
    rows = jnp.transpose(l_ref[...].astype(jnp.float32))
    if split:
        rows = score_scale * rows
        high = rows.astype(jnp.bfloat16)
        low = (rows - high.astype(jnp.float32)).astype(jnp.bfloat16)
    else:
        high = low = rows.astype(jnp.bfloat16)
    return jnp.concatenate([high, low], axis=1)


def chunk_of(width):
    return min(width, CHUNK)


def chunks(width, run):
    size = chunk_of(width)

    @pl.loop(0, width // size)
    def _(step):
        run(pl.ds(pl.multiple_of(step * size, size), size))


def cases(count, run):
    step = pl.program_id(0)

    @pl.when(step == 0)
    def _():
        run(True, False)

    if count > 1:

        @pl.when((step > 0) & (step < count))
        def _():
            run(True, True)

    @pl.when(step == count)
    def _():
        run(False, True)


def lse_kernel(l_ref, w_ref, out_ref, y_ref, part_ref, sum_ref, wide_ref, *, repeat, count):
    block, width = y_ref.shape

    def run(new, old):
        if old:
            highest = jnp.max(part_ref[...], axis=1, keepdims=True)
            wide_ref[...] = jnp.broadcast_to(highest, (block, LANES))
            sum_ref[...] = jnp.zeros(sum_ref.shape, jnp.float32)
        if new:
            part_ref[...] = jnp.full(part_ref.shape, -jnp.inf, jnp.float32)
            left = left_of(l_ref, True)

        def chunk(at):
            if old:
                terms = [jnp.exp(piece - wide_ref[...]) for piece in slices(y_ref[:, at])]
                sum_ref[...] += folded(terms, jnp.add)
            if new:
                right = jnp.concatenate([w_ref[:, at]] * repeat, axis=0)
                y = jnp.dot(left, right, preferred_element_type=jnp.float32)
                y_ref[:, at] = y
                part_ref[...] = jnp.maximum(part_ref[...], folded(slices(y), jnp.maximum))

        chunks(width, chunk)
        if old:
            summed = jnp.sum(sum_ref[...], axis=1, keepdims=True)
            lane = lax.broadcasted_iota(jnp.int32, (block, LANES), 1)
            both = jnp.where(lane == 0, wide_ref[...], summed)
            out_ref[...] = jnp.transpose(both)[0:8, :]

    cases(count, run)


def sink_kernel(
    l_ref, p_ref, w_ref, q_ref, *rest, first, rows_total, buckets_total, count
):
    if not first:
        one_ref, two_ref, *rest = rest
    sums_ref, pot_ref, row_ref, y_ref, part_ref, high_ref, wide_ref, wpot_ref, acc_ref = rest
    block, width = y_ref.shape

    def run(new, old):
        if new and not old:
            acc_ref[...] = jnp.zeros(acc_ref.shape, jnp.float32)

            def prepare(at):
                row = q_ref[0:1, at]
                if not first:
                    row = row - jnp.log((one_ref[0:1, at] + two_ref[0:1, at]) * float(rows_total))
                row_ref[0:1, at] = row
                wpot_ref[:, at] = pots(row, chunk_of(width), 0)

            chunks(width, prepare)
        if new:
            was = jnp.zeros((1, block), jnp.float32) if first else p_ref[0:1, :]
            left = jnp.concatenate([left_of(l_ref, False), left_pots(was, block)], axis=1)
            part_ref[...] = jnp.full(part_ref.shape, -jnp.inf if first else 0.0, jnp.float32)

        def chunk(at):
            if old:
                sums = [
                    jnp.sum((piece * wide_ref[...]).reshape(block // 8, 8, LANES), axis=0)
                    for piece in slices(y_ref[:, at])
                ]
                acc_ref[:, at] += jnp.concatenate(sums, axis=1)
            if new:
                right = jnp.concatenate([w_ref[:, at], wpot_ref[:, at]], axis=0)
                y = jnp.dot(left, right, preferred_element_type=jnp.float32)
                if first:
                    y_ref[:, at] = y
                    part_ref[...] = jnp.maximum(part_ref[...], folded(slices(y), jnp.maximum))
                else:
                    y = jnp.exp(y)
                    y_ref[:, at] = y
                    part_ref[...] += folded(slices(y), jnp.add)

        chunks(width, chunk)
        if new and first:
            highest = jnp.max(part_ref[...], axis=1, keepdims=True)
            high_ref[...] = jnp.broadcast_to(highest, (block, LANES))
            part_ref[...] = jnp.zeros(part_ref.shape, jnp.float32)

            def again(at):
                terms = [jnp.exp(piece - high_ref[...]) for piece in slices(y_ref[:, at])]
                y_ref[:, at] = jnp.concatenate(terms, axis=1)
                part_ref[...] += folded(terms, jnp.add)

            chunks(width, again)
        if new:
            summed = jnp.sum(part_ref[...], axis=1, keepdims=True) * float(buckets_total)
            wide_ref[...] = jnp.broadcast_to(1.0 / summed, (block, LANES))
            summed = row_of(summed)
            if first:
                pot_ref[...] = -(row_of(high_ref[...]) + jnp.log(summed))
            else:
                pot_ref[...] = was - jnp.log(summed)
        if not new:
            sums_ref[...] = jnp.sum(acc_ref[...], axis=0, keepdims=True)

    cases(count, run)


def final_kernel(l_ref, p_ref, u_ref, w_ref, q_ref, v_ref, r_ref, *rest, repeat, update):
    out_ref, wide_ref, wpot_ref, acc_ref = rest
    block = l_ref.shape[1]
    width = w_ref.shape[1]

    @pl.when(pl.program_id(0) == 0)
    def _():
        def prepare(at):
            wpot_ref[:, at] = pots(q_ref[0:1, at], chunk_of(width), 0)

        chunks(width, prepare)

    left = jnp.concatenate([left_of(l_ref, not update), left_pots(p_ref[0:1, :], block)], axis=1)
    wide_ref[...] = jnp.transpose(jnp.broadcast_to(u_ref[0:1, :], (LANES, block)))
    acc_ref[...] = jnp.zeros(acc_ref.shape, jnp.float32)

    def chunk(at):
        right = jnp.concatenate([w_ref[:, at]] * repeat + [wpot_ref[:, at]], axis=0)
        y = jnp.dot(left, right, preferred_element_type=jnp.float32)
        delta = jnp.concatenate(
            [
                (jnp.exp(piece) * (wide_ref[...] * factor - 1.0)).astype(jnp.bfloat16)
                for piece, factor in zip(slices(y), slices(v_ref[0:1, at]))
            ],
            axis=1,
        )
        acc_ref[...] += lax.dot_general(
            delta, r_ref[:, at], (((1,), (1,)), ((), ())), preferred_element_type=jnp.float32
        )

    chunks(width, chunk)
    gradient = score_scale * jnp.transpose(acc_ref[...])
    if update:
        moved = l_ref[...].astype(jnp.float32) - step_rate * gradient
        gradient = moved * lax.rsqrt(jnp.mean(moved * moved, axis=0, keepdims=True) + epsilon)
    out_ref[...] = gradient


VMEM = pltpu.VMEM


def block_of(count, width):
    return min(count, 256 if width <= 16384 else 128)


def params():
    return pltpu.CompilerParams(dimension_semantics=("arbitrary",), vmem_limit_bytes=60 * 1024 * 1024)


def cost(count, width, passes):
    return pl.CostEstimate(
        flops=2 * count * width * 256 * passes, transcendentals=count * width, bytes_accessed=width * 256 * 2
    )


def full(array):
    return pl.BlockSpec(array.shape, lambda k: (0, 0))


def lse(left, right, repeat):
    (dim, rows), width = left.shape, right.shape[1]
    block = block_of(rows, width)
    count = rows // block
    return pl.pallas_call(
        functools.partial(lse_kernel, repeat=repeat, count=count),
        grid=(count + 1,),
        in_specs=[pl.BlockSpec((dim, block), lambda k: (0, jnp.minimum(k, count - 1))), full(right)],
        out_specs=pl.BlockSpec((8, block), lambda k: (0, jnp.maximum(k - 1, 0))),
        out_shape=jax.ShapeDtypeStruct((8, rows), jnp.float32),
        scratch_shapes=[VMEM((block, width), jnp.float32)] + [VMEM((block, LANES), jnp.float32)] * 3,
        compiler_params=params(),
        cost_estimate=cost(rows, width, 1),
        name="row_lse",
    )(left, right)


def sink(left, p_rows, right, row, sums, rows_total, buckets_total):
    (dim, rows), width = left.shape, right.shape[1]
    block = block_of(rows, width)
    count = rows // block
    first = sums is None
    line = pl.BlockSpec((1, width), lambda k: (0, 0))
    lines = [row] if first else [row, *sums]
    pot_spec = pl.BlockSpec((8, block), lambda k: (0, jnp.minimum(k, count - 1)))
    return pl.pallas_call(
        functools.partial(
            sink_kernel, first=first, rows_total=rows_total, buckets_total=buckets_total, count=count
        ),
        grid=(count + 1,),
        in_specs=[
            pl.BlockSpec((dim, block), lambda k: (0, jnp.minimum(k, count - 1))),
            pot_spec,
            full(right),
        ]
        + [line] * len(lines),
        out_specs=[line, pot_spec, line],
        out_shape=[
            jax.ShapeDtypeStruct((1, width), jnp.float32),
            jax.ShapeDtypeStruct((8, rows), jnp.float32),
            jax.ShapeDtypeStruct((1, width), jnp.float32),
        ],
        scratch_shapes=[VMEM((block, width), jnp.float32)]
        + [VMEM((block, LANES), jnp.float32)] * 3
        + [VMEM((POTS, width), jnp.bfloat16), VMEM((8, width), jnp.float32)],
        compiler_params=params(),
        cost_estimate=cost(rows, width, 1),
        name="sinkhorn_first" if first else "sinkhorn_next",
    )(left, p_rows, right, *lines)


def final(left, p_row, u_row, right, q_row, v_row, other, repeat, update):
    (dim, rows), width = left.shape, right.shape[1]
    block = block_of(rows, width)
    line = pl.BlockSpec((1, width), lambda k: (0, 0))
    part = pl.BlockSpec((1, block), lambda k: (0, k))
    piece = pl.BlockSpec((dim, block), lambda k: (0, k))
    return pl.pallas_call(
        functools.partial(final_kernel, repeat=repeat, update=update),
        grid=(rows // block,),
        in_specs=[piece, part, part, full(right), line, line, full(other)],
        out_specs=piece,
        out_shape=jax.ShapeDtypeStruct((dim, rows), jnp.float32),
        scratch_shapes=[
            VMEM((block, LANES), jnp.float32),
            VMEM((POTS, width), jnp.bfloat16),
            VMEM((block, dim), jnp.float32),
        ],
        compiler_params=params(),
        cost_estimate=cost(rows, width, 2),
        name="centroid_update" if update else "code_gradient",
    )(left, p_row, u_row, right, q_row, v_row, other)


def small(kernel, index, arrays, out_shape, **settings):
    several = isinstance(out_shape, list)
    whole = lambda shape: pl.BlockSpec(shape, lambda k, index: (0, 0))
    specs = [whole(one.shape) for one in (out_shape if several else [out_shape])]
    return pl.pallas_call(
        functools.partial(kernel, **settings),
        grid_spec=pltpu.PrefetchScalarGridSpec(
            num_scalar_prefetch=1,
            grid=(1,),
            in_specs=[whole(one.shape) for one in arrays],
            out_specs=specs if several else specs[0],
        ),
        out_shape=out_shape,
        compiler_params=params(),
        cost_estimate=pl.CostEstimate(flops=0, transcendentals=0, bytes_accessed=4 << 20),
    )(index.reshape(1).astype(jnp.int32), *arrays)


def place(blocks, item):
    keys = sorted(blocks)
    dim, width = blocks[0].shape
    shape = jax.ShapeDtypeStruct((dim, width * len(keys)), jnp.float32)
    return small(place_kernel, item, [blocks[key] for key in keys], shape, keys=keys)


def step(code_rows, centroids):
    items = lax.axis_size("item")
    item = lax.axis_index("item")
    core = lax.axis_index("bucket") & 1
    rows_own, dim = code_rows.shape
    rows_total = rows_own * items
    rows_half = rows_own // 2
    buckets_own = centroids.shape[0]
    buckets_total = buckets_own * lax.axis_size("bucket")
    share = buckets_own // items
    log_rows = math.log(rows_total)
    codes_t = code_rows.T
    centroids_t = centroids.T

    def spread_rows(values):
        out = jnp.zeros((1, rows_total), jnp.float32)
        for half in range(2):
            piece = values[:, half * rows_half : (half + 1) * rows_half]
            out = lax.dynamic_update_slice(out, piece, (0, half * (rows_total // 2) + item * rows_half))
        return out

    def own_rows(values):
        return jnp.concatenate(
            [
                lax.dynamic_slice_in_dim(values, half * (rows_total // 2) + item * rows_half, rows_half, axis=1)
                for half in range(2)
            ],
            axis=1,
        )

    own_half = lax.dynamic_slice_in_dim(codes_t, core * rows_half, rows_half, axis=1).astype(jnp.float32)
    pieces = gather_blocks(own_half, "item")

    stats = []
    for part in range(2):
        stats.append(lse(codes_t[:, part * rows_half : (part + 1) * rows_half], centroids_t, 2)[0:2])
    stats = jnp.concatenate(stats, axis=1)
    for bit in bits_of("bucket"):
        received = swap(stats, "bucket", bit)
        highest = jnp.maximum(stats[0], received[0])
        summed = stats[1] * jnp.exp(stats[0] - highest) + received[1] * jnp.exp(received[0] - highest)
        stats = jnp.stack([highest, summed])
    first_own = -log_rows - (stats[0:1] + jnp.log(stats[1:2]))

    mine = place(pieces, item)
    theirs = swap(mine, "bucket", 1)
    right, other = small(
        table_kernel,
        core,
        [mine, theirs],
        [
            jax.ShapeDtypeStruct((2 * dim, rows_total), jnp.bfloat16),
            jax.ShapeDtypeStruct((dim, rows_total), jnp.bfloat16),
        ],
    )
    row = row_first = add_over(spread_rows(first_own), "item")

    own = lax.dynamic_slice_in_dim(centroids_t, item * share, share, axis=1)
    cols = jnp.zeros((8, share), jnp.float32)
    sums = None
    for iteration in range(ITERS):
        total, cols, row = sink(own, cols, right, row, sums, rows_total, buckets_total)
        total = add_over(total, "bucket")
        if iteration < ITERS - 1:
            for bit in bits_of("item")[:-1]:
                total = total + swap(total, "item", bit)
            sums = (total, swap(total, "item", bits_of("item")[-1]))

    col_own = cols[0:1]
    col = lax.dynamic_update_slice(jnp.zeros((1, buckets_own), jnp.float32), col_own, (0, item * share))
    if buckets_own == rows_total:
        both = add_over(jnp.concatenate([total, col], axis=0), "item")
        total, col = both[0:1], both[1:2]
    else:
        total, col = add_over(total, "item"), add_over(col, "item")
    row_scale = total * float(rows_total) * jnp.exp(row_first - row)
    row = row + log_rows

    update = final(own, col_own, jnp.exp(-col_own), right, row, row_scale, other, 1, True)
    pieces = gather_blocks(update, "item")

    rows_pot, rows_scale, cols_scale = own_rows(row), own_rows(row_scale), jnp.exp(-col)
    grads = []
    for part in range(4):
        at = slice(part * rows_own // 4, (part + 1) * rows_own // 4)
        grads.append(
            final(
                codes_t[:, at], rows_pot[:, at], rows_scale[:, at], centroids_t, col, cols_scale, centroids_t, 2, False
            )
        )
    new_centroids = place(pieces, item)
    grad_codes = jnp.concatenate(grads, axis=1)
    for bit in bits_of("bucket"):
        grad_codes = grad_codes + swap(grad_codes, "bucket", bit)
    return (grad_codes.T, new_centroids.T)


def solution(mesh):
    return jax.shard_map(
        step,
        mesh=mesh,
        in_specs=(P("item", None), P("bucket", None)),
        out_specs=(P("item", None), P("bucket", None)),
        check_vma=False,
    )
```

```python
import functools
import math

import jax
import jax.numpy as jnp
from jax import lax
from jax.experimental import pallas as pl
from jax.experimental.pallas import tpu as pltpu
from jax.sharding import PartitionSpec as P


ITERS = 3

score_scale = 20.0
step_rate = 0.2
epsilon = 1e-06

CHUNK = 2048
LANES = 128
POTS = 16


def swap(value, axis, bit):
    size = lax.axis_size(axis)
    return lax.ppermute(value, axis, [(k, k ^ bit) for k in range(size)])


def bits_of(axis):
    size = lax.axis_size(axis)
    return [1 << k for k in range(size.bit_length() - 1)]


def odd_swap(value, axis, bit):
    items, buckets = lax.axis_size("item"), lax.axis_size("bucket")
    pairs = []
    for item in range(items):
        for bucket in range(1, buckets, 2):
            other = (item ^ bit, bucket) if axis == "item" else (item, bucket ^ bit)
            pairs.append((item * buckets + bucket, other[0] * buckets + other[1]))
    return lax.ppermute(value, ("item", "bucket"), pairs)


def up(value):
    return lax.ppermute(value, "bucket", [(k, k + 1) for k in range(0, lax.axis_size("bucket"), 2)])


def down(value):
    return lax.ppermute(value, "bucket", [(k + 1, k) for k in range(0, lax.axis_size("bucket"), 2)])


def odd_add(value, axis, bits):
    for bit in bits:
        received = odd_swap(value, axis, bit)
        value = value + received
    return value


def gather_blocks(value, axis):
    held = {0: value}
    for bit in reversed(bits_of(axis)):
        for key, block in list(held.items()):
            held[key | bit] = swap(block, axis, bit)
    return held


def thirds(value):
    high = value.astype(jnp.bfloat16).astype(jnp.float32)
    middle = (value - high).astype(jnp.bfloat16).astype(jnp.float32)
    return high, middle, value - high - middle


def pots(row, width, at):
    sub = lax.broadcasted_iota(jnp.int32, (POTS, width), 0)
    high, middle, low = thirds(row)
    out = jnp.where(sub < 6, 1.0, 0.0)
    out = jnp.where(sub == at, high, out)
    out = jnp.where(sub == at + 1, middle, out)
    out = jnp.where(sub == at + 2, low, out)
    return out.astype(jnp.bfloat16)


def left_pots(row, width):
    return jnp.transpose(pots(row, width, 3).astype(jnp.float32)).astype(jnp.bfloat16)


def row_of(column):
    wide = jnp.broadcast_to(column, (column.shape[0], LANES))
    return jnp.transpose(wide)[0:8, :]


def slices(value):
    return [value[:, k * LANES : (k + 1) * LANES] for k in range(value.shape[1] // LANES)]


def folded(values, op):
    values = list(values)
    while len(values) > 1:
        values = [op(*values[k : k + 2]) if k + 1 < len(values) else values[k] for k in range(0, len(values), 2)]
    return values[0]


def place_kernel(item_ref, *refs, keys):
    pieces, out_ref = refs[: len(keys)], refs[len(keys)]
    for key, piece_ref in zip(keys, pieces):
        width = piece_ref.shape[1]
        at = pl.ds(pl.multiple_of((item_ref[0] ^ key) * width, width), width)
        out_ref[:, at] = piece_ref[...]


def table_kernel(core_ref, mine_ref, other_ref, right_ref, codes_ref):
    dim, width = mine_ref.shape
    for piece_ref, half in ((mine_ref, core_ref[0]), (other_ref, 1 - core_ref[0])):
        at = pl.ds(pl.multiple_of(half * width, width), width)
        piece = piece_ref[...]
        scaled = score_scale * piece
        high = scaled.astype(jnp.bfloat16)
        right_ref[0:dim, at] = high
        right_ref[dim : 2 * dim, at] = (scaled - high.astype(jnp.float32)).astype(jnp.bfloat16)
        codes_ref[:, at] = piece.astype(jnp.bfloat16)


def left_of(l_ref, split):
    rows = jnp.transpose(l_ref[...].astype(jnp.float32))
    if split:
        rows = score_scale * rows
        high = rows.astype(jnp.bfloat16)
        low = (rows - high.astype(jnp.float32)).astype(jnp.bfloat16)
    else:
        high = low = rows.astype(jnp.bfloat16)
    return jnp.concatenate([high, low], axis=1)


def chunk_of(width):
    return min(width, CHUNK)


def chunks(width, run):
    size = chunk_of(width)

    @pl.loop(0, width // size)
    def _(step):
        run(pl.ds(pl.multiple_of(step * size, size), size))


def cases(count, run):
    step = pl.program_id(0)

    @pl.when(step == 0)
    def _():
        run(True, False)

    if count > 1:

        @pl.when((step > 0) & (step < count))
        def _():
            run(True, True)

    @pl.when(step == count)
    def _():
        run(False, True)


def lse_kernel(l_ref, w_ref, *rest, repeat, count):
    out_ref, y_ref, part_ref, sum_ref, wide_ref = rest[-5:]
    block, width = y_ref.shape

    def run(new, old):
        if old:
            highest = jnp.max(part_ref[...], axis=1, keepdims=True)
            wide_ref[...] = jnp.broadcast_to(highest, (block, LANES))
            sum_ref[...] = jnp.zeros(sum_ref.shape, jnp.float32)
        if new:
            part_ref[...] = jnp.full(part_ref.shape, -jnp.inf, jnp.float32)
            left = left_of(l_ref, True)

        def chunk(at):
            if old:
                terms = [jnp.exp(piece - wide_ref[...]) for piece in slices(y_ref[:, at])]
                sum_ref[...] += folded(terms, jnp.add)
            if new:
                right = jnp.concatenate([w_ref[:, at]] * repeat, axis=0)
                y = jnp.dot(left, right, preferred_element_type=jnp.float32)
                y_ref[:, at] = y
                part_ref[...] = jnp.maximum(part_ref[...], folded(slices(y), jnp.maximum))

        chunks(width, chunk)
        if old:
            summed = jnp.sum(sum_ref[...], axis=1, keepdims=True)
            lane = lax.broadcasted_iota(jnp.int32, (block, LANES), 1)
            both = jnp.where(lane == 0, wide_ref[...], summed)
            out_ref[...] = jnp.transpose(both)[0:2, :]

    cases(count, run)


def sink_kernel(
    l_ref, w_ref, one_ref, two_ref, *rest, first, rows_total, buckets_total, count
):
    if not first:
        p_ref, q_ref, *rest = rest
    sums_ref, pot_ref, row_ref, y_ref, part_ref, high_ref, wide_ref, wpot_ref, acc_ref = rest
    block, width = y_ref.shape

    def run(new, old):
        if new and not old:
            acc_ref[...] = jnp.zeros(acc_ref.shape, jnp.float32)

            def prepare(at):
                row = one_ref[0:1, at] + two_ref[0:1, at]
                if not first:
                    row = q_ref[0:1, at] - jnp.log(row * float(rows_total))
                row_ref[0:1, at] = row
                wpot_ref[:, at] = pots(row, chunk_of(width), 0)

            chunks(width, prepare)
        if new:
            was = jnp.zeros((1, block), jnp.float32) if first else p_ref[0:1, :]
            left = jnp.concatenate([left_of(l_ref, False), left_pots(was, block)], axis=1)
            part_ref[...] = jnp.full(part_ref.shape, -jnp.inf if first else 0.0, jnp.float32)

        def chunk(at):
            if old:
                sums = [
                    jnp.sum((piece * wide_ref[...]).reshape(block // 8, 8, LANES), axis=0)
                    for piece in slices(y_ref[:, at])
                ]
                acc_ref[:, at] += jnp.concatenate(sums, axis=1)
            if new:
                right = jnp.concatenate([w_ref[:, at], wpot_ref[:, at]], axis=0)
                y = jnp.dot(left, right, preferred_element_type=jnp.float32)
                if first:
                    y_ref[:, at] = y
                    part_ref[...] = jnp.maximum(part_ref[...], folded(slices(y), jnp.maximum))
                else:
                    y = jnp.exp(y)
                    y_ref[:, at] = y
                    part_ref[...] += folded(slices(y), jnp.add)

        chunks(width, chunk)
        if new and first:
            highest = jnp.max(part_ref[...], axis=1, keepdims=True)
            high_ref[...] = jnp.broadcast_to(highest, (block, LANES))
            part_ref[...] = jnp.zeros(part_ref.shape, jnp.float32)

            def again(at):
                terms = [jnp.exp(piece - high_ref[...]) for piece in slices(y_ref[:, at])]
                y_ref[:, at] = jnp.concatenate(terms, axis=1)
                part_ref[...] += folded(terms, jnp.add)

            chunks(width, again)
        if new:
            summed = jnp.sum(part_ref[...], axis=1, keepdims=True) * float(buckets_total)
            wide_ref[...] = jnp.broadcast_to(1.0 / summed, (block, LANES))
            summed = row_of(summed)
            if first:
                pot_ref[...] = -(row_of(high_ref[...]) + jnp.log(summed))
            else:
                pot_ref[...] = was - jnp.log(summed)
        if not new:
            sums_ref[...] = jnp.sum(acc_ref[...], axis=0, keepdims=True)

    cases(count, run)


def final_kernel(l_ref, p_ref, w_ref, *rest, repeat, update, rows_total):
    out_ref, wide_ref, wpot_ref, v_ref, acc_ref = rest[-5:]
    if update:
        row_ref, start_ref, one_ref, two_ref, r_ref = rest[:5]
    else:
        col_ref, r_ref = rest[0], w_ref
    block = l_ref.shape[1]
    width = w_ref.shape[1]

    @pl.when(pl.program_id(0) == 0)
    def _():
        def prepare(at):
            if update:
                row = row_ref[0:1, at]
                mass = (one_ref[0:1, at] + two_ref[0:1, at]) * float(rows_total)
                v_ref[0:1, at] = mass * jnp.exp(start_ref[0:1, at] - row)
                row = row + math.log(rows_total)
            else:
                row = col_ref[0:1, at]
                v_ref[0:1, at] = jnp.exp(-row)
            wpot_ref[:, at] = pots(row, chunk_of(width), 0)

        chunks(width, prepare)

    factor_p = jnp.exp(-p_ref[0:1, :]) if update else p_ref[1:2, :]
    left = jnp.concatenate([left_of(l_ref, not update), left_pots(p_ref[0:1, :], block)], axis=1)
    wide_ref[...] = jnp.transpose(jnp.broadcast_to(factor_p, (LANES, block)))
    acc_ref[...] = jnp.zeros(acc_ref.shape, jnp.float32)

    def chunk(at):
        right = jnp.concatenate([w_ref[:, at]] * repeat + [wpot_ref[:, at]], axis=0)
        y = jnp.dot(left, right, preferred_element_type=jnp.float32)
        delta = jnp.concatenate(
            [
                (jnp.exp(piece) * (wide_ref[...] * factor - 1.0)).astype(jnp.bfloat16)
                for piece, factor in zip(slices(y), slices(v_ref[0:1, at]))
            ],
            axis=1,
        )
        acc_ref[...] += lax.dot_general(
            delta, r_ref[:, at], (((1,), (1,)), ((), ())), preferred_element_type=jnp.float32
        )

    chunks(width, chunk)
    gradient = score_scale * jnp.transpose(acc_ref[...])
    if update:
        moved = l_ref[...].astype(jnp.float32) - step_rate * gradient
        gradient = moved * lax.rsqrt(jnp.mean(moved * moved, axis=0, keepdims=True) + epsilon)
    out_ref[...] = gradient


VMEM = pltpu.VMEM


def block_of(count, width):
    return min(count, 256 if width <= 16384 else 128)


def params():
    return pltpu.CompilerParams(dimension_semantics=("arbitrary",), vmem_limit_bytes=60 * 1024 * 1024)


def cost(count, width, passes):
    return pl.CostEstimate(
        flops=2 * count * width * 256 * passes, transcendentals=count * width, bytes_accessed=width * 256 * 2
    )


def full(array):
    return pl.BlockSpec(array.shape, lambda k: (0, 0))


def lse(left, right, repeat, part, parts, before):
    (dim, rows), width = left.shape, right.shape[1]
    block = min(block_of(rows, width), rows // parts)
    count = rows // parts // block
    lead = part * count
    return pl.pallas_call(
        functools.partial(lse_kernel, repeat=repeat, count=count),
        grid=(count + 1,),
        in_specs=[pl.BlockSpec((dim, block), lambda k: (0, lead + jnp.minimum(k, count - 1))), full(right)]
        + [pl.BlockSpec(memory_space=pl.ANY)] * len(before),
        out_specs=pl.BlockSpec((2, block), lambda k: (0, lead + jnp.maximum(k - 1, 0))),
        out_shape=jax.ShapeDtypeStruct((2, rows), jnp.float32),
        scratch_shapes=[VMEM((block, width), jnp.float32)] + [VMEM((block, LANES), jnp.float32)] * 3,
        input_output_aliases={2: 0} if before else {},
        compiler_params=params(),
        cost_estimate=cost(rows // parts, width, 1),
        name="row_lse",
    )(left, right, *before)


def sink(left, right, one, two, old, rows_total, buckets_total):
    (dim, rows), width = left.shape, right.shape[1]
    block = block_of(rows, width)
    count = rows // block
    first = not old
    line = pl.BlockSpec((1, width), lambda k: (0, 0))
    pot_spec = pl.BlockSpec((8, block), lambda k: (0, jnp.minimum(k, count - 1)))
    return pl.pallas_call(
        functools.partial(
            sink_kernel, first=first, rows_total=rows_total, buckets_total=buckets_total, count=count
        ),
        grid=(count + 1,),
        in_specs=[
            pl.BlockSpec((dim, block), lambda k: (0, jnp.minimum(k, count - 1))),
            full(right),
            line,
            line,
        ]
        + ([] if first else [pot_spec, line]),
        out_specs=[line, pot_spec, line],
        out_shape=[
            jax.ShapeDtypeStruct((1, width), jnp.float32),
            jax.ShapeDtypeStruct((8, rows), jnp.float32),
            jax.ShapeDtypeStruct((1, width), jnp.float32),
        ],
        scratch_shapes=[VMEM((block, width), jnp.float32)]
        + [VMEM((block, LANES), jnp.float32)] * 3
        + [VMEM((POTS, width), jnp.bfloat16), VMEM((8, width), jnp.float32)],
        compiler_params=params(),
        cost_estimate=cost(rows, width, 1),
        name="sinkhorn_first" if first else "sinkhorn_next",
    )(left, right, one, two, *old)


def final(left, p_rows, right, lines, codes, repeat, update, rows_total, lead, steps, total, before):
    (dim, rows), width = left.shape, right.shape[1]
    block = block_of(rows, width)
    line = pl.BlockSpec((1, width), lambda k: (0, 0))
    into = total - steps if before else 0
    extra = [codes] if update else []
    return pl.pallas_call(
        functools.partial(final_kernel, repeat=repeat, update=update, rows_total=rows_total),
        grid=(steps,),
        in_specs=[
            pl.BlockSpec((dim, block), lambda k: (0, lead + k)),
            pl.BlockSpec((p_rows.shape[0], block), lambda k: (0, lead + k)),
            full(right),
        ]
        + [line] * len(lines)
        + [full(one) for one in extra]
        + [pl.BlockSpec(memory_space=pl.ANY)] * len(before),
        out_specs=pl.BlockSpec((dim, block), lambda k: (0, into + k)),
        out_shape=jax.ShapeDtypeStruct((dim, total * block), jnp.float32),
        scratch_shapes=[
            VMEM((block, LANES), jnp.float32),
            VMEM((POTS, width), jnp.bfloat16),
            VMEM((8, width), jnp.float32),
            VMEM((block, dim), jnp.float32),
        ],
        input_output_aliases={3 + len(lines) + len(extra): 0} if before else {},
        compiler_params=params(),
        cost_estimate=cost(steps * block, width, 2),
        name="centroid_update" if update else "code_gradient",
    )(left, p_rows, right, *lines, *extra, *before)


def small(kernel, index, arrays, out_shape, **settings):
    several = isinstance(out_shape, list)
    whole = lambda shape: pl.BlockSpec(shape, lambda k, index: (0, 0))
    specs = [whole(one.shape) for one in (out_shape if several else [out_shape])]
    return pl.pallas_call(
        functools.partial(kernel, **settings),
        grid_spec=pltpu.PrefetchScalarGridSpec(
            num_scalar_prefetch=1,
            grid=(1,),
            in_specs=[whole(one.shape) for one in arrays],
            out_specs=specs if several else specs[0],
        ),
        out_shape=out_shape,
        compiler_params=params(),
        cost_estimate=pl.CostEstimate(flops=0, transcendentals=0, bytes_accessed=4 << 20),
    )(index.reshape(1).astype(jnp.int32), *arrays)


def place(blocks, item):
    keys = sorted(blocks)
    dim, width = blocks[0].shape
    shape = jax.ShapeDtypeStruct((dim, width * len(keys)), jnp.float32)
    return small(place_kernel, item, [blocks[key] for key in keys], shape, keys=keys)


def step(code_rows, centroids):
    items = lax.axis_size("item")
    item = lax.axis_index("item")
    core = lax.axis_index("bucket") & 1
    rows_own, dim = code_rows.shape
    rows_total = rows_own * items
    rows_half = rows_own // 2
    buckets_own = centroids.shape[0]
    buckets_total = buckets_own * lax.axis_size("bucket")
    share = buckets_own // items
    log_rows = math.log(rows_total)
    codes_t = code_rows.T
    centroids_t = centroids.T

    def spread_rows(values):
        out = jnp.zeros((1, rows_total), jnp.float32)
        for half in range(2):
            piece = values[:, half * rows_half : (half + 1) * rows_half]
            out = lax.dynamic_update_slice(out, piece, (0, half * (rows_total // 2) + item * rows_half))
        return out

    def own_rows(values):
        return jnp.concatenate(
            [
                lax.dynamic_slice_in_dim(values, half * (rows_total // 2) + item * rows_half, rows_half, axis=1)
                for half in range(2)
            ],
            axis=1,
        )

    odd = core == 1
    bucket_bits, item_bits = bits_of("bucket")[1:], bits_of("item")

    def shared(value):
        return jnp.where(odd, value, 0.0), down(value)

    own_half = lax.dynamic_slice_in_dim(codes_t, core * rows_half, rows_half, axis=1).astype(jnp.float32)
    pieces = gather_blocks(own_half, "item")

    held = []
    for part in range(2):
        held = [lse(codes_t, centroids_t, 2, part, 2, held)]
    stats = held[0]
    for step_bit in [1] + bucket_bits:
        received = up(stats) if step_bit == 1 else odd_swap(stats, "bucket", step_bit)
        highest = jnp.maximum(stats[0:1], received[0:1])
        summed = stats[1:2] * jnp.exp(stats[0:1] - highest) + received[1:2] * jnp.exp(received[0:1] - highest)
        stats = jnp.concatenate([highest, summed], axis=0)
    first_own = -log_rows - (stats[0:1] + jnp.log(stats[1:2]))
    one, two = shared(odd_add(spread_rows(first_own), "item", item_bits))

    mine = place(pieces, item)
    theirs = swap(mine, "bucket", 1)
    right, codes = small(
        table_kernel,
        core,
        [mine, theirs],
        [
            jax.ShapeDtypeStruct((2 * dim, rows_total), jnp.bfloat16),
            jax.ShapeDtypeStruct((dim, rows_total), jnp.bfloat16),
        ],
    )

    own = lax.dynamic_slice_in_dim(centroids_t, item * share, share, axis=1)
    old = []
    row_first = None
    for iteration in range(ITERS):
        total, cols, row = sink(own, right, one, two, old, rows_total, buckets_total)
        old = [cols, row]
        if row_first is None:
            row_first = row
        if iteration < ITERS - 1:
            total = total + up(total)
            total = odd_add(odd_add(total, "bucket", bucket_bits), "item", item_bits)
            one, two = shared(total)

    col = lax.dynamic_update_slice(jnp.zeros((1, buckets_own), jnp.float32), cols[0:1], (0, item * share))
    received = up(jnp.concatenate([total, col], axis=1))
    total = odd_add(total + received[:, :rows_total], "bucket", bucket_bits)
    both = odd_add(jnp.concatenate([total, received[:, rows_total:], col], axis=1), "item", item_bits)
    lower = down(both[:, : rows_total + buckets_own])
    total = jnp.where(odd, both[:, :rows_total], 0.0)

    blocks = share // block_of(share, rows_total)
    update = final(own, cols, right, [row, row_first, total, lower], codes, 1, True, rows_total, 0, blocks, blocks, [])
    pieces = gather_blocks(update, "item")

    mass = (total + lower[:, :rows_total]) * float(rows_total)
    col = jnp.where(odd, both[:, rows_total + buckets_own :], lower[:, rows_total:])
    p_rows = own_rows(jnp.concatenate([row + log_rows, mass * jnp.exp(row_first - row)], axis=0))
    blocks = rows_own // block_of(rows_own, buckets_own)
    halves = []
    for half in range(2):
        held = []
        for part in range(2):
            steps = blocks // 4
            held = [
                final(
                    codes_t, p_rows, centroids_t, [col], None, 2, False, rows_total,
                    (2 * half + part) * steps, steps, 2 * steps, held,
                )
            ]
        grad = held[0]
        for bit in bits_of("bucket"):
            received = swap(grad, "bucket", bit)
            grad = grad + received
        halves.append(grad)
    new_centroids = place(pieces, item)
    return (jnp.concatenate(halves, axis=1).T, new_centroids.T)


def solution(mesh):
    return jax.shard_map(
        step,
        mesh=mesh,
        in_specs=(P("item", None), P("bucket", None)),
        out_specs=(P("item", None), P("bucket", None)),
        check_vma=False,
    )
```

```python
import functools
import math

import jax
import jax.numpy as jnp
from jax import lax
from jax.experimental import pallas as pl
from jax.experimental.pallas import tpu as pltpu
from jax.sharding import PartitionSpec as P


ITERS = 3

score_scale = 20.0
step_rate = 0.2
epsilon = 1e-06

CHUNK = 2048
LANES = 128
POTS = 16


def swap(value, axis, bit):
    size = lax.axis_size(axis)
    return lax.ppermute(value, axis, [(k, k ^ bit) for k in range(size)])


def bits_of(axis):
    size = lax.axis_size(axis)
    return [1 << k for k in range(size.bit_length() - 1)]


def joint_swap(value, flips):
    items, buckets = lax.axis_size("item"), lax.axis_size("bucket")
    item_bits = sum(bit for axis, bit in flips if axis == "item")
    bucket_bits = sum(bit for axis, bit in flips if axis == "bucket")
    pairs = [
        (item * buckets + bucket, (item ^ item_bits) * buckets + (bucket ^ bucket_bits))
        for item in range(items)
        for bucket in range(buckets)
    ]
    return lax.ppermute(value, ("item", "bucket"), pairs)


def groups_of(flips):
    pairs = [flips[k : k + 2] for k in range(0, len(flips), 2)]
    return [[[pair[0]]] if len(pair) == 1 else [[pair[0]], [pair[1]], pair] for pair in pairs]


def joined(terms):
    if len(terms) == 4:
        return (terms[0] + terms[1]) + (terms[2] + terms[3])
    return terms[0] + terms[1]


def exchanged(value, group):
    terms = [value]
    for flips in group:
        terms.append(joint_swap(value, flips))
    return terms


def gather_blocks(value, axis):
    held = {0: value}
    for bit in reversed(bits_of(axis)):
        for key, block in list(held.items()):
            held[key | bit] = swap(block, axis, bit)
    return held


def thirds(value):
    high = value.astype(jnp.bfloat16).astype(jnp.float32)
    middle = (value - high).astype(jnp.bfloat16).astype(jnp.float32)
    return high, middle, value - high - middle


def pots(row, width, at):
    sub = lax.broadcasted_iota(jnp.int32, (POTS, width), 0)
    high, middle, low = thirds(row)
    out = jnp.where(sub < 6, 1.0, 0.0)
    out = jnp.where(sub == at, high, out)
    out = jnp.where(sub == at + 1, middle, out)
    out = jnp.where(sub == at + 2, low, out)
    return out.astype(jnp.bfloat16)


def left_pots(row, width):
    return jnp.transpose(pots(row, width, 3).astype(jnp.float32)).astype(jnp.bfloat16)


def row_of(column):
    wide = jnp.broadcast_to(column, (column.shape[0], LANES))
    return jnp.transpose(wide)[0:8, :]


def slices(value):
    return [value[:, k * LANES : (k + 1) * LANES] for k in range(value.shape[1] // LANES)]


def folded(values, op):
    values = list(values)
    while len(values) > 1:
        values = [op(*values[k : k + 2]) if k + 1 < len(values) else values[k] for k in range(0, len(values), 2)]
    return values[0]


def place_kernel(item_ref, *refs, keys):
    pieces, out_ref = refs[: len(keys)], refs[len(keys)]
    for key, piece_ref in zip(keys, pieces):
        width = piece_ref.shape[1]
        at = pl.ds(pl.multiple_of((item_ref[0] ^ key) * width, width), width)
        out_ref[:, at] = piece_ref[...]


def table_kernel(core_ref, mine_ref, other_ref, right_ref, codes_ref):
    dim, width = mine_ref.shape
    for piece_ref, half in ((mine_ref, core_ref[0]), (other_ref, 1 - core_ref[0])):
        at = pl.ds(pl.multiple_of(half * width, width), width)
        piece = piece_ref[...]
        scaled = score_scale * piece
        high = scaled.astype(jnp.bfloat16)
        right_ref[0:dim, at] = high
        right_ref[dim : 2 * dim, at] = (scaled - high.astype(jnp.float32)).astype(jnp.bfloat16)
        codes_ref[:, at] = piece.astype(jnp.bfloat16)


def left_of(l_ref, split):
    rows = jnp.transpose(l_ref[...].astype(jnp.float32))
    if split:
        rows = score_scale * rows
        high = rows.astype(jnp.bfloat16)
        low = (rows - high.astype(jnp.float32)).astype(jnp.bfloat16)
    else:
        high = low = rows.astype(jnp.bfloat16)
    return jnp.concatenate([high, low], axis=1)


def chunk_of(width):
    return min(width, CHUNK)


def chunks(width, run):
    size = chunk_of(width)

    @pl.loop(0, width // size)
    def _(step):
        run(pl.ds(pl.multiple_of(step * size, size), size))


def cases(count, run):
    step = pl.program_id(0)

    @pl.when(step == 0)
    def _():
        run(True, False)

    if count > 1:

        @pl.when((step > 0) & (step < count))
        def _():
            run(True, True)

    @pl.when(step == count)
    def _():
        run(False, True)


def lse_kernel(l_ref, w_ref, *rest, repeat, count):
    out_ref, y_ref, part_ref, sum_ref, wide_ref = rest[-5:]
    block, width = y_ref.shape

    def run(new, old):
        if old:
            highest = jnp.max(part_ref[...], axis=1, keepdims=True)
            wide_ref[...] = jnp.broadcast_to(highest, (block, LANES))
            sum_ref[...] = jnp.zeros(sum_ref.shape, jnp.float32)
        if new:
            part_ref[...] = jnp.full(part_ref.shape, -jnp.inf, jnp.float32)
            left = left_of(l_ref, True)

        def chunk(at):
            if old:
                terms = [jnp.exp(piece - wide_ref[...]) for piece in slices(y_ref[:, at])]
                sum_ref[...] += folded(terms, jnp.add)
            if new:
                right = jnp.concatenate([w_ref[:, at]] * repeat, axis=0)
                y = jnp.dot(left, right, preferred_element_type=jnp.float32)
                y_ref[:, at] = y
                part_ref[...] = jnp.maximum(part_ref[...], folded(slices(y), jnp.maximum))

        chunks(width, chunk)
        if old:
            summed = jnp.sum(sum_ref[...], axis=1, keepdims=True)
            lane = lax.broadcasted_iota(jnp.int32, (block, LANES), 1)
            both = jnp.where(lane == 0, wide_ref[...], summed)
            out_ref[...] = jnp.transpose(both)[0:2, :]

    cases(count, run)


def sink_kernel(
    l_ref, w_ref, *rest, first, rows_total, buckets_total, count, terms
):
    term_refs, rest = rest[:terms], rest[terms:]
    if not first:
        p_ref, q_ref, *rest = rest
    sums_ref, pot_ref, row_ref, y_ref, part_ref, high_ref, wide_ref, wpot_ref, acc_ref = rest
    block, width = y_ref.shape

    def run(new, old):
        if new and not old:
            acc_ref[...] = jnp.zeros(acc_ref.shape, jnp.float32)

            def prepare(at):
                row = joined([term_ref[0:1, at] for term_ref in term_refs])
                if not first:
                    row = q_ref[0:1, at] - jnp.log(row * float(rows_total))
                row_ref[0:1, at] = row
                wpot_ref[:, at] = pots(row, chunk_of(width), 0)

            chunks(width, prepare)
        if new:
            was = jnp.zeros((1, block), jnp.float32) if first else p_ref[0:1, :]
            left = jnp.concatenate([left_of(l_ref, False), left_pots(was, block)], axis=1)
            part_ref[...] = jnp.full(part_ref.shape, -jnp.inf if first else 0.0, jnp.float32)

        def chunk(at):
            if old:
                sums = [
                    jnp.sum((piece * wide_ref[...]).reshape(block // 8, 8, LANES), axis=0)
                    for piece in slices(y_ref[:, at])
                ]
                acc_ref[:, at] += jnp.concatenate(sums, axis=1)
            if new:
                right = jnp.concatenate([w_ref[:, at], wpot_ref[:, at]], axis=0)
                y = jnp.dot(left, right, preferred_element_type=jnp.float32)
                if first:
                    y_ref[:, at] = y
                    part_ref[...] = jnp.maximum(part_ref[...], folded(slices(y), jnp.maximum))
                else:
                    y = jnp.exp(y)
                    y_ref[:, at] = y
                    part_ref[...] += folded(slices(y), jnp.add)

        chunks(width, chunk)
        if new and first:
            highest = jnp.max(part_ref[...], axis=1, keepdims=True)
            high_ref[...] = jnp.broadcast_to(highest, (block, LANES))
            part_ref[...] = jnp.zeros(part_ref.shape, jnp.float32)

            def again(at):
                terms = [jnp.exp(piece - high_ref[...]) for piece in slices(y_ref[:, at])]
                y_ref[:, at] = jnp.concatenate(terms, axis=1)
                part_ref[...] += folded(terms, jnp.add)

            chunks(width, again)
        if new:
            summed = jnp.sum(part_ref[...], axis=1, keepdims=True) * float(buckets_total)
            wide_ref[...] = jnp.broadcast_to(1.0 / summed, (block, LANES))
            summed = row_of(summed)
            if first:
                pot_ref[...] = -(row_of(high_ref[...]) + jnp.log(summed))
            else:
                pot_ref[...] = was - jnp.log(summed)
        if not new:
            sums_ref[...] = jnp.sum(acc_ref[...], axis=0, keepdims=True)

    cases(count, run)


def final_kernel(l_ref, p_ref, w_ref, *rest, repeat, update, rows_total, terms):
    out_ref, wide_ref, wpot_ref, v_ref, acc_ref = rest[-5:]
    if update:
        row_ref, start_ref, *term_refs = rest[: 2 + terms]
        r_ref = rest[2 + terms]
    else:
        col_ref, r_ref = rest[0], w_ref
    block = l_ref.shape[1]
    width = w_ref.shape[1]

    @pl.when(pl.program_id(0) == 0)
    def _():
        def prepare(at):
            if update:
                row = row_ref[0:1, at]
                mass = joined([term_ref[0:1, at] for term_ref in term_refs]) * float(rows_total)
                v_ref[0:1, at] = mass * jnp.exp(start_ref[0:1, at] - row)
                row = row + math.log(rows_total)
            else:
                row = col_ref[0:1, at]
                v_ref[0:1, at] = jnp.exp(-row)
            wpot_ref[:, at] = pots(row, chunk_of(width), 0)

        chunks(width, prepare)

    factor_p = jnp.exp(-p_ref[0:1, :]) if update else p_ref[1:2, :]
    left = jnp.concatenate([left_of(l_ref, not update), left_pots(p_ref[0:1, :], block)], axis=1)
    wide_ref[...] = jnp.transpose(jnp.broadcast_to(factor_p, (LANES, block)))
    acc_ref[...] = jnp.zeros(acc_ref.shape, jnp.float32)

    def chunk(at):
        right = jnp.concatenate([w_ref[:, at]] * repeat + [wpot_ref[:, at]], axis=0)
        y = jnp.dot(left, right, preferred_element_type=jnp.float32)
        delta = jnp.concatenate(
            [
                (jnp.exp(piece) * (wide_ref[...] * factor - 1.0)).astype(jnp.bfloat16)
                for piece, factor in zip(slices(y), slices(v_ref[0:1, at]))
            ],
            axis=1,
        )
        acc_ref[...] += lax.dot_general(
            delta, r_ref[:, at], (((1,), (1,)), ((), ())), preferred_element_type=jnp.float32
        )

    chunks(width, chunk)
    gradient = score_scale * jnp.transpose(acc_ref[...])
    if update:
        moved = l_ref[...].astype(jnp.float32) - step_rate * gradient
        gradient = moved * lax.rsqrt(jnp.mean(moved * moved, axis=0, keepdims=True) + epsilon)
    out_ref[...] = gradient


VMEM = pltpu.VMEM


def block_of(count, width):
    return min(count, 256 if width <= 16384 else 128)


def params():
    return pltpu.CompilerParams(dimension_semantics=("arbitrary",), vmem_limit_bytes=60 * 1024 * 1024)


def cost(count, width, passes):
    return pl.CostEstimate(
        flops=2 * count * width * 256 * passes, transcendentals=count * width, bytes_accessed=width * 256 * 2
    )


def full(array):
    return pl.BlockSpec(array.shape, lambda k: (0, 0))


def lse(left, right, repeat, part, parts, before):
    (dim, rows), width = left.shape, right.shape[1]
    block = min(block_of(rows, width), rows // parts)
    count = rows // parts // block
    lead = part * count
    return pl.pallas_call(
        functools.partial(lse_kernel, repeat=repeat, count=count),
        grid=(count + 1,),
        in_specs=[pl.BlockSpec((dim, block), lambda k: (0, lead + jnp.minimum(k, count - 1))), full(right)]
        + [pl.BlockSpec(memory_space=pl.ANY)] * len(before),
        out_specs=pl.BlockSpec((2, block), lambda k: (0, lead + jnp.maximum(k - 1, 0))),
        out_shape=jax.ShapeDtypeStruct((2, rows), jnp.float32),
        scratch_shapes=[VMEM((block, width), jnp.float32)] + [VMEM((block, LANES), jnp.float32)] * 3,
        input_output_aliases={2: 0} if before else {},
        compiler_params=params(),
        cost_estimate=cost(rows // parts, width, 1),
        name="row_lse",
    )(left, right, *before)


def sink(left, right, terms, old, rows_total, buckets_total):
    (dim, rows), width = left.shape, right.shape[1]
    block = block_of(rows, width)
    count = rows // block
    first = not old
    line = pl.BlockSpec((1, width), lambda k: (0, 0))
    pot_spec = pl.BlockSpec((8, block), lambda k: (0, jnp.minimum(k, count - 1)))
    return pl.pallas_call(
        functools.partial(
            sink_kernel, first=first, rows_total=rows_total, buckets_total=buckets_total, count=count,
            terms=len(terms),
        ),
        grid=(count + 1,),
        in_specs=[
            pl.BlockSpec((dim, block), lambda k: (0, jnp.minimum(k, count - 1))),
            full(right),
        ]
        + [line] * len(terms)
        + ([] if first else [pot_spec, line]),
        out_specs=[line, pot_spec, line],
        out_shape=[
            jax.ShapeDtypeStruct((1, width), jnp.float32),
            jax.ShapeDtypeStruct((8, rows), jnp.float32),
            jax.ShapeDtypeStruct((1, width), jnp.float32),
        ],
        scratch_shapes=[VMEM((block, width), jnp.float32)]
        + [VMEM((block, LANES), jnp.float32)] * 3
        + [VMEM((POTS, width), jnp.bfloat16), VMEM((8, width), jnp.float32)],
        compiler_params=params(),
        cost_estimate=cost(rows, width, 1),
        name="sinkhorn_first" if first else "sinkhorn_next",
    )(left, right, *terms, *old)


def final(left, p_rows, right, lines, codes, repeat, update, rows_total, lead, steps, total, before):
    (dim, rows), width = left.shape, right.shape[1]
    block = block_of(rows, width)
    line = pl.BlockSpec((1, width), lambda k: (0, 0))
    into = total - steps if before else 0
    extra = [codes] if update else []
    return pl.pallas_call(
        functools.partial(
            final_kernel, repeat=repeat, update=update, rows_total=rows_total, terms=len(lines) - 2
        ),
        grid=(steps,),
        in_specs=[
            pl.BlockSpec((dim, block), lambda k: (0, lead + k)),
            pl.BlockSpec((p_rows.shape[0], block), lambda k: (0, lead + k)),
            full(right),
        ]
        + [line] * len(lines)
        + [full(one) for one in extra]
        + [pl.BlockSpec(memory_space=pl.ANY)] * len(before),
        out_specs=pl.BlockSpec((dim, block), lambda k: (0, into + k)),
        out_shape=jax.ShapeDtypeStruct((dim, total * block), jnp.float32),
        scratch_shapes=[
            VMEM((block, LANES), jnp.float32),
            VMEM((POTS, width), jnp.bfloat16),
            VMEM((8, width), jnp.float32),
            VMEM((block, dim), jnp.float32),
        ],
        input_output_aliases={3 + len(lines) + len(extra): 0} if before else {},
        compiler_params=params(),
        cost_estimate=cost(steps * block, width, 2),
        name="centroid_update" if update else "code_gradient",
    )(left, p_rows, right, *lines, *extra, *before)


def small(kernel, index, arrays, out_shape, **settings):
    several = isinstance(out_shape, list)
    whole = lambda shape: pl.BlockSpec(shape, lambda k, index: (0, 0))
    specs = [whole(one.shape) for one in (out_shape if several else [out_shape])]
    return pl.pallas_call(
        functools.partial(kernel, **settings),
        grid_spec=pltpu.PrefetchScalarGridSpec(
            num_scalar_prefetch=1,
            grid=(1,),
            in_specs=[whole(one.shape) for one in arrays],
            out_specs=specs if several else specs[0],
        ),
        out_shape=out_shape,
        compiler_params=params(),
        cost_estimate=pl.CostEstimate(flops=0, transcendentals=0, bytes_accessed=4 << 20),
    )(index.reshape(1).astype(jnp.int32), *arrays)


def place(blocks, item):
    keys = sorted(blocks)
    dim, width = blocks[0].shape
    shape = jax.ShapeDtypeStruct((dim, width * len(keys)), jnp.float32)
    return small(place_kernel, item, [blocks[key] for key in keys], shape, keys=keys)


def step(code_rows, centroids):
    items = lax.axis_size("item")
    item = lax.axis_index("item")
    core = lax.axis_index("bucket") & 1
    rows_own, dim = code_rows.shape
    rows_total = rows_own * items
    rows_half = rows_own // 2
    buckets_own = centroids.shape[0]
    buckets_total = buckets_own * lax.axis_size("bucket")
    share = buckets_own // items
    log_rows = math.log(rows_total)
    codes_t = code_rows.T
    centroids_t = centroids.T

    def spread_rows(values, item):
        out = jnp.zeros((1, rows_total), jnp.float32)
        for half in range(2):
            piece = values[:, half * rows_half : (half + 1) * rows_half]
            out = lax.dynamic_update_slice(out, piece, (0, half * (rows_total // 2) + item * rows_half))
        return out

    def own_rows(values):
        return jnp.concatenate(
            [
                lax.dynamic_slice_in_dim(values, half * (rows_total // 2) + item * rows_half, rows_half, axis=1)
                for half in range(2)
            ],
            axis=1,
        )

    side_bits = [("bucket", bit) for bit in bits_of("bucket")[1:]]
    item_bits = [("item", bit) for bit in bits_of("item")]

    own_half = lax.dynamic_slice_in_dim(codes_t, core * rows_half, rows_half, axis=1).astype(jnp.float32)
    pieces = gather_blocks(own_half, "item")

    held = []
    for part in range(2):
        held = [lse(codes_t, centroids_t, 2, part, 2, held)]

    def merged(first, second):
        highest = jnp.maximum(first[0:1], second[0:1])
        summed = first[1:2] * jnp.exp(first[0:1] - highest) + second[1:2] * jnp.exp(second[0:1] - highest)
        return jnp.concatenate([highest, summed], axis=0)

    def potential(stats):
        return -log_rows - (stats[0:1] + jnp.log(stats[1:2]))

    stats = held[0]
    for flips in [[("bucket", 1)]] + [[flip] for flip in side_bits[:-1]]:
        stats = merged(stats, joint_swap(stats, flips))
    terms = exchanged(stats, groups_of([side_bits[-1], item_bits[0]])[0])
    rows = spread_rows(potential(merged(terms[0], terms[1])), item)
    rows = rows + spread_rows(potential(merged(terms[2], terms[3])), item ^ 1)
    groups = groups_of(item_bits[1:])
    for group in groups[:-1]:
        rows = joined(exchanged(rows, group))
    terms = exchanged(rows, groups[-1])

    mine = place(pieces, item)
    theirs = swap(mine, "bucket", 1)
    right, codes = small(
        table_kernel,
        core,
        [mine, theirs],
        [
            jax.ShapeDtypeStruct((2 * dim, rows_total), jnp.bfloat16),
            jax.ShapeDtypeStruct((dim, rows_total), jnp.bfloat16),
        ],
    )

    own = lax.dynamic_slice_in_dim(centroids_t, item * share, share, axis=1)
    old = []
    row_first = None
    for iteration in range(ITERS):
        total, cols, row = sink(own, right, terms, old, rows_total, buckets_total)
        old = [cols, row]
        if row_first is None:
            row_first = row
        if iteration < ITERS - 1:
            total = total + swap(total, "bucket", 1)
            groups = groups_of(side_bits + item_bits)
            for group in groups[:-1]:
                total = joined(exchanged(total, group))
            terms = exchanged(total, groups[-1])

    col = lax.dynamic_update_slice(jnp.zeros((1, buckets_own), jnp.float32), cols[0:1], (0, item * share))
    total = total + swap(total, "bucket", 1)
    groups = groups_of(side_bits + item_bits)
    for group in groups[:-1]:
        sums, held_cols = [total], [col]
        for flips in group:
            alone = any(axis == "bucket" for axis, _ in flips)
            sent = total if alone else jnp.concatenate([total, col], axis=1)
            received = joint_swap(sent, flips)
            sums.append(received[:, :rows_total])
            if not alone:
                held_cols.append(received[:, rows_total:])
        total = joined(sums)
        col = functools.reduce(jnp.add, held_cols)
    terms = exchanged(jnp.concatenate([total, col], axis=1), groups[-1])

    blocks = share // block_of(share, rows_total)
    update = final(
        own, cols, right, [row, row_first, *terms], codes, 1, True, rows_total, 0, blocks, blocks, []
    )
    pieces = gather_blocks(update, "item")

    both = joined(terms)
    mass, col = both[:, :rows_total] * float(rows_total), both[:, rows_total:]
    p_rows = own_rows(jnp.concatenate([row + log_rows, mass * jnp.exp(row_first - row)], axis=0))
    blocks = rows_own // block_of(rows_own, buckets_own)
    halves = []
    done = 0
    for sizes in [[blocks // 2], [blocks // 4, blocks // 4]]:
        held = []
        for steps in sizes:
            held = [
                final(codes_t, p_rows, centroids_t, [col], None, 2, False, rows_total, done, steps, sum(sizes), held)
            ]
            done += steps
        grad = held[0]
        for bit in bits_of("bucket"):
            received = swap(grad, "bucket", bit)
            grad = grad + received
        halves.append(grad)
    new_centroids = place(pieces, item)
    return (jnp.concatenate(halves, axis=1).T, new_centroids.T)


def solution(mesh):
    return jax.shard_map(
        step,
        mesh=mesh,
        in_specs=(P("item", None), P("bucket", None)),
        out_specs=(P("item", None), P("bucket", None)),
        check_vma=False,
    )
```

```python
import functools
import math

import jax
import jax.numpy as jnp
from jax import lax
from jax.experimental import pallas as pl
from jax.experimental.pallas import tpu as pltpu
from jax.sharding import PartitionSpec as P


ITERS = 3

score_scale = 20.0
step_rate = 0.2
epsilon = 1e-06

CHUNK = 2048
SUB = 512
LANES = 128
POTS = 16


def swap(value, axis, bit):
    size = lax.axis_size(axis)
    return lax.ppermute(value, axis, [(k, k ^ bit) for k in range(size)])


def bits_of(axis):
    size = lax.axis_size(axis)
    return [1 << k for k in range(size.bit_length() - 1)]


def joint_swap(value, flips):
    items, buckets = lax.axis_size("item"), lax.axis_size("bucket")
    item_bits = sum(bit for axis, bit in flips if axis == "item")
    bucket_bits = sum(bit for axis, bit in flips if axis == "bucket")
    pairs = [
        (item * buckets + bucket, (item ^ item_bits) * buckets + (bucket ^ bucket_bits))
        for item in range(items)
        for bucket in range(buckets)
    ]
    return lax.ppermute(value, ("item", "bucket"), pairs)


def groups_of(flips):
    pairs = [flips[k : k + 2] for k in range(0, len(flips), 2)]
    return [[[pair[0]]] if len(pair) == 1 else [[pair[0]], [pair[1]], pair] for pair in pairs]


def joined(terms):
    if len(terms) == 4:
        return (terms[0] + terms[1]) + (terms[2] + terms[3])
    return terms[0] + terms[1]


def exchanged(value, group):
    terms = [value]
    for flips in group:
        terms.append(joint_swap(value, flips))
    return terms


def gather_blocks(value, axis):
    held = {0: value}
    for bit in reversed(bits_of(axis)):
        for key, block in list(held.items()):
            held[key | bit] = swap(block, axis, bit)
    return held


def thirds(value):
    high = value.astype(jnp.bfloat16).astype(jnp.float32)
    middle = (value - high).astype(jnp.bfloat16).astype(jnp.float32)
    return high, middle, value - high - middle


def pots(row, width, at):
    sub = lax.broadcasted_iota(jnp.int32, (POTS, width), 0)
    high, middle, low = thirds(row)
    out = jnp.where(sub < 6, 1.0, 0.0)
    out = jnp.where(sub == at, high, out)
    out = jnp.where(sub == at + 1, middle, out)
    out = jnp.where(sub == at + 2, low, out)
    return out.astype(jnp.bfloat16)


def left_pots(row, width):
    return jnp.transpose(pots(row, width, 3).astype(jnp.float32)).astype(jnp.bfloat16)


def row_of(column):
    wide = jnp.broadcast_to(column, (column.shape[0], LANES))
    return jnp.transpose(wide)[0:8, :]


def slices(value):
    return [value[:, k * LANES : (k + 1) * LANES] for k in range(value.shape[1] // LANES)]


def folded(values, op):
    values = list(values)
    while len(values) > 1:
        values = [op(*values[k : k + 2]) if k + 1 < len(values) else values[k] for k in range(0, len(values), 2)]
    return values[0]


def place_kernel(item_ref, *refs, keys):
    pieces, out_ref = refs[: len(keys)], refs[len(keys)]
    for key, piece_ref in zip(keys, pieces):
        width = piece_ref.shape[1]
        at = pl.ds(pl.multiple_of((item_ref[0] ^ key) * width, width), width)
        out_ref[:, at] = piece_ref[...]


def table_kernel(core_ref, mine_ref, other_ref, right_ref, codes_ref):
    dim, width = mine_ref.shape
    for piece_ref, half in ((mine_ref, core_ref[0]), (other_ref, 1 - core_ref[0])):
        at = pl.ds(pl.multiple_of(half * width, width), width)
        piece = piece_ref[...]
        scaled = score_scale * piece
        high = scaled.astype(jnp.bfloat16)
        right_ref[0:dim, at] = high
        right_ref[dim : 2 * dim, at] = (scaled - high.astype(jnp.float32)).astype(jnp.bfloat16)
        codes_ref[:, at] = piece.astype(jnp.bfloat16)


def left_of(l_ref, split):
    rows = jnp.transpose(l_ref[...].astype(jnp.float32))
    if split:
        rows = score_scale * rows
        high = rows.astype(jnp.bfloat16)
        low = (rows - high.astype(jnp.float32)).astype(jnp.bfloat16)
    else:
        high = low = rows.astype(jnp.bfloat16)
    return jnp.concatenate([high, low], axis=1)


def chunk_of(width):
    return min(width, CHUNK)


def chunks(width, run):
    size = chunk_of(width)

    @pl.loop(0, width // size)
    def _(step):
        run(step, pl.ds(pl.multiple_of(step * size, size), size))


def cases(count, run):
    step = pl.program_id(0)

    @pl.when(step == 0)
    def _():
        run(True, False)

    if count > 1:

        @pl.when((step > 0) & (step < count))
        def _():
            run(True, True)

    @pl.when(step == count)
    def _():
        run(False, True)


def raised(pieces, high_ref, sum_ref):
    was = high_ref[...]
    high = jnp.maximum(was, folded(pieces, jnp.maximum))
    terms = [jnp.exp(piece - high) for piece in pieces]
    high_ref[...] = high
    sum_ref[...] = sum_ref[...] * jnp.exp(was - high) + folded(terms, jnp.add)
    return high, terms


def settled(high_ref, sum_ref):
    highest = jnp.max(high_ref[...], axis=1, keepdims=True)
    return highest, jnp.sum(sum_ref[...] * jnp.exp(high_ref[...] - highest), axis=1, keepdims=True)


def lse_kernel(l_ref, w_ref, *rest, repeat):
    out_ref, high_ref, sum_ref = rest[-3:]
    width = w_ref.shape[1]
    left = left_of(l_ref, True)
    high_ref[...] = jnp.full(high_ref.shape, -jnp.inf, jnp.float32)
    sum_ref[...] = jnp.zeros(sum_ref.shape, jnp.float32)

    def chunk(_, at):
        right = jnp.concatenate([w_ref[:, at]] * repeat, axis=0)
        for at in range(0, right.shape[1], SUB):
            y = jnp.dot(left, right[:, at : at + SUB], preferred_element_type=jnp.float32)
            raised(slices(y), high_ref, sum_ref)

    chunks(width, chunk)
    highest, summed = settled(high_ref, sum_ref)
    lane = lax.broadcasted_iota(jnp.int32, high_ref.shape, 1)
    out_ref[...] = jnp.transpose(jnp.where(lane == 0, highest, summed))[0:2, :]


def sink_kernel(
    l_ref, w_ref, *rest, first, rows_total, buckets_total, count, terms
):
    term_refs, rest = rest[:terms], rest[terms:]
    if not first:
        p_ref, q_ref, *rest = rest
    sums_ref, pot_ref, row_ref, y_ref, part_ref, high_ref, highs_ref, wide_ref, wpot_ref, acc_ref = rest
    block, width = y_ref.shape

    def run(new, old):
        if new and not old:
            acc_ref[...] = jnp.zeros(acc_ref.shape, jnp.float32)

            def prepare(_, at):
                row = joined([term_ref[0:1, at] for term_ref in term_refs])
                if not first:
                    row = q_ref[0:1, at] - jnp.log(row * float(rows_total))
                row_ref[0:1, at] = row
                wpot_ref[:, at] = pots(row, chunk_of(width), 0)

            chunks(width, prepare)
        if new:
            was = jnp.zeros((1, block), jnp.float32) if first else p_ref[0:1, :]
            left = jnp.concatenate([left_of(l_ref, False), left_pots(was, block)], axis=1)
            part_ref[...] = jnp.zeros(part_ref.shape, jnp.float32)
            if first:
                high_ref[...] = jnp.full(high_ref.shape, -jnp.inf, jnp.float32)

        def chunk(step, at):
            if old:
                each = chunk_of(width) // SUB
                sums = []
                for number, piece in enumerate(slices(y_ref[:, at])):
                    wide = wide_ref[step * each + number * LANES // SUB if first else 0]
                    sums.append(jnp.sum((piece * wide).reshape(block // 8, 8, LANES), axis=0))
                acc_ref[:, at] += jnp.concatenate(sums, axis=1)
            if new:
                right = jnp.concatenate([w_ref[:, at], wpot_ref[:, at]], axis=0)
                if first:
                    terms = []
                    for number in range(right.shape[1] // SUB):
                        piece = right[:, number * SUB : (number + 1) * SUB]
                        y = jnp.dot(left, piece, preferred_element_type=jnp.float32)
                        high, more = raised(slices(y), high_ref, part_ref)
                        highs_ref[step * (right.shape[1] // SUB) + number] = high
                        terms += more
                    y_ref[:, at] = jnp.concatenate(terms, axis=1)
                else:
                    y = jnp.exp(jnp.dot(left, right, preferred_element_type=jnp.float32))
                    y_ref[:, at] = y
                    part_ref[...] += folded(slices(y), jnp.add)

        chunks(width, chunk)
        if new and first:
            highest, summed = settled(high_ref, part_ref)
            summed = summed * float(buckets_total)
            for number in range(highs_ref.shape[0]):
                wide_ref[number] = jnp.exp(highs_ref[number] - highest) / summed
            pot_ref[...] = -row_of(highest + jnp.log(summed))
        elif new:
            summed = jnp.sum(part_ref[...], axis=1, keepdims=True) * float(buckets_total)
            wide_ref[0] = jnp.broadcast_to(1.0 / summed, (block, LANES))
            pot_ref[...] = was - jnp.log(row_of(summed))
        if not new:
            sums_ref[...] = jnp.sum(acc_ref[...], axis=0, keepdims=True)

    cases(count, run)


def final_kernel(l_ref, p_ref, w_ref, *rest, repeat, update, rows_total, terms):
    out_ref, wide_ref, wpot_ref, v_ref, acc_ref = rest[-5:]
    if update:
        row_ref, start_ref, *term_refs = rest[: 2 + terms]
        r_ref = rest[2 + terms]
    else:
        col_ref, r_ref = rest[0], w_ref
    block = l_ref.shape[1]
    width = w_ref.shape[1]

    @pl.when(pl.program_id(0) == 0)
    def _():
        def prepare(_, at):
            if update:
                row = row_ref[0:1, at]
                mass = joined([term_ref[0:1, at] for term_ref in term_refs]) * float(rows_total)
                v_ref[0:1, at] = mass * jnp.exp(start_ref[0:1, at] - row)
                row = row + math.log(rows_total)
            else:
                row = col_ref[0:1, at]
                v_ref[0:1, at] = jnp.exp(-row)
            wpot_ref[:, at] = pots(row, chunk_of(width), 0)

        chunks(width, prepare)

    factor_p = jnp.exp(-p_ref[0:1, :]) if update else p_ref[1:2, :]
    left = jnp.concatenate([left_of(l_ref, not update), left_pots(p_ref[0:1, :], block)], axis=1)
    wide_ref[...] = jnp.transpose(jnp.broadcast_to(factor_p, (LANES, block)))
    acc_ref[...] = jnp.zeros(acc_ref.shape, jnp.float32)

    def chunk(_, at):
        right = jnp.concatenate([w_ref[:, at]] * repeat + [wpot_ref[:, at]], axis=0)
        y = jnp.dot(left, right, preferred_element_type=jnp.float32)
        delta = jnp.concatenate(
            [
                (jnp.exp(piece) * (wide_ref[...] * factor - 1.0)).astype(jnp.bfloat16)
                for piece, factor in zip(slices(y), slices(v_ref[0:1, at]))
            ],
            axis=1,
        )
        acc_ref[...] += lax.dot_general(
            r_ref[:, at], delta, (((1,), (1,)), ((), ())), preferred_element_type=jnp.float32
        )

    chunks(width, chunk)
    gradient = score_scale * acc_ref[...]
    if update:
        moved = l_ref[...].astype(jnp.float32) - step_rate * gradient
        gradient = moved * lax.rsqrt(jnp.mean(moved * moved, axis=0, keepdims=True) + epsilon)
    out_ref[...] = gradient


VMEM = pltpu.VMEM


def block_of(count, width):
    return min(count, 256 if width <= 16384 else 128)


def params():
    return pltpu.CompilerParams(dimension_semantics=("arbitrary",), vmem_limit_bytes=60 * 1024 * 1024)


def cost(count, width, passes):
    return pl.CostEstimate(
        flops=2 * count * width * 256 * passes, transcendentals=count * width, bytes_accessed=width * 256 * 2
    )


def full(array):
    return pl.BlockSpec(array.shape, lambda k: (0, 0))


def lse(left, right, repeat, part, parts, before):
    (dim, rows), width = left.shape, right.shape[1]
    block = min(block_of(rows, width), rows // parts)
    count = rows // parts // block
    lead = part * count
    return pl.pallas_call(
        functools.partial(lse_kernel, repeat=repeat),
        grid=(count,),
        in_specs=[pl.BlockSpec((dim, block), lambda k: (0, lead + k)), full(right)]
        + [pl.BlockSpec(memory_space=pl.ANY)] * len(before),
        out_specs=pl.BlockSpec((2, block), lambda k: (0, lead + k)),
        out_shape=jax.ShapeDtypeStruct((2, rows), jnp.float32),
        scratch_shapes=[VMEM((block, LANES), jnp.float32)] * 2,
        input_output_aliases={2: 0} if before else {},
        compiler_params=params(),
        cost_estimate=cost(rows // parts, width, 1),
        name="row_lse",
    )(left, right, *before)


def sink(left, item, rows, right, terms, old, rows_total, buckets_total):
    dim, width = left.shape[0], right.shape[1]
    block = block_of(rows, width)
    count = rows // block
    first = not old
    line = pl.BlockSpec((1, width), lambda k, at: (0, 0))
    pot_spec = pl.BlockSpec((8, block), lambda k, at: (0, jnp.minimum(k, count - 1)))
    kernel = functools.partial(
        sink_kernel, first=first, rows_total=rows_total, buckets_total=buckets_total, count=count,
        terms=len(terms),
    )
    return pl.pallas_call(
        lambda at_ref, *refs: kernel(*refs),
        grid_spec=pltpu.PrefetchScalarGridSpec(num_scalar_prefetch=1, grid=(count + 1,),
        in_specs=[
            pl.BlockSpec((dim, block), lambda k, at: (0, at[0] * count + jnp.minimum(k, count - 1))),
            pl.BlockSpec(right.shape, lambda k, at: (0, 0)),
        ]
        + [line] * len(terms)
        + ([] if first else [pot_spec, line]),
        out_specs=[line, pot_spec, line],
        scratch_shapes=[VMEM((block, width), jnp.float32)]
        + [VMEM((block, LANES), jnp.float32)] * 2
        + [VMEM((width // SUB if first else 1, block, LANES), jnp.float32)] * 2
        + [VMEM((POTS, width), jnp.bfloat16), VMEM((8, width), jnp.float32)],
        ),
        out_shape=[
            jax.ShapeDtypeStruct((1, width), jnp.float32),
            jax.ShapeDtypeStruct((8, rows), jnp.float32),
            jax.ShapeDtypeStruct((1, width), jnp.float32),
        ],
        compiler_params=params(),
        cost_estimate=cost(rows, width, 1),
        name="sinkhorn_first" if first else "sinkhorn_next",
    )(item.reshape(1).astype(jnp.int32), left, right, *terms, *old)


def final(left, item, rows, p_rows, right, lines, codes, repeat, update, rows_total, lead, steps, total, before):
    dim, width = left.shape[0], right.shape[1]
    block = block_of(rows, width)
    count = rows // block
    into = total - steps if before else 0
    extra = [codes] if update else []
    kernel = functools.partial(
        final_kernel, repeat=repeat, update=update, rows_total=rows_total, terms=len(lines) - 2
    )
    scalars = [item.reshape(1).astype(jnp.int32)] if update else []
    line = pl.BlockSpec((1, width), lambda k, *at: (0, 0))
    in_specs = [
        pl.BlockSpec((dim, block), lambda k, *at: (0, (at[0][0] * count if at else 0) + lead + k)),
        pl.BlockSpec((p_rows.shape[0], block), lambda k, *at: (0, lead + k)),
        pl.BlockSpec(right.shape, lambda k, *at: (0, 0)),
    ]
    in_specs += [line] * len(lines) + [pl.BlockSpec(one.shape, lambda k, *at: (0, 0)) for one in extra]
    in_specs += [pl.BlockSpec(memory_space=pl.ANY)] * len(before)
    return pl.pallas_call(
        (lambda at_ref, *refs: kernel(*refs)) if update else kernel,
        grid_spec=pltpu.PrefetchScalarGridSpec(
            num_scalar_prefetch=len(scalars),
            grid=(steps,),
            in_specs=in_specs,
            out_specs=pl.BlockSpec((dim, block), lambda k, *at: (0, into + k)),
            scratch_shapes=[
                VMEM((block, LANES), jnp.float32),
                VMEM((POTS, width), jnp.bfloat16),
                VMEM((8, width), jnp.float32),
                VMEM((dim, block), jnp.float32),
            ],
        ),
        out_shape=jax.ShapeDtypeStruct((dim, total * block), jnp.float32),
        input_output_aliases={len(scalars) + 3 + len(lines) + len(extra): 0} if before else {},
        compiler_params=params(),
        cost_estimate=cost(steps * block, width, 2),
        name="centroid_update" if update else "code_gradient",
    )(*scalars, left, p_rows, right, *lines, *extra, *before)


def small(kernel, index, arrays, out_shape, **settings):
    several = isinstance(out_shape, list)
    whole = lambda shape: pl.BlockSpec(shape, lambda k, index: (0, 0))
    specs = [whole(one.shape) for one in (out_shape if several else [out_shape])]
    return pl.pallas_call(
        functools.partial(kernel, **settings),
        grid_spec=pltpu.PrefetchScalarGridSpec(
            num_scalar_prefetch=1,
            grid=(1,),
            in_specs=[whole(one.shape) for one in arrays],
            out_specs=specs if several else specs[0],
        ),
        out_shape=out_shape,
        compiler_params=params(),
        cost_estimate=pl.CostEstimate(flops=0, transcendentals=0, bytes_accessed=4 << 20),
    )(index.reshape(1).astype(jnp.int32), *arrays)


def place(blocks, item):
    keys = sorted(blocks)
    dim, width = blocks[0].shape
    shape = jax.ShapeDtypeStruct((dim, width * len(keys)), jnp.float32)
    return small(place_kernel, item, [blocks[key] for key in keys], shape, keys=keys)


def step(code_rows, centroids):
    items = lax.axis_size("item")
    item = lax.axis_index("item")
    core = lax.axis_index("bucket") & 1
    rows_own, dim = code_rows.shape
    rows_total = rows_own * items
    rows_half = rows_own // 2
    buckets_own = centroids.shape[0]
    buckets_total = buckets_own * lax.axis_size("bucket")
    share = buckets_own // items
    log_rows = math.log(rows_total)
    codes_t = code_rows.T
    centroids_t = centroids.T

    def spread_rows(values, item):
        out = jnp.zeros((1, rows_total), jnp.float32)
        for half in range(2):
            piece = values[:, half * rows_half : (half + 1) * rows_half]
            out = lax.dynamic_update_slice(out, piece, (0, half * (rows_total // 2) + item * rows_half))
        return out

    def own_rows(values):
        return jnp.concatenate(
            [
                lax.dynamic_slice_in_dim(values, half * (rows_total // 2) + item * rows_half, rows_half, axis=1)
                for half in range(2)
            ],
            axis=1,
        )

    side_bits = [("bucket", bit) for bit in bits_of("bucket")[1:]]
    item_bits = [("item", bit) for bit in bits_of("item")]

    own_half = lax.dynamic_slice_in_dim(codes_t, core * rows_half, rows_half, axis=1).astype(jnp.float32)
    pieces = gather_blocks(own_half, "item")

    held = []
    for part in range(2):
        held = [lse(codes_t, centroids_t, 2, part, 2, held)]

    def merged(first, second):
        highest = jnp.maximum(first[0:1], second[0:1])
        summed = first[1:2] * jnp.exp(first[0:1] - highest) + second[1:2] * jnp.exp(second[0:1] - highest)
        return jnp.concatenate([highest, summed], axis=0)

    def potential(stats):
        return -log_rows - (stats[0:1] + jnp.log(stats[1:2]))

    stats = held[0]
    for flips in [[("bucket", 1)]] + [[flip] for flip in side_bits[:-1]]:
        received = joint_swap(stats, flips)
        stats = merged(stats, received)
    terms = exchanged(stats, groups_of([side_bits[-1], item_bits[0]])[0])
    rows = spread_rows(potential(merged(terms[0], terms[1])), item)
    rows = rows + spread_rows(potential(merged(terms[2], terms[3])), item ^ 1)
    groups = groups_of(item_bits[1:])
    for group in groups[:-1]:
        rows = joined(exchanged(rows, group))
    terms = exchanged(rows, groups[-1])

    mine = place(pieces, item)
    theirs = swap(mine, "bucket", 1)
    right, codes = small(
        table_kernel,
        core,
        [mine, theirs],
        [
            jax.ShapeDtypeStruct((2 * dim, rows_total), jnp.bfloat16),
            jax.ShapeDtypeStruct((dim, rows_total), jnp.bfloat16),
        ],
    )

    old = []
    row_first = None
    for iteration in range(ITERS):
        total, cols, row = sink(centroids_t, item, share, right, terms, old, rows_total, buckets_total)
        old = [cols, row]
        if row_first is None:
            row_first = row
        if iteration < ITERS - 1:
            total = total + swap(total, "bucket", 1)
            groups = groups_of(side_bits + item_bits)
            for group in groups[:-1]:
                total = joined(exchanged(total, group))
            terms = exchanged(total, groups[-1])

    col = lax.dynamic_update_slice(jnp.zeros((1, buckets_own), jnp.float32), cols[0:1], (0, item * share))
    total = total + swap(total, "bucket", 1)
    groups = groups_of(side_bits + item_bits)
    for group in groups[:-1]:
        sums, held_cols = [total], [col]
        for flips in group:
            alone = any(axis == "bucket" for axis, _ in flips)
            sent = total if alone else jnp.concatenate([total, col], axis=1)
            received = joint_swap(sent, flips)
            sums.append(received[:, :rows_total])
            if not alone:
                held_cols.append(received[:, rows_total:])
        total = joined(sums)
        col = functools.reduce(jnp.add, held_cols)
    terms = exchanged(jnp.concatenate([total, col], axis=1), groups[-1])

    blocks = share // block_of(share, rows_total)
    update = final(
        centroids_t, item, share, cols, right, [row, row_first, *terms], codes, 1, True, rows_total, 0, blocks, blocks, []
    )
    pieces = gather_blocks(update, "item")

    both = joined(terms)
    mass, col = both[:, :rows_total] * float(rows_total), both[:, rows_total:]
    p_rows = own_rows(jnp.concatenate([row + log_rows, mass * jnp.exp(row_first - row)], axis=0))
    blocks = rows_own // block_of(rows_own, buckets_own)
    halves = []
    done = 0
    for sizes in [[blocks // 2], [blocks // 4, blocks // 4]]:
        held = []
        for steps in sizes:
            held = [
                final(
                    codes_t, item, rows_own, p_rows, centroids_t, [col], None, 2, False, rows_total, done, steps, sum(sizes), held
                )
            ]
            done += steps
        grad = held[0]
        for bit in bits_of("bucket"):
            received = swap(grad, "bucket", bit)
            grad = grad + received
        halves.append(grad)
    new_centroids = place(pieces, item)
    return (jnp.concatenate(halves, axis=1).T, new_centroids.T)


def solution(mesh):
    return jax.shard_map(
        step,
        mesh=mesh,
        in_specs=(P("item", None), P("bucket", None)),
        out_specs=(P("item", None), P("bucket", None)),
        check_vma=False,
    )
```

```python
import functools
import math

import jax
import jax.numpy as jnp
from jax import lax
from jax.experimental import pallas as pl
from jax.experimental.pallas import tpu as pltpu
from jax.sharding import PartitionSpec as P


ITERS = 3

score_scale = 20.0
step_rate = 0.2
epsilon = 1e-06

CHUNK = 4096
SUB = 512
LANES = 128
POTS = 16


def swap(value, axis, bit):
    size = lax.axis_size(axis)
    return lax.ppermute(value, axis, [(k, k ^ bit) for k in range(size)])


def bits_of(axis):
    size = lax.axis_size(axis)
    return [1 << k for k in range(size.bit_length() - 1)]


def joint_swap(value, flips):
    items, buckets = lax.axis_size("item"), lax.axis_size("bucket")
    item_bits = sum(bit for axis, bit in flips if axis == "item")
    bucket_bits = sum(bit for axis, bit in flips if axis == "bucket")
    pairs = [
        (item * buckets + bucket, (item ^ item_bits) * buckets + (bucket ^ bucket_bits))
        for item in range(items)
        for bucket in range(buckets)
    ]
    return lax.ppermute(value, ("item", "bucket"), pairs)


def groups_of(flips):
    pairs = [flips[k : k + 2] for k in range(0, len(flips), 2)]
    return [[[pair[0]]] if len(pair) == 1 else [[pair[0]], [pair[1]], pair] for pair in pairs]


def joined(terms):
    if len(terms) == 4:
        return (terms[0] + terms[1]) + (terms[2] + terms[3])
    return terms[0] + terms[1]


def exchanged(value, group):
    terms = [value]
    for flips in group:
        terms.append(joint_swap(value, flips))
    return terms


def gather_blocks(value, axis):
    held = {0: value}
    for bit in reversed(bits_of(axis)):
        for key, block in list(held.items()):
            held[key | bit] = swap(block, axis, bit)
    return held


def thirds(value):
    high = value.astype(jnp.bfloat16).astype(jnp.float32)
    middle = (value - high).astype(jnp.bfloat16).astype(jnp.float32)
    return high, middle, value - high - middle


def pots(row, width, at):
    sub = lax.broadcasted_iota(jnp.int32, (POTS, width), 0)
    high, middle, low = thirds(row)
    out = jnp.where(sub < 6, 1.0, 0.0)
    out = jnp.where(sub == at, high, out)
    out = jnp.where(sub == at + 1, middle, out)
    out = jnp.where(sub == at + 2, low, out)
    return out.astype(jnp.bfloat16)


def left_pots(row, width):
    return jnp.transpose(pots(row, width, 3).astype(jnp.float32)).astype(jnp.bfloat16)


def row_of(column):
    wide = jnp.broadcast_to(column, (column.shape[0], LANES))
    return jnp.transpose(wide)[0:8, :]


def slices(value):
    return [value[:, k * LANES : (k + 1) * LANES] for k in range(value.shape[1] // LANES)]


def folded(values, op):
    values = list(values)
    while len(values) > 1:
        values = [op(*values[k : k + 2]) if k + 1 < len(values) else values[k] for k in range(0, len(values), 2)]
    return values[0]


def place_kernel(item_ref, *refs, keys):
    pieces, out_ref = refs[: len(keys)], refs[len(keys)]
    for key, piece_ref in zip(keys, pieces):
        width = piece_ref.shape[1]
        at = pl.ds(pl.multiple_of((item_ref[0] ^ key) * width, width), width)
        out_ref[:, at] = piece_ref[...]


def table_kernel(core_ref, mine_ref, other_ref, right_ref, codes_ref):
    dim, width = mine_ref.shape
    for piece_ref, half in ((mine_ref, core_ref[0]), (other_ref, 1 - core_ref[0])):
        at = pl.ds(pl.multiple_of(half * width, width), width)
        piece = piece_ref[...]
        scaled = score_scale * piece
        high = scaled.astype(jnp.bfloat16)
        right_ref[0:dim, at] = high
        right_ref[dim : 2 * dim, at] = (scaled - high.astype(jnp.float32)).astype(jnp.bfloat16)
        codes_ref[:, at] = piece.astype(jnp.bfloat16)


def left_of(l_ref, split):
    rows = jnp.transpose(l_ref[...].astype(jnp.float32))
    if split:
        rows = score_scale * rows
        high = rows.astype(jnp.bfloat16)
        low = (rows - high.astype(jnp.float32)).astype(jnp.bfloat16)
    else:
        high = low = rows.astype(jnp.bfloat16)
    return jnp.concatenate([high, low], axis=1)


def chunk_of(width):
    return min(width, CHUNK)


def chunks(width, run):
    size = chunk_of(width)

    @pl.loop(0, width // size)
    def _(step):
        run(step, pl.ds(pl.multiple_of(step * size, size), size))


def cases(count, run):
    step = pl.program_id(0)

    @pl.when(step == 0)
    def _():
        run(True, False)

    if count > 1:

        @pl.when((step > 0) & (step < count))
        def _():
            run(True, True)

    @pl.when(step == count)
    def _():
        run(False, True)


def raised(pieces, high_ref, sum_ref):
    was = high_ref[...]
    high = jnp.maximum(was, folded(pieces, jnp.maximum))
    terms = [jnp.exp(piece - high) for piece in pieces]
    high_ref[...] = high
    sum_ref[...] = sum_ref[...] * jnp.exp(was - high) + folded(terms, jnp.add)
    return high, terms


def settled(high_ref, sum_ref):
    highest = jnp.max(high_ref[...], axis=1, keepdims=True)
    return highest, jnp.sum(sum_ref[...] * jnp.exp(high_ref[...] - highest), axis=1, keepdims=True)


def lse_kernel(l_ref, w_ref, *rest, repeat):
    out_ref, high_ref, sum_ref = rest[-3:]
    width = w_ref.shape[1]
    left = left_of(l_ref, True)
    high_ref[...] = jnp.full(high_ref.shape, -jnp.inf, jnp.float32)
    sum_ref[...] = jnp.zeros(sum_ref.shape, jnp.float32)

    def chunk(_, at):
        right = jnp.concatenate([w_ref[:, at]] * repeat, axis=0)
        for at in range(0, right.shape[1], SUB):
            y = jnp.dot(left, right[:, at : at + SUB], preferred_element_type=jnp.float32)
            raised(slices(y), high_ref, sum_ref)

    chunks(width, chunk)
    highest, summed = settled(high_ref, sum_ref)
    lane = lax.broadcasted_iota(jnp.int32, high_ref.shape, 1)
    out_ref[...] = jnp.transpose(jnp.where(lane == 0, highest, summed))[0:2, :]


def sink_kernel(
    l_ref, w_ref, *rest, first, rows_total, buckets_total, count, terms
):
    term_refs, rest = rest[:terms], rest[terms:]
    if not first:
        p_ref, q_ref, *rest = rest
    sums_ref, pot_ref, row_ref, y_ref, part_ref, high_ref, wide_ref, wpot_ref, acc_ref = rest
    block, width = y_ref.shape

    def run(new, old):
        if new and not old:
            acc_ref[...] = jnp.zeros(acc_ref.shape, jnp.float32)

            def prepare(_, at):
                row = joined([term_ref[0:1, at] for term_ref in term_refs])
                if not first:
                    row = q_ref[0:1, at] - jnp.log(row * float(rows_total))
                row_ref[0:1, at] = row
                wpot_ref[:, at] = pots(row, chunk_of(width), 0)

            chunks(width, prepare)
        if new:
            was = jnp.zeros((1, block), jnp.float32) if first else p_ref[0:1, :]
            left = jnp.concatenate([left_of(l_ref, False), left_pots(was, block)], axis=1)
            part_ref[...] = jnp.full(part_ref.shape, -jnp.inf if first else 0.0, jnp.float32)

        def chunk(_, at):
            if old:
                sums = [
                    jnp.sum((piece * wide_ref[...]).reshape(block // 8, 8, LANES), axis=0)
                    for piece in slices(y_ref[:, at])
                ]
                acc_ref[:, at] += jnp.concatenate(sums, axis=1)
            if new:
                right = jnp.concatenate([w_ref[:, at], wpot_ref[:, at]], axis=0)
                y = jnp.dot(left, right, preferred_element_type=jnp.float32)
                if first:
                    y_ref[:, at] = y
                    part_ref[...] = jnp.maximum(part_ref[...], folded(slices(y), jnp.maximum))
                else:
                    y = jnp.exp(y)
                    y_ref[:, at] = y
                    part_ref[...] += folded(slices(y), jnp.add)

        chunks(width, chunk)
        if new and first:
            highest = jnp.max(part_ref[...], axis=1, keepdims=True)
            high_ref[...] = jnp.broadcast_to(highest, (block, LANES))
            part_ref[...] = jnp.zeros(part_ref.shape, jnp.float32)

            def again(_, at):
                terms = [jnp.exp(piece - high_ref[...]) for piece in slices(y_ref[:, at])]
                y_ref[:, at] = jnp.concatenate(terms, axis=1)
                part_ref[...] += folded(terms, jnp.add)

            chunks(width, again)
        if new:
            summed = jnp.sum(part_ref[...], axis=1, keepdims=True) * float(buckets_total)
            wide_ref[...] = jnp.broadcast_to(1.0 / summed, (block, LANES))
            summed = row_of(summed)
            if first:
                pot_ref[...] = -(row_of(high_ref[...]) + jnp.log(summed))
            else:
                pot_ref[...] = was - jnp.log(summed)
        if not new:
            sums_ref[...] = jnp.sum(acc_ref[...], axis=0, keepdims=True)

    cases(count, run)


def final_kernel(l_ref, p_ref, w_ref, *rest, repeat, update, rows_total, terms):
    out_ref, wide_ref, wpot_ref, v_ref, acc_ref = rest[-5:]
    if update:
        row_ref, start_ref, *term_refs = rest[: 2 + terms]
        r_ref = rest[2 + terms]
    else:
        col_ref, r_ref = rest[0], w_ref
    block = l_ref.shape[1]
    width = w_ref.shape[1]

    @pl.when(pl.program_id(0) == 0)
    def _():
        def prepare(_, at):
            if update:
                row = row_ref[0:1, at]
                mass = joined([term_ref[0:1, at] for term_ref in term_refs]) * float(rows_total)
                v_ref[0:1, at] = mass * jnp.exp(start_ref[0:1, at] - row)
                row = row + math.log(rows_total)
            else:
                row = col_ref[0:1, at]
                v_ref[0:1, at] = jnp.exp(-row)
            wpot_ref[:, at] = pots(row, chunk_of(width), 0)

        chunks(width, prepare)

    factor_p = jnp.exp(-p_ref[0:1, :]) if update else p_ref[1:2, :]
    left = jnp.concatenate([left_of(l_ref, not update), left_pots(p_ref[0:1, :], block)], axis=1)
    wide_ref[...] = jnp.transpose(jnp.broadcast_to(factor_p, (LANES, block)))
    acc_ref[...] = jnp.zeros(acc_ref.shape, jnp.float32)

    def chunk(_, at):
        right = jnp.concatenate([w_ref[:, at]] * repeat + [wpot_ref[:, at]], axis=0)
        y = jnp.dot(left, right, preferred_element_type=jnp.float32)
        delta = jnp.concatenate(
            [
                (jnp.exp(piece) * (wide_ref[...] * factor - 1.0)).astype(jnp.bfloat16)
                for piece, factor in zip(slices(y), slices(v_ref[0:1, at]))
            ],
            axis=1,
        )
        acc_ref[...] += lax.dot_general(
            delta, r_ref[:, at], (((1,), (1,)), ((), ())), preferred_element_type=jnp.float32
        )

    chunks(width, chunk)
    gradient = score_scale * jnp.transpose(acc_ref[...])
    if update:
        moved = l_ref[...].astype(jnp.float32) - step_rate * gradient
        gradient = moved * lax.rsqrt(jnp.mean(moved * moved, axis=0, keepdims=True) + epsilon)
    out_ref[...] = gradient


VMEM = pltpu.VMEM


def block_of(count, width):
    return min(count, 512 if width <= 16384 else 128)


def params():
    return pltpu.CompilerParams(dimension_semantics=("arbitrary",), vmem_limit_bytes=60 * 1024 * 1024)


def cost(count, width, passes):
    return pl.CostEstimate(
        flops=2 * count * width * 256 * passes, transcendentals=count * width, bytes_accessed=width * 256 * 2
    )


def full(array):
    return pl.BlockSpec(array.shape, lambda k: (0, 0))


def lse(left, right, repeat, part, parts, before):
    (dim, rows), width = left.shape, right.shape[1]
    block = min(block_of(rows, width), rows // parts)
    count = rows // parts // block
    lead = part * count
    return pl.pallas_call(
        functools.partial(lse_kernel, repeat=repeat),
        grid=(count,),
        in_specs=[pl.BlockSpec((dim, block), lambda k: (0, lead + k)), full(right)]
        + [pl.BlockSpec(memory_space=pl.ANY)] * len(before),
        out_specs=pl.BlockSpec((2, block), lambda k: (0, lead + k)),
        out_shape=jax.ShapeDtypeStruct((2, rows), jnp.float32),
        scratch_shapes=[VMEM((block, LANES), jnp.float32)] * 2,
        input_output_aliases={2: 0} if before else {},
        compiler_params=params(),
        cost_estimate=cost(rows // parts, width, 1),
        name="row_lse",
    )(left, right, *before)


def sink(left, item, rows, right, terms, old, rows_total, buckets_total):
    dim, width = left.shape[0], right.shape[1]
    block = block_of(rows, width)
    count = rows // block
    first = not old
    line = pl.BlockSpec((1, width), lambda k, at: (0, 0))
    pot_spec = pl.BlockSpec((8, block), lambda k, at: (0, jnp.minimum(k, count - 1)))
    kernel = functools.partial(
        sink_kernel, first=first, rows_total=rows_total, buckets_total=buckets_total, count=count,
        terms=len(terms),
    )
    return pl.pallas_call(
        lambda at_ref, *refs: kernel(*refs),
        grid_spec=pltpu.PrefetchScalarGridSpec(num_scalar_prefetch=1, grid=(count + 1,),
        in_specs=[
            pl.BlockSpec((dim, block), lambda k, at: (0, at[0] * count + jnp.minimum(k, count - 1))),
            pl.BlockSpec(right.shape, lambda k, at: (0, 0)),
        ]
        + [line] * len(terms)
        + ([] if first else [pot_spec, line]),
        out_specs=[line, pot_spec, line],
        scratch_shapes=[VMEM((block, width), jnp.float32)]
        + [VMEM((block, LANES), jnp.float32)] * 3
        + [VMEM((POTS, width), jnp.bfloat16), VMEM((8, width), jnp.float32)],
        ),
        out_shape=[
            jax.ShapeDtypeStruct((1, width), jnp.float32),
            jax.ShapeDtypeStruct((8, rows), jnp.float32),
            jax.ShapeDtypeStruct((1, width), jnp.float32),
        ],
        compiler_params=params(),
        cost_estimate=cost(rows, width, 1),
        name="sinkhorn_first" if first else "sinkhorn_next",
    )(item.reshape(1).astype(jnp.int32), left, right, *terms, *old)


def final(left, item, rows, p_rows, right, lines, codes, repeat, update, rows_total, block, lead, steps, total, before):
    dim, width = left.shape[0], right.shape[1]
    count = rows // block
    into = total - steps if before else 0
    extra = [codes] if update else []
    kernel = functools.partial(
        final_kernel, repeat=repeat, update=update, rows_total=rows_total, terms=len(lines) - 2
    )
    scalars = [item.reshape(1).astype(jnp.int32)] if update else []
    line = pl.BlockSpec((1, width), lambda k, *at: (0, 0))
    in_specs = [
        pl.BlockSpec((dim, block), lambda k, *at: (0, (at[0][0] * count if at else 0) + lead + k)),
        pl.BlockSpec((p_rows.shape[0], block), lambda k, *at: (0, lead + k)),
        pl.BlockSpec(right.shape, lambda k, *at: (0, 0)),
    ]
    in_specs += [line] * len(lines) + [pl.BlockSpec(one.shape, lambda k, *at: (0, 0)) for one in extra]
    in_specs += [pl.BlockSpec(memory_space=pl.ANY)] * len(before)
    return pl.pallas_call(
        (lambda at_ref, *refs: kernel(*refs)) if update else kernel,
        grid_spec=pltpu.PrefetchScalarGridSpec(
            num_scalar_prefetch=len(scalars),
            grid=(steps,),
            in_specs=in_specs,
            out_specs=pl.BlockSpec((dim, block), lambda k, *at: (0, into + k)),
            scratch_shapes=[
                VMEM((block, LANES), jnp.float32),
                VMEM((POTS, width), jnp.bfloat16),
                VMEM((8, width), jnp.float32),
                VMEM((block, dim), jnp.float32),
            ],
        ),
        out_shape=jax.ShapeDtypeStruct((dim, total * block), jnp.float32),
        input_output_aliases={len(scalars) + 3 + len(lines) + len(extra): 0} if before else {},
        compiler_params=params(),
        cost_estimate=cost(steps * block, width, 2),
        name="centroid_update" if update else "code_gradient",
    )(*scalars, left, p_rows, right, *lines, *extra, *before)


def small(kernel, index, arrays, out_shape, **settings):
    several = isinstance(out_shape, list)
    whole = lambda shape: pl.BlockSpec(shape, lambda k, index: (0, 0))
    specs = [whole(one.shape) for one in (out_shape if several else [out_shape])]
    return pl.pallas_call(
        functools.partial(kernel, **settings),
        grid_spec=pltpu.PrefetchScalarGridSpec(
            num_scalar_prefetch=1,
            grid=(1,),
            in_specs=[whole(one.shape) for one in arrays],
            out_specs=specs if several else specs[0],
        ),
        out_shape=out_shape,
        compiler_params=params(),
        cost_estimate=pl.CostEstimate(flops=0, transcendentals=0, bytes_accessed=4 << 20),
    )(index.reshape(1).astype(jnp.int32), *arrays)


def place(blocks, item):
    keys = sorted(blocks)
    dim, width = blocks[0].shape
    shape = jax.ShapeDtypeStruct((dim, width * len(keys)), jnp.float32)
    return small(place_kernel, item, [blocks[key] for key in keys], shape, keys=keys)


def step(code_rows, centroids):
    items = lax.axis_size("item")
    item = lax.axis_index("item")
    core = lax.axis_index("bucket") & 1
    rows_own, dim = code_rows.shape
    rows_total = rows_own * items
    rows_half = rows_own // 2
    buckets_own = centroids.shape[0]
    buckets_total = buckets_own * lax.axis_size("bucket")
    share = buckets_own // items
    log_rows = math.log(rows_total)
    codes_t = code_rows.T
    centroids_t = centroids.T

    def spread_rows(values, item):
        out = jnp.zeros((1, rows_total), jnp.float32)
        for half in range(2):
            piece = values[:, half * rows_half : (half + 1) * rows_half]
            out = lax.dynamic_update_slice(out, piece, (0, half * (rows_total // 2) + item * rows_half))
        return out

    def own_rows(values):
        return jnp.concatenate(
            [
                lax.dynamic_slice_in_dim(values, half * (rows_total // 2) + item * rows_half, rows_half, axis=1)
                for half in range(2)
            ],
            axis=1,
        )

    side_bits = [("bucket", bit) for bit in bits_of("bucket")[1:]]
    item_bits = [("item", bit) for bit in bits_of("item")]

    own_half = lax.dynamic_slice_in_dim(codes_t, core * rows_half, rows_half, axis=1).astype(jnp.float32)
    pieces = gather_blocks(own_half, "item")

    held = []
    for part in range(2):
        held = [lse(codes_t, centroids_t, 2, part, 2, held)]

    def merged(first, second):
        highest = jnp.maximum(first[0:1], second[0:1])
        summed = first[1:2] * jnp.exp(first[0:1] - highest) + second[1:2] * jnp.exp(second[0:1] - highest)
        return jnp.concatenate([highest, summed], axis=0)

    def potential(stats):
        return -log_rows - (stats[0:1] + jnp.log(stats[1:2]))

    stats = held[0]
    for flips in [[("bucket", 1)]] + [[flip] for flip in side_bits[:-1]]:
        received = joint_swap(stats, flips)
        stats = merged(stats, received)
    terms = exchanged(stats, groups_of([side_bits[-1], item_bits[0]])[0])
    rows = spread_rows(potential(merged(terms[0], terms[1])), item)
    rows = rows + spread_rows(potential(merged(terms[2], terms[3])), item ^ 1)
    groups = groups_of(item_bits[1:])
    for group in groups[:-1]:
        rows = joined(exchanged(rows, group))
    terms = exchanged(rows, groups[-1])

    mine = place(pieces, item)
    theirs = swap(mine, "bucket", 1)
    right, codes = small(
        table_kernel,
        core,
        [mine, theirs],
        [
            jax.ShapeDtypeStruct((2 * dim, rows_total), jnp.bfloat16),
            jax.ShapeDtypeStruct((dim, rows_total), jnp.bfloat16),
        ],
    )

    old = []
    row_first = None
    for iteration in range(ITERS):
        total, cols, row = sink(centroids_t, item, share, right, terms, old, rows_total, buckets_total)
        old = [cols, row]
        if row_first is None:
            row_first = row
        if iteration < ITERS - 1:
            total = total + swap(total, "bucket", 1)
            groups = groups_of(side_bits + item_bits)
            for group in groups[:-1]:
                total = joined(exchanged(total, group))
            terms = exchanged(total, groups[-1])

    col = lax.dynamic_update_slice(jnp.zeros((1, buckets_own), jnp.float32), cols[0:1], (0, item * share))
    total = total + swap(total, "bucket", 1)
    groups = groups_of(side_bits + item_bits)
    for group in groups[:-1]:
        sums, held_cols = [total], [col]
        for flips in group:
            alone = any(axis == "bucket" for axis, _ in flips)
            sent = total if alone else jnp.concatenate([total, col], axis=1)
            received = joint_swap(sent, flips)
            sums.append(received[:, :rows_total])
            if not alone:
                held_cols.append(received[:, rows_total:])
        total = joined(sums)
        col = functools.reduce(jnp.add, held_cols)
    terms = exchanged(jnp.concatenate([total, col], axis=1), groups[-1])

    block = block_of(share, rows_total)
    update = final(
        centroids_t, item, share, cols, right, [row, row_first, *terms], codes, 1, True, rows_total,
        block, 0, share // block, share // block, [],
    )
    pieces = gather_blocks(update, "item")

    both = joined(terms)
    mass, col = both[:, :rows_total] * float(rows_total), both[:, rows_total:]
    p_rows = own_rows(jnp.concatenate([row + log_rows, mass * jnp.exp(row_first - row)], axis=0))
    halves = []
    for half, calls in enumerate([1, 2]):
        held = []
        for call in range(calls):
            block = rows_half // calls
            held = [
                final(
                    codes_t, item, rows_own, p_rows, centroids_t, [col], None, 2, False, rows_total,
                    block, half * calls + call, 1, calls, held,
                )
            ]
        grad = held[0]
        for bit in bits_of("bucket"):
            received = swap(grad, "bucket", bit)
            grad = grad + received
        halves.append(grad)
    new_centroids = place(pieces, item)
    return (jnp.concatenate(halves, axis=1).T, new_centroids.T)


def solution(mesh):
    return jax.shard_map(
        step,
        mesh=mesh,
        in_specs=(P("item", None), P("bucket", None)),
        out_specs=(P("item", None), P("bucket", None)),
        check_vma=False,
    )
```

```python
import functools
import math

import jax
import jax.numpy as jnp
from jax import lax
from jax.experimental import pallas as pl
from jax.experimental.pallas import tpu as pltpu
from jax.sharding import PartitionSpec as P


ITERS = 3

score_scale = 20.0
step_rate = 0.2
epsilon = 1e-06

CHUNK = 4096
SUB = 512
LANES = 128
POTS = 16


def swap(value, axis, bit):
    size = lax.axis_size(axis)
    return lax.ppermute(value, axis, [(k, k ^ bit) for k in range(size)])


def bits_of(axis):
    size = lax.axis_size(axis)
    return [1 << k for k in range(size.bit_length() - 1)]


def joint_swap(value, flips):
    items, buckets = lax.axis_size("item"), lax.axis_size("bucket")
    item_bits = sum(bit for axis, bit in flips if axis == "item")
    bucket_bits = sum(bit for axis, bit in flips if axis == "bucket")
    pairs = [
        (item * buckets + bucket, (item ^ item_bits) * buckets + (bucket ^ bucket_bits))
        for item in range(items)
        for bucket in range(buckets)
    ]
    return lax.ppermute(value, ("item", "bucket"), pairs)


def groups_of(flips):
    pairs = [flips[k : k + 2] for k in range(0, len(flips), 2)]
    return [[[pair[0]]] if len(pair) == 1 else [[pair[0]], [pair[1]], pair] for pair in pairs]


def joined(terms):
    if len(terms) == 4:
        return (terms[0] + terms[1]) + (terms[2] + terms[3])
    return terms[0] + terms[1]


def exchanged(value, group):
    terms = [value]
    for flips in group:
        terms.append(joint_swap(value, flips))
    return terms


def gather_blocks(value, axis):
    held = {0: value}
    for bit in reversed(bits_of(axis)):
        for key, block in list(held.items()):
            held[key | bit] = swap(block, axis, bit)
    return held


def thirds(value):
    high = value.astype(jnp.bfloat16).astype(jnp.float32)
    middle = (value - high).astype(jnp.bfloat16).astype(jnp.float32)
    return high, middle, value - high - middle


def pots(row, width, at):
    sub = lax.broadcasted_iota(jnp.int32, (POTS, width), 0)
    high, middle, low = thirds(row)
    out = jnp.where(sub < 6, 1.0, 0.0)
    out = jnp.where(sub == at, high, out)
    out = jnp.where(sub == at + 1, middle, out)
    out = jnp.where(sub == at + 2, low, out)
    return out.astype(jnp.bfloat16)


def left_pots(row, width):
    return jnp.transpose(pots(row, width, 3).astype(jnp.float32)).astype(jnp.bfloat16)


def row_of(column):
    wide = jnp.broadcast_to(column, (column.shape[0], LANES))
    return jnp.transpose(wide)[0:8, :]


def slices(value):
    return [value[:, k * LANES : (k + 1) * LANES] for k in range(value.shape[1] // LANES)]


def folded(values, op):
    values = list(values)
    while len(values) > 1:
        values = [op(*values[k : k + 2]) if k + 1 < len(values) else values[k] for k in range(0, len(values), 2)]
    return values[0]


def place_kernel(item_ref, *refs, keys):
    pieces, out_ref = refs[: len(keys)], refs[len(keys)]
    for key, piece_ref in zip(keys, pieces):
        width = piece_ref.shape[1]
        at = pl.ds(pl.multiple_of((item_ref[0] ^ key) * width, width), width)
        out_ref[:, at] = piece_ref[...]


def table_kernel(core_ref, mine_ref, other_ref, right_ref, codes_ref):
    dim, width = mine_ref.shape
    for piece_ref, half in ((mine_ref, core_ref[0]), (other_ref, 1 - core_ref[0])):
        at = pl.ds(pl.multiple_of(half * width, width), width)
        piece = piece_ref[...]
        scaled = score_scale * piece
        high = scaled.astype(jnp.bfloat16)
        right_ref[0:dim, at] = high
        right_ref[dim : 2 * dim, at] = (scaled - high.astype(jnp.float32)).astype(jnp.bfloat16)
        codes_ref[:, at] = piece.astype(jnp.bfloat16)


def left_of(l_ref, split):
    rows = jnp.transpose(l_ref[...].astype(jnp.float32))
    if split:
        rows = score_scale * rows
        high = rows.astype(jnp.bfloat16)
        low = (rows - high.astype(jnp.float32)).astype(jnp.bfloat16)
    else:
        high = low = rows.astype(jnp.bfloat16)
    return jnp.concatenate([high, low], axis=1)


def chunk_of(width):
    return min(width, CHUNK)


def chunks(width, run):
    size = chunk_of(width)

    @pl.loop(0, width // size)
    def _(step):
        run(step, pl.ds(pl.multiple_of(step * size, size), size))


def cases(count, run):
    step = pl.program_id(0)

    @pl.when(step == 0)
    def _():
        run(True, False)

    if count > 1:

        @pl.when((step > 0) & (step < count))
        def _():
            run(True, True)

    @pl.when(step == count)
    def _():
        run(False, True)


def raised(pieces, high_ref, sum_ref):
    was = high_ref[...]
    high = jnp.maximum(was, folded(pieces, jnp.maximum))
    terms = [jnp.exp(piece - high) for piece in pieces]
    high_ref[...] = high
    sum_ref[...] = sum_ref[...] * jnp.exp(was - high) + folded(terms, jnp.add)
    return high, terms


def settled(high_ref, sum_ref):
    highest = jnp.max(high_ref[...], axis=1, keepdims=True)
    return highest, jnp.sum(sum_ref[...] * jnp.exp(high_ref[...] - highest), axis=1, keepdims=True)


def lse_kernel(l_ref, w_ref, *rest, repeat):
    out_ref, high_ref, sum_ref = rest[-3:]
    width = w_ref.shape[1]
    left = left_of(l_ref, True)
    high_ref[...] = jnp.full(high_ref.shape, -jnp.inf, jnp.float32)
    sum_ref[...] = jnp.zeros(sum_ref.shape, jnp.float32)

    def chunk(_, at):
        right = jnp.concatenate([w_ref[:, at]] * repeat, axis=0)
        for at in range(0, right.shape[1], SUB):
            y = jnp.dot(left, right[:, at : at + SUB], preferred_element_type=jnp.float32)
            raised(slices(y), high_ref, sum_ref)

    chunks(width, chunk)
    highest, summed = settled(high_ref, sum_ref)
    lane = lax.broadcasted_iota(jnp.int32, high_ref.shape, 1)
    out_ref[...] = jnp.transpose(jnp.where(lane == 0, highest, summed))[0:2, :]


def sink_kernel(
    l_ref, w_ref, *rest, first, rows_total, buckets_total, count, terms
):
    term_refs, rest = rest[:terms], rest[terms:]
    if not first:
        p_ref, q_ref, *rest = rest
    sums_ref, pot_ref, row_ref, y_ref, part_ref, high_ref, wide_ref, wpot_ref, acc_ref = rest
    block, width = y_ref.shape

    def run(new, old):
        if new and not old:
            acc_ref[...] = jnp.zeros(acc_ref.shape, jnp.float32)

            def prepare(_, at):
                row = joined([term_ref[0:1, at] for term_ref in term_refs])
                if not first:
                    row = q_ref[0:1, at] - jnp.log(row * float(rows_total))
                row_ref[0:1, at] = row
                wpot_ref[:, at] = pots(row, chunk_of(width), 0)

            chunks(width, prepare)
        if new:
            was = jnp.zeros((1, block), jnp.float32) if first else p_ref[0:1, :]
            left = jnp.concatenate([left_of(l_ref, False), left_pots(was, block)], axis=1)
            part_ref[...] = jnp.full(part_ref.shape, -jnp.inf if first else 0.0, jnp.float32)

        def chunk(_, at):
            if old:
                sums = [
                    jnp.sum((piece * wide_ref[...]).reshape(block // 8, 8, LANES), axis=0)
                    for piece in slices(y_ref[:, at])
                ]
                acc_ref[:, at] += jnp.concatenate(sums, axis=1)
            if new:
                right = jnp.concatenate([w_ref[:, at], wpot_ref[:, at]], axis=0)
                y = jnp.dot(left, right, preferred_element_type=jnp.float32)
                if first:
                    y_ref[:, at] = y
                    part_ref[...] = jnp.maximum(part_ref[...], folded(slices(y), jnp.maximum))
                else:
                    y = jnp.exp(y)
                    y_ref[:, at] = y
                    part_ref[...] += folded(slices(y), jnp.add)

        chunks(width, chunk)
        if new and first:
            highest = jnp.max(part_ref[...], axis=1, keepdims=True)
            high_ref[...] = jnp.broadcast_to(highest, (block, LANES))
            part_ref[...] = jnp.zeros(part_ref.shape, jnp.float32)

            def again(_, at):
                terms = [jnp.exp(piece - high_ref[...]) for piece in slices(y_ref[:, at])]
                y_ref[:, at] = jnp.concatenate(terms, axis=1)
                part_ref[...] += folded(terms, jnp.add)

            chunks(width, again)
        if new:
            summed = jnp.sum(part_ref[...], axis=1, keepdims=True) * float(buckets_total)
            wide_ref[...] = jnp.broadcast_to(1.0 / summed, (block, LANES))
            summed = row_of(summed)
            if first:
                pot_ref[...] = -(row_of(high_ref[...]) + jnp.log(summed))
            else:
                pot_ref[...] = was - jnp.log(summed)
        if not new:
            sums_ref[...] = jnp.sum(acc_ref[...], axis=0, keepdims=True)

    cases(count, run)


def final_kernel(l_ref, p_ref, w_ref, *rest, repeat, update, rows_total, terms):
    out_ref, wide_ref, wpot_ref, v_ref, acc_ref = rest[-5:]
    if update:
        row_ref, start_ref, *term_refs = rest[: 2 + terms]
        r_ref = rest[2 + terms]
    else:
        col_ref, r_ref = rest[0], w_ref
    block = l_ref.shape[1]
    width = w_ref.shape[1]

    @pl.when(pl.program_id(0) == 0)
    def _():
        def prepare(_, at):
            if update:
                row = row_ref[0:1, at]
                mass = joined([term_ref[0:1, at] for term_ref in term_refs]) * float(rows_total)
                v_ref[0:1, at] = mass * jnp.exp(start_ref[0:1, at] - row)
                row = row + math.log(rows_total)
            else:
                row = col_ref[0:1, at]
                v_ref[0:1, at] = jnp.exp(-row)
            wpot_ref[:, at] = pots(row, chunk_of(width), 0)

        chunks(width, prepare)

    factor_p = jnp.exp(-p_ref[0:1, :]) if update else p_ref[1:2, :]
    left = jnp.concatenate([left_of(l_ref, not update), left_pots(p_ref[0:1, :], block)], axis=1)
    wide_ref[...] = jnp.transpose(jnp.broadcast_to(factor_p, (LANES, block)))
    acc_ref[...] = jnp.zeros(acc_ref.shape, jnp.float32)

    def chunk(_, at):
        right = jnp.concatenate([w_ref[:, at]] * repeat + [wpot_ref[:, at]], axis=0)
        y = jnp.dot(left, right, preferred_element_type=jnp.float32)
        delta = jnp.concatenate(
            [
                (jnp.exp(piece) * (wide_ref[...] * factor - 1.0)).astype(jnp.bfloat16)
                for piece, factor in zip(slices(y), slices(v_ref[0:1, at]))
            ],
            axis=1,
        )
        acc_ref[...] += lax.dot_general(
            delta, r_ref[:, at], (((1,), (1,)), ((), ())), preferred_element_type=jnp.float32
        )

    chunks(width, chunk)
    gradient = score_scale * jnp.transpose(acc_ref[...])
    if update:
        moved = l_ref[...].astype(jnp.float32) - step_rate * gradient
        gradient = moved * lax.rsqrt(jnp.mean(moved * moved, axis=0, keepdims=True) + epsilon)
    out_ref[...] = gradient


VMEM = pltpu.VMEM


def block_of(count, width):
    return min(count, 512 if width <= 16384 else 128)


def params():
    return pltpu.CompilerParams(dimension_semantics=("arbitrary",), vmem_limit_bytes=48 * 1024 * 1024)


def cost(count, width, passes):
    return pl.CostEstimate(
        flops=2 * count * width * 256 * passes, transcendentals=count * width, bytes_accessed=width * 256 * 2
    )


def full(array):
    return pl.BlockSpec(array.shape, lambda k: (0, 0))


def lse(left, right, repeat, part, parts, before):
    (dim, rows), width = left.shape, right.shape[1]
    block = min(block_of(rows, width), rows // parts)
    count = rows // parts // block
    lead = part * count
    return pl.pallas_call(
        functools.partial(lse_kernel, repeat=repeat),
        grid=(count,),
        in_specs=[pl.BlockSpec((dim, block), lambda k: (0, lead + k)), full(right)]
        + [pl.BlockSpec(memory_space=pl.ANY)] * len(before),
        out_specs=pl.BlockSpec((2, block), lambda k: (0, lead + k)),
        out_shape=jax.ShapeDtypeStruct((2, rows), jnp.float32),
        scratch_shapes=[VMEM((block, LANES), jnp.float32)] * 2,
        input_output_aliases={2: 0} if before else {},
        compiler_params=params(),
        cost_estimate=cost(rows // parts, width, 1),
        name="row_lse",
    )(left, right, *before)


def sink(left, item, rows, right, terms, old, rows_total, buckets_total):
    dim, width = left.shape[0], right.shape[1]
    block = block_of(rows, width)
    count = rows // block
    first = not old
    line = pl.BlockSpec((1, width), lambda k, at: (0, 0))
    pot_spec = pl.BlockSpec((8, block), lambda k, at: (0, jnp.minimum(k, count - 1)))
    kernel = functools.partial(
        sink_kernel, first=first, rows_total=rows_total, buckets_total=buckets_total, count=count,
        terms=len(terms),
    )
    return pl.pallas_call(
        lambda at_ref, *refs: kernel(*refs),
        grid_spec=pltpu.PrefetchScalarGridSpec(num_scalar_prefetch=1, grid=(count + 1,),
        in_specs=[
            pl.BlockSpec((dim, block), lambda k, at: (0, at[0] * count + jnp.minimum(k, count - 1))),
            pl.BlockSpec(memory_space=pltpu.VMEM),
        ]
        + [pl.BlockSpec(memory_space=pltpu.VMEM)] * len(terms)
        + ([] if first else [pot_spec, line]),
        out_specs=[pl.BlockSpec(memory_space=pltpu.VMEM), pot_spec, line],
        scratch_shapes=[VMEM((block, width), jnp.float32)]
        + [VMEM((block, LANES), jnp.float32)] * 3
        + [VMEM((POTS, width), jnp.bfloat16), VMEM((8, width), jnp.float32)],
        ),
        out_shape=[
            jax.ShapeDtypeStruct((1, width), jnp.float32),
            jax.ShapeDtypeStruct((8, rows), jnp.float32),
            jax.ShapeDtypeStruct((1, width), jnp.float32),
        ],
        compiler_params=params(),
        cost_estimate=cost(rows, width, 1),
        name="sinkhorn_first" if first else "sinkhorn_next",
    )(item.reshape(1).astype(jnp.int32), left, right, *terms, *old)


def final(left, item, rows, p_rows, right, lines, codes, repeat, update, rows_total, block, lead, steps, total, before):
    dim, width = left.shape[0], right.shape[1]
    count = rows // block
    into = total - steps if before else 0
    extra = [codes] if update else []
    kernel = functools.partial(
        final_kernel, repeat=repeat, update=update, rows_total=rows_total, terms=len(lines) - 2
    )
    scalars = [item.reshape(1).astype(jnp.int32)] if update else []
    line = pl.BlockSpec((1, width), lambda k, *at: (0, 0))
    in_specs = [
        pl.BlockSpec((dim, block), lambda k, *at: (0, (at[0][0] * count if at else 0) + lead + k)),
        pl.BlockSpec((p_rows.shape[0], block), lambda k, *at: (0, lead + k)),
        pl.BlockSpec(memory_space=pltpu.VMEM) if update else pl.BlockSpec(right.shape, lambda k, *at: (0, 0)),
    ]
    in_specs += [line] * min(len(lines), 2) + [pl.BlockSpec(memory_space=pltpu.VMEM)] * (len(lines) - 2) + [pl.BlockSpec(memory_space=pltpu.VMEM) for one in extra]
    in_specs += [pl.BlockSpec(memory_space=pl.ANY)] * len(before)
    return pl.pallas_call(
        (lambda at_ref, *refs: kernel(*refs)) if update else kernel,
        grid_spec=pltpu.PrefetchScalarGridSpec(
            num_scalar_prefetch=len(scalars),
            grid=(steps,),
            in_specs=in_specs,
            out_specs=pl.BlockSpec((dim, block), lambda k, *at: (0, into + k)),
            scratch_shapes=[
                VMEM((block, LANES), jnp.float32),
                VMEM((POTS, width), jnp.bfloat16),
                VMEM((8, width), jnp.float32),
                VMEM((block, dim), jnp.float32),
            ],
        ),
        out_shape=jax.ShapeDtypeStruct((dim, total * block), jnp.float32),
        input_output_aliases={len(scalars) + 3 + len(lines) + len(extra): 0} if before else {},
        compiler_params=params(),
        cost_estimate=cost(steps * block, width, 2),
        name="centroid_update" if update else "code_gradient",
    )(*scalars, left, p_rows, right, *lines, *extra, *before)


def small(kernel, index, arrays, out_shape, **settings):
    several = isinstance(out_shape, list)
    near = pl.BlockSpec(memory_space=pltpu.VMEM)
    whole = lambda shape: pl.BlockSpec(shape, lambda k, index: (0, 0))
    specs = [near] * 2 if several else [whole(out_shape.shape)]
    return pl.pallas_call(
        functools.partial(kernel, **settings),
        grid_spec=pltpu.PrefetchScalarGridSpec(
            num_scalar_prefetch=1,
            grid=(1,),
            in_specs=[whole(one.shape) for one in arrays],
            out_specs=specs if several else specs[0],
        ),
        out_shape=out_shape,
        compiler_params=params(),
        cost_estimate=pl.CostEstimate(flops=0, transcendentals=0, bytes_accessed=4 << 20),
    )(index.reshape(1).astype(jnp.int32), *arrays)


def place(blocks, item):
    keys = sorted(blocks)
    dim, width = blocks[0].shape
    shape = jax.ShapeDtypeStruct((dim, width * len(keys)), jnp.float32)
    return small(place_kernel, item, [blocks[key] for key in keys], shape, keys=keys)


def store_kernel(at_ref, *refs, count):
    for number in range(count):

        @pl.when(pl.program_id(0) == number)
        def _():
            refs[-1][...] = refs[number][...]


def store(pieces, item, keys, total, before):
    dim, width = pieces[0].shape
    at = jnp.stack([item ^ key for key in keys]).astype(jnp.int32)
    return pl.pallas_call(
        functools.partial(store_kernel, count=len(keys)),
        grid_spec=pltpu.PrefetchScalarGridSpec(
            num_scalar_prefetch=1,
            grid=(len(keys),),
            in_specs=[pl.BlockSpec(memory_space=pltpu.VMEM)] * len(keys)
            + [pl.BlockSpec(memory_space=pl.ANY)] * len(before),
            out_specs=pl.BlockSpec((dim, width), lambda k, at: (0, at[k])),
        ),
        out_shape=jax.ShapeDtypeStruct((dim, width * total), jnp.float32),
        input_output_aliases={1 + len(keys): 0} if before else {},
        compiler_params=params(),
        cost_estimate=pl.CostEstimate(flops=0, transcendentals=0, bytes_accessed=(1 << 19) * len(keys)),
    )(at, *[pieces[key] for key in keys], *before)


def step(code_rows, centroids):
    items = lax.axis_size("item")
    item = lax.axis_index("item")
    core = lax.axis_index("bucket") & 1
    rows_own, dim = code_rows.shape
    rows_total = rows_own * items
    rows_half = rows_own // 2
    buckets_own = centroids.shape[0]
    buckets_total = buckets_own * lax.axis_size("bucket")
    share = buckets_own // items
    log_rows = math.log(rows_total)
    codes_t = code_rows.T
    centroids_t = centroids.T

    def spread_rows(values, item):
        out = jnp.zeros((1, rows_total), jnp.float32)
        for half in range(2):
            piece = values[:, half * rows_half : (half + 1) * rows_half]
            out = lax.dynamic_update_slice(out, piece, (0, half * (rows_total // 2) + item * rows_half))
        return out

    def own_rows(values):
        return jnp.concatenate(
            [
                lax.dynamic_slice_in_dim(values, half * (rows_total // 2) + item * rows_half, rows_half, axis=1)
                for half in range(2)
            ],
            axis=1,
        )

    side_bits = [("bucket", bit) for bit in bits_of("bucket")[1:]]
    item_bits = [("item", bit) for bit in bits_of("item")]

    own_half = lax.dynamic_slice_in_dim(codes_t, core * rows_half, rows_half, axis=1).astype(jnp.float32)
    pieces = gather_blocks(own_half, "item")

    held = []
    for part in range(2):
        held = [lse(codes_t, centroids_t, 2, part, 2, held)]

    def merged(first, second):
        highest = jnp.maximum(first[0:1], second[0:1])
        summed = first[1:2] * jnp.exp(first[0:1] - highest) + second[1:2] * jnp.exp(second[0:1] - highest)
        return jnp.concatenate([highest, summed], axis=0)

    def potential(stats):
        return -log_rows - (stats[0:1] + jnp.log(stats[1:2]))

    stats = held[0]
    for flips in [[("bucket", 1)]] + [[flip] for flip in side_bits[:-1]]:
        received = joint_swap(stats, flips)
        stats = merged(stats, received)
    terms = exchanged(stats, groups_of([side_bits[-1], item_bits[0]])[0])
    rows = spread_rows(potential(merged(terms[0], terms[1])), item)
    rows = rows + spread_rows(potential(merged(terms[2], terms[3])), item ^ 1)
    groups = groups_of(item_bits[1:])
    for group in groups[:-1]:
        rows = joined(exchanged(rows, group))
    terms = exchanged(rows, groups[-1])

    mine = place(pieces, item)
    theirs = swap(mine, "bucket", 1)
    right, codes = small(
        table_kernel,
        core,
        [mine, theirs],
        [
            jax.ShapeDtypeStruct((2 * dim, rows_total), jnp.bfloat16),
            jax.ShapeDtypeStruct((dim, rows_total), jnp.bfloat16),
        ],
    )

    old = []
    row_first = None
    for iteration in range(ITERS):
        total, cols, row = sink(centroids_t, item, share, right, terms, old, rows_total, buckets_total)
        old = [cols, row]
        if row_first is None:
            row_first = row
        if iteration < ITERS - 1:
            total = total + swap(total, "bucket", 1)
            groups = groups_of(side_bits + item_bits)
            for group in groups[:-1]:
                total = joined(exchanged(total, group))
            terms = exchanged(total, groups[-1])

    col = lax.dynamic_update_slice(jnp.zeros((1, buckets_own), jnp.float32), cols[0:1], (0, item * share))
    total = total + swap(total, "bucket", 1)
    groups = groups_of(side_bits + item_bits)
    for group in groups[:-1]:
        sums, held_cols = [total], [col]
        for flips in group:
            alone = any(axis == "bucket" for axis, _ in flips)
            sent = total if alone else jnp.concatenate([total, col], axis=1)
            received = joint_swap(sent, flips)
            sums.append(received[:, :rows_total])
            if not alone:
                held_cols.append(received[:, rows_total:])
        total = joined(sums)
        col = functools.reduce(jnp.add, held_cols)
    terms = exchanged(jnp.concatenate([total, col], axis=1), groups[-1])

    block = block_of(share, rows_total)
    update = final(
        centroids_t, item, share, cols, right, [row, row_first, *terms], codes, 1, True, rows_total,
        block, 0, share // block, share // block, [],
    )
    pieces = gather_blocks(update, "item")

    both = joined(terms)
    mass, col = both[:, :rows_total] * float(rows_total), both[:, rows_total:]
    p_rows = own_rows(jnp.concatenate([row + log_rows, mass * jnp.exp(row_first - row)], axis=0))
    halves = []
    for half, calls in enumerate([1, 2]):
        held = []
        for call in range(calls):
            block = rows_half // calls
            held = [
                final(
                    codes_t, item, rows_own, p_rows, centroids_t, [col], None, 2, False, rows_total,
                    block, half * calls + call, 1, calls, held,
                )
            ]
        grad = held[0]
        for bit in bits_of("bucket"):
            received = swap(grad, "bucket", bit)
            grad = grad + received
        halves.append(grad)
    keys = sorted(pieces)
    new_centroids = store(pieces, item, keys[:-1], items, [])
    new_centroids = store(pieces, item, keys[-1:], items, [new_centroids])
    return (jnp.concatenate(halves, axis=1).T, new_centroids.T)


def solution(mesh):
    return jax.shard_map(
        step,
        mesh=mesh,
        in_specs=(P("item", None), P("bucket", None)),
        out_specs=(P("item", None), P("bucket", None)),
        check_vma=False,
    )
```

```python
import functools
import math

import jax
import jax.numpy as jnp
from jax import lax
from jax.experimental import pallas as pl
from jax.experimental.pallas import tpu as pltpu
from jax.sharding import PartitionSpec as P


ITERS = 3

score_scale = 20.0
step_rate = 0.2
epsilon = 1e-06

CHUNK = 4096
SUB = 512
LANES = 128
POTS = 16


def swap(value, axis, bit):
    size = lax.axis_size(axis)
    return lax.ppermute(value, axis, [(k, k ^ bit) for k in range(size)])


def bits_of(axis):
    size = lax.axis_size(axis)
    return [1 << k for k in range(size.bit_length() - 1)]


def joint_swap(value, flips):
    items, buckets = lax.axis_size("item"), lax.axis_size("bucket")
    item_bits = sum(bit for axis, bit in flips if axis == "item")
    bucket_bits = sum(bit for axis, bit in flips if axis == "bucket")
    pairs = [
        (item * buckets + bucket, (item ^ item_bits) * buckets + (bucket ^ bucket_bits))
        for item in range(items)
        for bucket in range(buckets)
    ]
    return lax.ppermute(value, ("item", "bucket"), pairs)


def groups_of(flips):
    pairs = [flips[k : k + 2] for k in range(0, len(flips), 2)]
    return [[[pair[0]]] if len(pair) == 1 else [[pair[0]], [pair[1]], pair] for pair in pairs]


def joined(terms):
    if len(terms) == 4:
        return (terms[0] + terms[1]) + (terms[2] + terms[3])
    return terms[0] + terms[1]


def exchanged(value, group):
    terms = [value]
    for flips in group:
        terms.append(joint_swap(value, flips))
    return terms


def gather_blocks(value, axis):
    held = {0: value}
    for bit in reversed(bits_of(axis)):
        for key, block in list(held.items()):
            held[key | bit] = swap(block, axis, bit)
    return held


def thirds(value):
    high = value.astype(jnp.bfloat16).astype(jnp.float32)
    middle = (value - high).astype(jnp.bfloat16).astype(jnp.float32)
    return high, middle, value - high - middle


def pots(row, width, at):
    sub = lax.broadcasted_iota(jnp.int32, (POTS, width), 0)
    high, middle, low = thirds(row)
    out = jnp.where(sub < 6, 1.0, 0.0)
    out = jnp.where(sub == at, high, out)
    out = jnp.where(sub == at + 1, middle, out)
    out = jnp.where(sub == at + 2, low, out)
    return out.astype(jnp.bfloat16)


def left_pots(row, width):
    return jnp.transpose(pots(row, width, 3).astype(jnp.float32)).astype(jnp.bfloat16)


def row_of(column):
    wide = jnp.broadcast_to(column, (column.shape[0], LANES))
    return jnp.transpose(wide)[0:8, :]


def slices(value):
    return [value[:, k * LANES : (k + 1) * LANES] for k in range(value.shape[1] // LANES)]


def folded(values, op):
    values = list(values)
    while len(values) > 1:
        values = [op(*values[k : k + 2]) if k + 1 < len(values) else values[k] for k in range(0, len(values), 2)]
    return values[0]


def place_kernel(item_ref, *refs, keys):
    pieces, out_ref = refs[: len(keys)], refs[len(keys)]
    for key, piece_ref in zip(keys, pieces):
        width = piece_ref.shape[1]
        at = pl.ds(pl.multiple_of((item_ref[0] ^ key) * width, width), width)
        out_ref[:, at] = piece_ref[...]


def table_kernel(core_ref, mine_ref, other_ref, right_ref, codes_ref):
    dim, width = mine_ref.shape
    for piece_ref, half in ((mine_ref, core_ref[0]), (other_ref, 1 - core_ref[0])):
        at = pl.ds(pl.multiple_of(half * width, width), width)
        piece = piece_ref[...]
        scaled = score_scale * piece
        high = scaled.astype(jnp.bfloat16)
        right_ref[0:dim, at] = high
        right_ref[dim : 2 * dim, at] = (scaled - high.astype(jnp.float32)).astype(jnp.bfloat16)
        codes_ref[:, at] = piece.astype(jnp.bfloat16)


def left_of(l_ref, split):
    rows = jnp.transpose(l_ref[...].astype(jnp.float32))
    if split:
        rows = score_scale * rows
        high = rows.astype(jnp.bfloat16)
        low = (rows - high.astype(jnp.float32)).astype(jnp.bfloat16)
    else:
        high = low = rows.astype(jnp.bfloat16)
    return jnp.concatenate([high, low], axis=1)


def chunk_of(width):
    return min(width, CHUNK)


def chunks(width, run):
    size = chunk_of(width)

    @pl.loop(0, width // size)
    def _(step):
        run(step, pl.ds(pl.multiple_of(step * size, size), size))


def cases(count, run):
    step = pl.program_id(0)

    @pl.when(step == 0)
    def _():
        run(True, False)

    if count > 1:

        @pl.when((step > 0) & (step < count))
        def _():
            run(True, True)

    @pl.when(step == count)
    def _():
        run(False, True)


def raised(pieces, high_ref, sum_ref):
    was = high_ref[...]
    high = jnp.maximum(was, folded(pieces, jnp.maximum))
    terms = [jnp.exp(piece - high) for piece in pieces]
    high_ref[...] = high
    sum_ref[...] = sum_ref[...] * jnp.exp(was - high) + folded(terms, jnp.add)
    return high, terms


def settled(high_ref, sum_ref):
    highest = jnp.max(high_ref[...], axis=1, keepdims=True)
    return highest, jnp.sum(sum_ref[...] * jnp.exp(high_ref[...] - highest), axis=1, keepdims=True)


def lse_kernel(l_ref, w_ref, *rest, repeat):
    out_ref, high_ref, sum_ref = rest[-3:]
    width = w_ref.shape[1]
    left = left_of(l_ref, True)
    high_ref[...] = jnp.full(high_ref.shape, -jnp.inf, jnp.float32)
    sum_ref[...] = jnp.zeros(sum_ref.shape, jnp.float32)

    def chunk(_, at):
        right = jnp.concatenate([w_ref[:, at]] * repeat, axis=0)
        for at in range(0, right.shape[1], SUB):
            y = jnp.dot(left, right[:, at : at + SUB], preferred_element_type=jnp.float32)
            raised(slices(y), high_ref, sum_ref)

    chunks(width, chunk)
    highest, summed = settled(high_ref, sum_ref)
    lane = lax.broadcasted_iota(jnp.int32, high_ref.shape, 1)
    out_ref[...] = jnp.transpose(jnp.where(lane == 0, highest, summed))[0:2, :]


def sink_kernel(
    l_ref, w_ref, *rest, first, rows_total, buckets_total, count, terms
):
    term_refs, rest = rest[:terms], rest[terms:]
    if not first:
        p_ref, q_ref, *rest = rest
    sums_ref, pot_ref, row_ref, y_ref, part_ref, high_ref, wide_ref, wpot_ref, acc_ref = rest
    block, width = y_ref.shape

    def run(new, old):
        if new and not old:
            acc_ref[...] = jnp.zeros(acc_ref.shape, jnp.float32)

            def prepare(_, at):
                row = joined([term_ref[0:1, at] for term_ref in term_refs])
                if not first:
                    row = q_ref[0:1, at] - jnp.log(row * float(rows_total))
                row_ref[0:1, at] = row
                wpot_ref[:, at] = pots(row, chunk_of(width), 0)

            chunks(width, prepare)
        if new:
            was = jnp.zeros((1, block), jnp.float32) if first else p_ref[0:1, :]
            left = jnp.concatenate([left_of(l_ref, False), left_pots(was, block)], axis=1)
            part_ref[...] = jnp.full(part_ref.shape, -jnp.inf if first else 0.0, jnp.float32)

        def chunk(_, at):
            if old:
                sums = [
                    jnp.sum((piece * wide_ref[...]).reshape(block // 8, 8, LANES), axis=0)
                    for piece in slices(y_ref[:, at])
                ]
                acc_ref[:, at] += jnp.concatenate(sums, axis=1)
            if new:
                right = jnp.concatenate([w_ref[:, at], wpot_ref[:, at]], axis=0)
                y = jnp.dot(left, right, preferred_element_type=jnp.float32)
                if first:
                    y_ref[:, at] = y
                    part_ref[...] = jnp.maximum(part_ref[...], folded(slices(y), jnp.maximum))
                else:
                    y = jnp.exp(y)
                    y_ref[:, at] = y
                    part_ref[...] += folded(slices(y), jnp.add)

        chunks(width, chunk)
        if new and first:
            highest = jnp.max(part_ref[...], axis=1, keepdims=True)
            high_ref[...] = jnp.broadcast_to(highest, (block, LANES))
            part_ref[...] = jnp.zeros(part_ref.shape, jnp.float32)

            def again(_, at):
                terms = [jnp.exp(piece - high_ref[...]) for piece in slices(y_ref[:, at])]
                y_ref[:, at] = jnp.concatenate(terms, axis=1)
                part_ref[...] += folded(terms, jnp.add)

            chunks(width, again)
        if new:
            summed = jnp.sum(part_ref[...], axis=1, keepdims=True) * float(buckets_total)
            wide_ref[...] = jnp.broadcast_to(1.0 / summed, (block, LANES))
            summed = row_of(summed)
            if first:
                pot_ref[...] = -(row_of(high_ref[...]) + jnp.log(summed))
            else:
                pot_ref[...] = was - jnp.log(summed)
        if not new:
            sums_ref[...] = jnp.sum(acc_ref[...], axis=0, keepdims=True)

    cases(count, run)


def final_kernel(l_ref, p_ref, w_ref, *rest, repeat, update, rows_total, terms):
    out_ref, wide_ref, wpot_ref, v_ref, acc_ref = rest[-5:]
    if update:
        row_ref, start_ref, *term_refs = rest[: 2 + terms]
        r_ref = rest[2 + terms]
    else:
        col_ref, r_ref = rest[0], w_ref
    block = l_ref.shape[1]
    width = w_ref.shape[1]

    @pl.when(pl.program_id(0) == 0)
    def _():
        def prepare(_, at):
            if update:
                row = row_ref[0:1, at]
                mass = joined([term_ref[0:1, at] for term_ref in term_refs]) * float(rows_total)
                v_ref[0:1, at] = mass * jnp.exp(start_ref[0:1, at] - row)
                row = row + math.log(rows_total)
            else:
                row = col_ref[0:1, at]
                v_ref[0:1, at] = jnp.exp(-row)
            wpot_ref[:, at] = pots(row, chunk_of(width), 0)

        chunks(width, prepare)

    factor_p = jnp.exp(-p_ref[0:1, :]) if update else p_ref[1:2, :]
    left = jnp.concatenate([left_of(l_ref, not update), left_pots(p_ref[0:1, :], block)], axis=1)
    wide_ref[...] = jnp.transpose(jnp.broadcast_to(factor_p, (LANES, block)))
    acc_ref[...] = jnp.zeros(acc_ref.shape, jnp.float32)

    def chunk(_, at):
        right = jnp.concatenate([w_ref[:, at]] * repeat + [wpot_ref[:, at]], axis=0)
        y = jnp.dot(left, right, preferred_element_type=jnp.float32)
        delta = jnp.concatenate(
            [
                (jnp.exp(piece) * (wide_ref[...] * factor - 1.0)).astype(jnp.bfloat16)
                for piece, factor in zip(slices(y), slices(v_ref[0:1, at]))
            ],
            axis=1,
        )
        acc_ref[...] += lax.dot_general(
            delta, r_ref[:, at], (((1,), (1,)), ((), ())), preferred_element_type=jnp.float32
        )

    chunks(width, chunk)
    gradient = score_scale * jnp.transpose(acc_ref[...])
    if update:
        moved = l_ref[...].astype(jnp.float32) - step_rate * gradient
        gradient = moved * lax.rsqrt(jnp.mean(moved * moved, axis=0, keepdims=True) + epsilon)
    out_ref[...] = gradient


VMEM = pltpu.VMEM


def block_of(count, width):
    return min(count, 512 if width <= 16384 else 128)


def params():
    return pltpu.CompilerParams(dimension_semantics=("arbitrary",), vmem_limit_bytes=40 * 1024 * 1024)


def cost(count, width, passes):
    return pl.CostEstimate(
        flops=2 * count * width * 256 * passes, transcendentals=count * width, bytes_accessed=width * 256 * 2
    )


def full(array):
    return pl.BlockSpec(array.shape, lambda k: (0, 0))


def lse(left, right, repeat, part, parts, before):
    (dim, rows), width = left.shape, right.shape[1]
    block = min(block_of(rows, width), rows // parts)
    count = rows // parts // block
    lead = part * count
    return pl.pallas_call(
        functools.partial(lse_kernel, repeat=repeat),
        grid=(count,),
        in_specs=[pl.BlockSpec((dim, block), lambda k: (0, lead + k)), full(right)]
        + [pl.BlockSpec(memory_space=pl.ANY)] * len(before),
        out_specs=pl.BlockSpec((2, block), lambda k: (0, lead + k)),
        out_shape=jax.ShapeDtypeStruct((2, rows), jnp.float32),
        scratch_shapes=[VMEM((block, LANES), jnp.float32)] * 2,
        input_output_aliases={2: 0} if before else {},
        compiler_params=params(),
        cost_estimate=cost(rows // parts, width, 1),
        name="row_lse",
    )(left, right, *before)


def sink(left, item, rows, right, terms, old, rows_total, buckets_total):
    dim, width = left.shape[0], right.shape[1]
    block = block_of(rows, width)
    count = rows // block
    first = not old
    line = pl.BlockSpec((1, width), lambda k, at: (0, 0))
    pot_spec = pl.BlockSpec((8, block), lambda k, at: (0, jnp.minimum(k, count - 1)))
    kernel = functools.partial(
        sink_kernel, first=first, rows_total=rows_total, buckets_total=buckets_total, count=count,
        terms=len(terms),
    )
    return pl.pallas_call(
        lambda at_ref, *refs: kernel(*refs),
        grid_spec=pltpu.PrefetchScalarGridSpec(num_scalar_prefetch=1, grid=(count + 1,),
        in_specs=[
            pl.BlockSpec((dim, block), lambda k, at: (0, at[0] * count + jnp.minimum(k, count - 1))),
            pl.BlockSpec(memory_space=pltpu.VMEM),
        ]
        + [pl.BlockSpec(memory_space=pltpu.VMEM)] * len(terms)
        + ([] if first else [pot_spec, line]),
        out_specs=[pl.BlockSpec(memory_space=pltpu.VMEM), pot_spec, line],
        scratch_shapes=[VMEM((block, width), jnp.float32)]
        + [VMEM((block, LANES), jnp.float32)] * 3
        + [VMEM((POTS, width), jnp.bfloat16), VMEM((8, width), jnp.float32)],
        ),
        out_shape=[
            jax.ShapeDtypeStruct((1, width), jnp.float32),
            jax.ShapeDtypeStruct((8, rows), jnp.float32),
            jax.ShapeDtypeStruct((1, width), jnp.float32),
        ],
        compiler_params=params(),
        cost_estimate=cost(rows, width, 1),
        name="sinkhorn_first" if first else "sinkhorn_next",
    )(item.reshape(1).astype(jnp.int32), left, right, *terms, *old)


def final(left, item, rows, p_rows, right, lines, codes, repeat, update, rows_total, block, lead, steps, total, before):
    dim, width = left.shape[0], right.shape[1]
    count = rows // block
    into = total - steps if before else 0
    extra = [codes] if update else []
    kernel = functools.partial(
        final_kernel, repeat=repeat, update=update, rows_total=rows_total, terms=len(lines) - 2
    )
    scalars = [item.reshape(1).astype(jnp.int32)] if update else []
    line = pl.BlockSpec((1, width), lambda k, *at: (0, 0))
    in_specs = [
        pl.BlockSpec((dim, block), lambda k, *at: (0, (at[0][0] * count if at else 0) + lead + k)),
        pl.BlockSpec((p_rows.shape[0], block), lambda k, *at: (0, lead + k)),
        pl.BlockSpec(memory_space=pltpu.VMEM) if update else pl.BlockSpec(right.shape, lambda k, *at: (0, 0)),
    ]
    in_specs += [line] * min(len(lines), 2) + [pl.BlockSpec(memory_space=pltpu.VMEM)] * (len(lines) - 2) + [pl.BlockSpec(memory_space=pltpu.VMEM) for one in extra]
    in_specs += [pl.BlockSpec(memory_space=pl.ANY)] * len(before)
    return pl.pallas_call(
        (lambda at_ref, *refs: kernel(*refs)) if update else kernel,
        grid_spec=pltpu.PrefetchScalarGridSpec(
            num_scalar_prefetch=len(scalars),
            grid=(steps,),
            in_specs=in_specs,
            out_specs=pl.BlockSpec((dim, block), lambda k, *at: (0, into + k)),
            scratch_shapes=[
                VMEM((block, LANES), jnp.float32),
                VMEM((POTS, width), jnp.bfloat16),
                VMEM((8, width), jnp.float32),
                VMEM((block, dim), jnp.float32),
            ],
        ),
        out_shape=jax.ShapeDtypeStruct((dim, total * block), jnp.float32),
        input_output_aliases={len(scalars) + 3 + len(lines) + len(extra): 0} if before else {},
        compiler_params=params(),
        cost_estimate=cost(steps * block, width, 2),
        name="centroid_update" if update else "code_gradient",
    )(*scalars, left, p_rows, right, *lines, *extra, *before)


def small(kernel, index, arrays, out_shape, **settings):
    several = isinstance(out_shape, list)
    near = pl.BlockSpec(memory_space=pltpu.VMEM)
    whole = lambda shape: pl.BlockSpec(shape, lambda k, index: (0, 0))
    specs = [near] * 2 if several else [whole(out_shape.shape)]
    return pl.pallas_call(
        functools.partial(kernel, **settings),
        grid_spec=pltpu.PrefetchScalarGridSpec(
            num_scalar_prefetch=1,
            grid=(1,),
            in_specs=[whole(one.shape) for one in arrays],
            out_specs=specs if several else specs[0],
        ),
        out_shape=out_shape,
        compiler_params=params(),
        cost_estimate=pl.CostEstimate(flops=0, transcendentals=0, bytes_accessed=4 << 20),
    )(index.reshape(1).astype(jnp.int32), *arrays)


def place(blocks, item):
    keys = sorted(blocks)
    dim, width = blocks[0].shape
    shape = jax.ShapeDtypeStruct((dim, width * len(keys)), jnp.float32)
    return small(place_kernel, item, [blocks[key] for key in keys], shape, keys=keys)


def store_kernel(at_ref, *refs, count):
    for number in range(count):

        @pl.when(pl.program_id(0) == number)
        def _():
            refs[-1][...] = refs[number][...]


def store(pieces, item, keys, total, before):
    dim, width = pieces[0].shape
    at = jnp.stack([item ^ key for key in keys]).astype(jnp.int32)
    return pl.pallas_call(
        functools.partial(store_kernel, count=len(keys)),
        grid_spec=pltpu.PrefetchScalarGridSpec(
            num_scalar_prefetch=1,
            grid=(len(keys),),
            in_specs=[pl.BlockSpec(memory_space=pltpu.VMEM)] * len(keys)
            + [pl.BlockSpec(memory_space=pl.ANY)] * len(before),
            out_specs=pl.BlockSpec((dim, width), lambda k, at: (0, at[k])),
        ),
        out_shape=jax.ShapeDtypeStruct((dim, width * total), jnp.float32),
        input_output_aliases={1 + len(keys): 0} if before else {},
        compiler_params=params(),
        cost_estimate=pl.CostEstimate(flops=0, transcendentals=0, bytes_accessed=(1 << 19) * len(keys)),
    )(at, *[pieces[key] for key in keys], *before)


def step(code_rows, centroids):
    items = lax.axis_size("item")
    item = lax.axis_index("item")
    core = lax.axis_index("bucket") & 1
    rows_own, dim = code_rows.shape
    rows_total = rows_own * items
    rows_half = rows_own // 2
    buckets_own = centroids.shape[0]
    buckets_total = buckets_own * lax.axis_size("bucket")
    share = buckets_own // items
    log_rows = math.log(rows_total)
    codes_t = code_rows.T
    centroids_t = centroids.T

    def spread_rows(values, item):
        out = jnp.zeros((1, rows_total), jnp.float32)
        for half in range(2):
            piece = values[:, half * rows_half : (half + 1) * rows_half]
            out = lax.dynamic_update_slice(out, piece, (0, half * (rows_total // 2) + item * rows_half))
        return out

    def own_rows(values):
        return jnp.concatenate(
            [
                lax.dynamic_slice_in_dim(values, half * (rows_total // 2) + item * rows_half, rows_half, axis=1)
                for half in range(2)
            ],
            axis=1,
        )

    side_bits = [("bucket", bit) for bit in bits_of("bucket")[1:]]
    item_bits = [("item", bit) for bit in bits_of("item")]

    own_half = lax.dynamic_slice_in_dim(codes_t, core * rows_half, rows_half, axis=1).astype(jnp.float32)
    pieces = gather_blocks(own_half, "item")

    held = []
    for part in range(2):
        held = [lse(codes_t, centroids_t, 2, part, 2, held)]

    def merged(first, second):
        highest = jnp.maximum(first[0:1], second[0:1])
        summed = first[1:2] * jnp.exp(first[0:1] - highest) + second[1:2] * jnp.exp(second[0:1] - highest)
        return jnp.concatenate([highest, summed], axis=0)

    def potential(stats):
        return -log_rows - (stats[0:1] + jnp.log(stats[1:2]))

    stats = held[0]
    for flips in [[("bucket", 1)]] + [[flip] for flip in side_bits[:-1]]:
        received = joint_swap(stats, flips)
        stats = merged(stats, received)
    terms = exchanged(stats, groups_of([side_bits[-1], item_bits[0]])[0])
    rows = spread_rows(potential(merged(terms[0], terms[1])), item)
    rows = rows + spread_rows(potential(merged(terms[2], terms[3])), item ^ 1)
    groups = groups_of(item_bits[1:])
    for group in groups[:-1]:
        rows = joined(exchanged(rows, group))
    terms = exchanged(rows, groups[-1])

    mine = place(pieces, item)
    theirs = swap(mine, "bucket", 1)
    right, codes = small(
        table_kernel,
        core,
        [mine, theirs],
        [
            jax.ShapeDtypeStruct((2 * dim, rows_total), jnp.bfloat16),
            jax.ShapeDtypeStruct((dim, rows_total), jnp.bfloat16),
        ],
    )

    old = []
    row_first = None
    for iteration in range(ITERS):
        total, cols, row = sink(centroids_t, item, share, right, terms, old, rows_total, buckets_total)
        old = [cols, row]
        if row_first is None:
            row_first = row
        if iteration < ITERS - 1:
            total = total + swap(total, "bucket", 1)
            groups = groups_of(side_bits + item_bits)
            for group in groups[:-1]:
                total = joined(exchanged(total, group))
            terms = exchanged(total, groups[-1])

    col = lax.dynamic_update_slice(jnp.zeros((1, buckets_own), jnp.float32), cols[0:1], (0, item * share))
    total = total + swap(total, "bucket", 1)
    groups = groups_of(side_bits + item_bits)
    for group in groups[:-1]:
        sums, held_cols = [total], [col]
        for flips in group:
            alone = any(axis == "bucket" for axis, _ in flips)
            sent = total if alone else jnp.concatenate([total, col], axis=1)
            received = joint_swap(sent, flips)
            sums.append(received[:, :rows_total])
            if not alone:
                held_cols.append(received[:, rows_total:])
        total = joined(sums)
        col = functools.reduce(jnp.add, held_cols)
    terms = exchanged(jnp.concatenate([total, col], axis=1), groups[-1])

    block = block_of(share, rows_total)
    update = final(
        centroids_t, item, share, cols, right, [row, row_first, *terms], codes, 1, True, rows_total,
        block, 0, share // block, share // block, [],
    )
    pieces = gather_blocks(update, "item")

    both = joined(terms)
    mass, col = both[:, :rows_total] * float(rows_total), both[:, rows_total:]
    p_rows = own_rows(jnp.concatenate([row + log_rows, mass * jnp.exp(row_first - row)], axis=0))
    halves = []
    for half, calls in enumerate([2, 2]):
        held = []
        for call in range(calls):
            block = rows_half // calls
            held = [
                final(
                    codes_t, item, rows_own, p_rows, centroids_t, [col], None, 2, False, rows_total,
                    block, half * calls + call, 1, calls, held,
                )
            ]
        grad = held[0]
        for bit in bits_of("bucket"):
            received = swap(grad, "bucket", bit)
            grad = grad + received
        halves.append(grad)
    keys = sorted(pieces)
    early = [key for key in keys if not key & 1 or key < 5]
    new_centroids = store(pieces, item, early, items, [])
    new_centroids = store(pieces, item, [key for key in keys if key not in early], items, [new_centroids])
    return (jnp.concatenate(halves, axis=1).T, new_centroids.T)


def solution(mesh):
    return jax.shard_map(
        step,
        mesh=mesh,
        in_specs=(P("item", None), P("bucket", None)),
        out_specs=(P("item", None), P("bucket", None)),
        check_vma=False,
    )
```

```python
import functools
import math

import jax
import jax.numpy as jnp
from jax import lax
from jax.experimental import pallas as pl
from jax.experimental.pallas import tpu as pltpu
from jax.sharding import PartitionSpec as P


ITERS = 3

score_scale = 20.0
step_rate = 0.2
epsilon = 1e-06

CHUNK = 4096
SUB = 512
LANES = 128
POTS = 16


def swap(value, axis, bit):
    size = lax.axis_size(axis)
    return lax.ppermute(value, axis, [(k, k ^ bit) for k in range(size)])


def bits_of(axis):
    size = lax.axis_size(axis)
    return [1 << k for k in range(size.bit_length() - 1)]


def joint_swap(value, flips):
    items, buckets = lax.axis_size("item"), lax.axis_size("bucket")
    item_bits = sum(bit for axis, bit in flips if axis == "item")
    bucket_bits = sum(bit for axis, bit in flips if axis == "bucket")
    pairs = [
        (item * buckets + bucket, (item ^ item_bits) * buckets + (bucket ^ bucket_bits))
        for item in range(items)
        for bucket in range(buckets)
    ]
    return lax.ppermute(value, ("item", "bucket"), pairs)


def groups_of(flips):
    pairs = [flips[k : k + 2] for k in range(0, len(flips), 2)]
    return [[[pair[0]]] if len(pair) == 1 else [[pair[0]], [pair[1]], pair] for pair in pairs]


def joined(terms):
    if len(terms) == 4:
        return (terms[0] + terms[1]) + (terms[2] + terms[3])
    return terms[0] + terms[1]


def exchanged(value, group):
    terms = [value]
    for flips in group:
        terms.append(joint_swap(value, flips))
    return terms


def gather_blocks(value, axis):
    held = {0: value}
    for bit in reversed(bits_of(axis)):
        for key, block in list(held.items()):
            held[key | bit] = swap(block, axis, bit)
    return held


def thirds(value):
    high = value.astype(jnp.bfloat16).astype(jnp.float32)
    middle = (value - high).astype(jnp.bfloat16).astype(jnp.float32)
    return high, middle, value - high - middle


def pots(row, width, at):
    sub = lax.broadcasted_iota(jnp.int32, (POTS, width), 0)
    high, middle, low = thirds(row)
    out = jnp.where(sub < 6, 1.0, 0.0)
    out = jnp.where(sub == at, high, out)
    out = jnp.where(sub == at + 1, middle, out)
    out = jnp.where(sub == at + 2, low, out)
    return out.astype(jnp.bfloat16)


def left_pots(row, width):
    return jnp.transpose(pots(row, width, 3).astype(jnp.float32)).astype(jnp.bfloat16)


def row_of(column):
    wide = jnp.broadcast_to(column, (column.shape[0], LANES))
    return jnp.transpose(wide)[0:8, :]


def slices(value):
    return [value[:, k * LANES : (k + 1) * LANES] for k in range(value.shape[1] // LANES)]


def folded(values, op):
    values = list(values)
    while len(values) > 1:
        values = [op(*values[k : k + 2]) if k + 1 < len(values) else values[k] for k in range(0, len(values), 2)]
    return values[0]


def place_kernel(item_ref, *refs, keys):
    pieces, out_ref = refs[: len(keys)], refs[len(keys)]
    for key, piece_ref in zip(keys, pieces):
        width = piece_ref.shape[1]
        at = pl.ds(pl.multiple_of((item_ref[0] ^ key) * width, width), width)
        out_ref[:, at] = piece_ref[...]


def table_kernel(core_ref, mine_ref, other_ref, right_ref, codes_ref):
    dim, width = mine_ref.shape
    for piece_ref, half in ((mine_ref, core_ref[0]), (other_ref, 1 - core_ref[0])):
        at = pl.ds(pl.multiple_of(half * width, width), width)
        piece = piece_ref[...]
        scaled = score_scale * piece
        high = scaled.astype(jnp.bfloat16)
        right_ref[0:dim, at] = high
        right_ref[dim : 2 * dim, at] = (scaled - high.astype(jnp.float32)).astype(jnp.bfloat16)
        codes_ref[:, at] = piece.astype(jnp.bfloat16)


def left_of(l_ref, split):
    rows = jnp.transpose(l_ref[...].astype(jnp.float32))
    if split:
        rows = score_scale * rows
        high = rows.astype(jnp.bfloat16)
        low = (rows - high.astype(jnp.float32)).astype(jnp.bfloat16)
    else:
        high = low = rows.astype(jnp.bfloat16)
    return jnp.concatenate([high, low], axis=1)


def chunk_of(width):
    return min(width, CHUNK)


def chunks(width, run):
    size = chunk_of(width)

    @pl.loop(0, width // size)
    def _(step):
        run(step, pl.ds(pl.multiple_of(step * size, size), size))


def cases(count, run):
    step = pl.program_id(0)

    @pl.when(step == 0)
    def _():
        run(True, False)

    if count > 1:

        @pl.when((step > 0) & (step < count))
        def _():
            run(True, True)

    @pl.when(step == count)
    def _():
        run(False, True)


def raised(pieces, high_ref, sum_ref):
    was = high_ref[...]
    high = jnp.maximum(was, folded(pieces, jnp.maximum))
    terms = [jnp.exp(piece - high) for piece in pieces]
    high_ref[...] = high
    sum_ref[...] = sum_ref[...] * jnp.exp(was - high) + folded(terms, jnp.add)
    return high, terms


def settled(high_ref, sum_ref):
    highest = jnp.max(high_ref[...], axis=1, keepdims=True)
    return highest, jnp.sum(sum_ref[...] * jnp.exp(high_ref[...] - highest), axis=1, keepdims=True)


def lse_kernel(l_ref, w_ref, *rest, repeat):
    out_ref, high_ref, sum_ref = rest[-3:]
    width = w_ref.shape[1]
    left = left_of(l_ref, True)
    high_ref[...] = jnp.full(high_ref.shape, -jnp.inf, jnp.float32)
    sum_ref[...] = jnp.zeros(sum_ref.shape, jnp.float32)

    def chunk(_, at):
        right = jnp.concatenate([w_ref[:, at]] * repeat, axis=0)
        for at in range(0, right.shape[1], SUB):
            y = jnp.dot(left, right[:, at : at + SUB], preferred_element_type=jnp.float32)
            raised(slices(y), high_ref, sum_ref)

    chunks(width, chunk)
    highest, summed = settled(high_ref, sum_ref)
    lane = lax.broadcasted_iota(jnp.int32, high_ref.shape, 1)
    out_ref[...] = jnp.transpose(jnp.where(lane == 0, highest, summed))[0:2, :]


def sink_kernel(
    l_ref, w_ref, *rest, first, rows_total, buckets_total, count, terms
):
    term_refs, rest = rest[:terms], rest[terms:]
    if not first:
        p_ref, q_ref, *rest = rest
    sums_ref, pot_ref, row_ref, y_ref, part_ref, high_ref, wide_ref, wpot_ref, acc_ref = rest
    block, width = y_ref.shape

    def run(new, old):
        if new and not old:
            acc_ref[...] = jnp.zeros(acc_ref.shape, jnp.float32)

            def prepare(_, at):
                row = joined([term_ref[0:1, at] for term_ref in term_refs])
                if not first:
                    row = q_ref[0:1, at] - jnp.log(row * float(rows_total))
                row_ref[0:1, at] = row
                wpot_ref[:, at] = pots(row, chunk_of(width), 0)

            chunks(width, prepare)
        if new:
            was = jnp.zeros((1, block), jnp.float32) if first else p_ref[0:1, :]
            left = jnp.concatenate([left_of(l_ref, False), left_pots(was, block)], axis=1)
            part_ref[...] = jnp.full(part_ref.shape, -jnp.inf if first else 0.0, jnp.float32)

        def chunk(_, at):
            if old:
                sums = [
                    jnp.sum((piece * wide_ref[...]).reshape(block // 8, 8, LANES), axis=0)
                    for piece in slices(y_ref[:, at])
                ]
                acc_ref[:, at] += jnp.concatenate(sums, axis=1)
            if new:
                right = jnp.concatenate([w_ref[:, at], wpot_ref[:, at]], axis=0)
                y = jnp.dot(left, right, preferred_element_type=jnp.float32)
                if first:
                    y_ref[:, at] = y
                    part_ref[...] = jnp.maximum(part_ref[...], folded(slices(y), jnp.maximum))
                else:
                    y = jnp.exp(y)
                    y_ref[:, at] = y
                    part_ref[...] += folded(slices(y), jnp.add)

        chunks(width, chunk)
        if new and first:
            highest = jnp.max(part_ref[...], axis=1, keepdims=True)
            high_ref[...] = jnp.broadcast_to(highest, (block, LANES))
            part_ref[...] = jnp.zeros(part_ref.shape, jnp.float32)

            def again(_, at):
                terms = [jnp.exp(piece - high_ref[...]) for piece in slices(y_ref[:, at])]
                y_ref[:, at] = jnp.concatenate(terms, axis=1)
                part_ref[...] += folded(terms, jnp.add)

            chunks(width, again)
        if new:
            summed = jnp.sum(part_ref[...], axis=1, keepdims=True) * float(buckets_total)
            wide_ref[...] = jnp.broadcast_to(1.0 / summed, (block, LANES))
            summed = row_of(summed)
            if first:
                pot_ref[...] = -(row_of(high_ref[...]) + jnp.log(summed))
            else:
                pot_ref[...] = was - jnp.log(summed)
        if not new:
            sums_ref[...] = jnp.sum(acc_ref[...], axis=0, keepdims=True)

    cases(count, run)


def final_kernel(l_ref, p_ref, w_ref, *rest, repeat, update, rows_total, terms):
    out_ref, wide_ref, wpot_ref, v_ref, acc_ref = rest[-5:]
    if update:
        row_ref, start_ref, *term_refs = rest[: 2 + terms]
        r_ref = rest[2 + terms]
    else:
        col_ref, r_ref = rest[0], w_ref
    block = l_ref.shape[1]
    width = w_ref.shape[1]

    @pl.when(pl.program_id(0) == 0)
    def _():
        def prepare(_, at):
            if update:
                row = row_ref[0:1, at]
                mass = joined([term_ref[0:1, at] for term_ref in term_refs]) * float(rows_total)
                v_ref[0:1, at] = mass * jnp.exp(start_ref[0:1, at] - row)
                row = row + math.log(rows_total)
            else:
                row = col_ref[0:1, at]
                v_ref[0:1, at] = jnp.exp(-row)
            wpot_ref[:, at] = pots(row, chunk_of(width), 0)

        chunks(width, prepare)

    factor_p = jnp.exp(-p_ref[0:1, :]) if update else p_ref[1:2, :]
    left = jnp.concatenate([left_of(l_ref, not update), left_pots(p_ref[0:1, :], block)], axis=1)
    wide_ref[...] = jnp.transpose(jnp.broadcast_to(factor_p, (LANES, block)))
    acc_ref[...] = jnp.zeros(acc_ref.shape, jnp.float32)

    def chunk(_, at):
        right = jnp.concatenate([w_ref[:, at]] * repeat + [wpot_ref[:, at]], axis=0)
        y = jnp.dot(left, right, preferred_element_type=jnp.float32)
        delta = jnp.concatenate(
            [
                (jnp.exp(piece) * (wide_ref[...] * factor - 1.0)).astype(jnp.bfloat16)
                for piece, factor in zip(slices(y), slices(v_ref[0:1, at]))
            ],
            axis=1,
        )
        acc_ref[...] += lax.dot_general(
            delta, r_ref[:, at], (((1,), (1,)), ((), ())), preferred_element_type=jnp.float32
        )

    chunks(width, chunk)
    gradient = score_scale * jnp.transpose(acc_ref[...])
    if update:
        moved = l_ref[...].astype(jnp.float32) - step_rate * gradient
        gradient = moved * lax.rsqrt(jnp.mean(moved * moved, axis=0, keepdims=True) + epsilon)
    out_ref[...] = gradient


VMEM = pltpu.VMEM


def block_of(count, width):
    return min(count, 512 if width <= 16384 else 128)


def params():
    return pltpu.CompilerParams(dimension_semantics=("arbitrary",), vmem_limit_bytes=40 * 1024 * 1024)


def cost(count, width, passes):
    return pl.CostEstimate(
        flops=2 * count * width * 256 * passes, transcendentals=count * width, bytes_accessed=width * 256 * 2
    )


def full(array):
    return pl.BlockSpec(array.shape, lambda k: (0, 0))


def lse(left, right, repeat, part, parts, before):
    (dim, rows), width = left.shape, right.shape[1]
    block = min(block_of(rows, width), rows // parts)
    count = rows // parts // block
    lead = part * count
    return pl.pallas_call(
        functools.partial(lse_kernel, repeat=repeat),
        grid=(count,),
        in_specs=[pl.BlockSpec((dim, block), lambda k: (0, lead + k)), full(right)]
        + [pl.BlockSpec(memory_space=pl.ANY)] * len(before),
        out_specs=pl.BlockSpec((2, block), lambda k: (0, lead + k)),
        out_shape=jax.ShapeDtypeStruct((2, rows), jnp.float32),
        scratch_shapes=[VMEM((block, LANES), jnp.float32)] * 2,
        input_output_aliases={2: 0} if before else {},
        compiler_params=params(),
        cost_estimate=cost(rows // parts, width, 1),
        name="row_lse",
    )(left, right, *before)


def sink(left, item, rows, right, terms, old, rows_total, buckets_total):
    dim, width = left.shape[0], right.shape[1]
    block = block_of(rows, width)
    count = rows // block
    first = not old
    line = pl.BlockSpec((1, width), lambda k, at: (0, 0))
    pot_spec = pl.BlockSpec((8, block), lambda k, at: (0, jnp.minimum(k, count - 1)))
    kernel = functools.partial(
        sink_kernel, first=first, rows_total=rows_total, buckets_total=buckets_total, count=count,
        terms=len(terms),
    )
    return pl.pallas_call(
        lambda at_ref, *refs: kernel(*refs),
        grid_spec=pltpu.PrefetchScalarGridSpec(num_scalar_prefetch=1, grid=(count + 1,),
        in_specs=[
            pl.BlockSpec((dim, block), lambda k, at: (0, at[0] * count + jnp.minimum(k, count - 1))),
            pl.BlockSpec(memory_space=pltpu.VMEM),
        ]
        + [pl.BlockSpec(memory_space=pltpu.VMEM)] * len(terms)
        + ([] if first else [pot_spec, line]),
        out_specs=[pl.BlockSpec(memory_space=pltpu.VMEM), pot_spec, line],
        scratch_shapes=[VMEM((block, width), jnp.float32)]
        + [VMEM((block, LANES), jnp.float32)] * 3
        + [VMEM((POTS, width), jnp.bfloat16), VMEM((8, width), jnp.float32)],
        ),
        out_shape=[
            jax.ShapeDtypeStruct((1, width), jnp.float32),
            jax.ShapeDtypeStruct((8, rows), jnp.float32),
            jax.ShapeDtypeStruct((1, width), jnp.float32),
        ],
        compiler_params=params(),
        cost_estimate=cost(rows, width, 1),
        name="sinkhorn_first" if first else "sinkhorn_next",
    )(item.reshape(1).astype(jnp.int32), left, right, *terms, *old)


def final(left, item, rows, p_rows, right, lines, codes, repeat, update, rows_total, block, lead, steps, total, before):
    dim, width = left.shape[0], right.shape[1]
    count = rows // block
    into = total - steps if before else 0
    extra = [codes] if update else []
    kernel = functools.partial(
        final_kernel, repeat=repeat, update=update, rows_total=rows_total, terms=len(lines) - 2
    )
    scalars = [item.reshape(1).astype(jnp.int32)] if update else []
    line = pl.BlockSpec((1, width), lambda k, *at: (0, 0))
    in_specs = [
        pl.BlockSpec((dim, block), lambda k, *at: (0, (at[0][0] * count if at else 0) + lead + k)),
        pl.BlockSpec((p_rows.shape[0], block), lambda k, *at: (0, lead + k)),
        pl.BlockSpec(memory_space=pltpu.VMEM) if update else pl.BlockSpec(right.shape, lambda k, *at: (0, 0)),
    ]
    in_specs += [line] * min(len(lines), 2) + [pl.BlockSpec(memory_space=pltpu.VMEM)] * (len(lines) - 2) + [pl.BlockSpec(memory_space=pltpu.VMEM) for one in extra]
    in_specs += [pl.BlockSpec(memory_space=pl.ANY)] * len(before)
    return pl.pallas_call(
        (lambda at_ref, *refs: kernel(*refs)) if update else kernel,
        grid_spec=pltpu.PrefetchScalarGridSpec(
            num_scalar_prefetch=len(scalars),
            grid=(steps,),
            in_specs=in_specs,
            out_specs=pl.BlockSpec((dim, block), lambda k, *at: (0, into + k)),
            scratch_shapes=[
                VMEM((block, LANES), jnp.float32),
                VMEM((POTS, width), jnp.bfloat16),
                VMEM((8, width), jnp.float32),
                VMEM((block, dim), jnp.float32),
            ],
        ),
        out_shape=jax.ShapeDtypeStruct((dim, total * block), jnp.float32),
        input_output_aliases={len(scalars) + 3 + len(lines) + len(extra): 0} if before else {},
        compiler_params=params(),
        cost_estimate=cost(steps * block, width, 2),
        name="centroid_update" if update else "code_gradient",
    )(*scalars, left, p_rows, right, *lines, *extra, *before)


def small(kernel, index, arrays, out_shape, **settings):
    several = isinstance(out_shape, list)
    near = pl.BlockSpec(memory_space=pltpu.VMEM)
    whole = lambda shape: pl.BlockSpec(shape, lambda k, index: (0, 0))
    specs = [near] * 2 if several else [whole(out_shape.shape)]
    return pl.pallas_call(
        functools.partial(kernel, **settings),
        grid_spec=pltpu.PrefetchScalarGridSpec(
            num_scalar_prefetch=1,
            grid=(1,),
            in_specs=[whole(one.shape) for one in arrays],
            out_specs=specs if several else specs[0],
        ),
        out_shape=out_shape,
        compiler_params=params(),
        cost_estimate=pl.CostEstimate(flops=0, transcendentals=0, bytes_accessed=4 << 20),
    )(index.reshape(1).astype(jnp.int32), *arrays)


def place(blocks, item):
    keys = sorted(blocks)
    dim, width = blocks[0].shape
    shape = jax.ShapeDtypeStruct((dim, width * len(keys)), jnp.float32)
    return small(place_kernel, item, [blocks[key] for key in keys], shape, keys=keys)


def store_kernel(at_ref, *refs, count):
    out_ref, sems = refs[-2:]
    width = refs[0].shape[1]
    copies = []
    for number in range(count):
        at = pl.ds(pl.multiple_of(at_ref[number] * width, width), width)
        copies.append(pltpu.make_async_copy(refs[number], out_ref.at[:, at], sems.at[number]))
    for copy in copies:
        copy.start()
    for copy in copies:
        copy.wait()


def store(pieces, item, keys, total, before):
    dim, width = pieces[0].shape
    at = jnp.stack([item ^ key for key in keys]).astype(jnp.int32)
    return pl.pallas_call(
        functools.partial(store_kernel, count=len(keys)),
        grid_spec=pltpu.PrefetchScalarGridSpec(
            num_scalar_prefetch=1,
            grid=(1,),
            in_specs=[pl.BlockSpec(memory_space=pltpu.VMEM)] * len(keys)
            + [pl.BlockSpec(memory_space=pl.ANY)] * len(before),
            out_specs=pl.BlockSpec(memory_space=pl.ANY),
            scratch_shapes=[pltpu.SemaphoreType.DMA((len(keys),))],
        ),
        out_shape=jax.ShapeDtypeStruct((dim, width * total), jnp.float32),
        input_output_aliases={1 + len(keys): 0} if before else {},
        compiler_params=params(),
        cost_estimate=pl.CostEstimate(flops=0, transcendentals=0, bytes_accessed=(1 << 19) * len(keys)),
    )(at, *[pieces[key] for key in keys], *before)


def step(code_rows, centroids):
    items = lax.axis_size("item")
    item = lax.axis_index("item")
    core = lax.axis_index("bucket") & 1
    rows_own, dim = code_rows.shape
    rows_total = rows_own * items
    rows_half = rows_own // 2
    buckets_own = centroids.shape[0]
    buckets_total = buckets_own * lax.axis_size("bucket")
    share = buckets_own // items
    log_rows = math.log(rows_total)
    codes_t = code_rows.T
    centroids_t = centroids.T

    def spread_rows(values, item):
        out = jnp.zeros((1, rows_total), jnp.float32)
        for half in range(2):
            piece = values[:, half * rows_half : (half + 1) * rows_half]
            out = lax.dynamic_update_slice(out, piece, (0, half * (rows_total // 2) + item * rows_half))
        return out

    def own_rows(values):
        return jnp.concatenate(
            [
                lax.dynamic_slice_in_dim(values, half * (rows_total // 2) + item * rows_half, rows_half, axis=1)
                for half in range(2)
            ],
            axis=1,
        )

    side_bits = [("bucket", bit) for bit in bits_of("bucket")[1:]]
    item_bits = [("item", bit) for bit in bits_of("item")]

    own_half = lax.dynamic_slice_in_dim(codes_t, core * rows_half, rows_half, axis=1).astype(jnp.float32)
    pieces = gather_blocks(own_half, "item")

    held = []
    for part in range(2):
        held = [lse(codes_t, centroids_t, 2, part, 2, held)]

    def merged(first, second):
        highest = jnp.maximum(first[0:1], second[0:1])
        summed = first[1:2] * jnp.exp(first[0:1] - highest) + second[1:2] * jnp.exp(second[0:1] - highest)
        return jnp.concatenate([highest, summed], axis=0)

    def potential(stats):
        return -log_rows - (stats[0:1] + jnp.log(stats[1:2]))

    stats = held[0]
    for flips in [[("bucket", 1)]] + [[flip] for flip in side_bits[:-1]]:
        received = joint_swap(stats, flips)
        stats = merged(stats, received)
    terms = exchanged(stats, groups_of([side_bits[-1], item_bits[0]])[0])
    rows = spread_rows(potential(merged(terms[0], terms[1])), item)
    rows = rows + spread_rows(potential(merged(terms[2], terms[3])), item ^ 1)
    groups = groups_of(item_bits[1:])
    for group in groups[:-1]:
        rows = joined(exchanged(rows, group))
    terms = exchanged(rows, groups[-1])

    mine = place(pieces, item)
    theirs = swap(mine, "bucket", 1)
    right, codes = small(
        table_kernel,
        core,
        [mine, theirs],
        [
            jax.ShapeDtypeStruct((2 * dim, rows_total), jnp.bfloat16),
            jax.ShapeDtypeStruct((dim, rows_total), jnp.bfloat16),
        ],
    )

    old = []
    row_first = None
    for iteration in range(ITERS):
        total, cols, row = sink(centroids_t, item, share, right, terms, old, rows_total, buckets_total)
        old = [cols, row]
        if row_first is None:
            row_first = row
        if iteration < ITERS - 1:
            total = total + swap(total, "bucket", 1)
            groups = groups_of(side_bits + item_bits)
            for group in groups[:-1]:
                total = joined(exchanged(total, group))
            terms = exchanged(total, groups[-1])

    col = lax.dynamic_update_slice(jnp.zeros((1, buckets_own), jnp.float32), cols[0:1], (0, item * share))
    total = total + swap(total, "bucket", 1)
    groups = groups_of(side_bits + item_bits)
    for group in groups[:-1]:
        sums, held_cols = [total], [col]
        for flips in group:
            alone = any(axis == "bucket" for axis, _ in flips)
            sent = total if alone else jnp.concatenate([total, col], axis=1)
            received = joint_swap(sent, flips)
            sums.append(received[:, :rows_total])
            if not alone:
                held_cols.append(received[:, rows_total:])
        total = joined(sums)
        col = functools.reduce(jnp.add, held_cols)
    terms = exchanged(jnp.concatenate([total, col], axis=1), groups[-1])

    block = block_of(share, rows_total)
    update = final(
        centroids_t, item, share, cols, right, [row, row_first, *terms], codes, 1, True, rows_total,
        block, 0, share // block, share // block, [],
    )
    pieces = gather_blocks(update, "item")

    both = joined(terms)
    mass, col = both[:, :rows_total] * float(rows_total), both[:, rows_total:]
    p_rows = own_rows(jnp.concatenate([row + log_rows, mass * jnp.exp(row_first - row)], axis=0))
    halves = []
    for half, calls in enumerate([2, 2]):
        held = []
        for call in range(calls):
            block = rows_half // calls
            held = [
                final(
                    codes_t, item, rows_own, p_rows, centroids_t, [col], None, 2, False, rows_total,
                    block, half * calls + call, 1, calls, held,
                )
            ]
        grad = held[0]
        for bit in bits_of("bucket"):
            received = swap(grad, "bucket", bit)
            grad = grad + received
        halves.append(grad)
    keys = sorted(pieces)
    early = [key for key in keys if not key & 1 or key < 5]
    new_centroids = store(pieces, item, early, items, [])
    new_centroids = store(pieces, item, [key for key in keys if key not in early], items, [new_centroids])
    return (jnp.concatenate(halves, axis=1).T, new_centroids.T)


def solution(mesh):
    return jax.shard_map(
        step,
        mesh=mesh,
        in_specs=(P("item", None), P("bucket", None)),
        out_specs=(P("item", None), P("bucket", None)),
        check_vma=False,
    )
```
